32 devices in a mesh: rep: 8 (over z, y), shard: 4 (over x, core).
Axes of the slice: x: 2, y: 2, z: 4, core: 2. Of those that a mesh axis runs over, the one named last changes fastest.
Arguments:
- tokens: bfloat16 [32, 512, 1024], P('rep', 'shard'), may hold values from -6 to 6
- enc_states: bfloat16 [32, 256, 1024], P(('rep', 'shard')), may hold values from -6 to 6
- cotangent: bfloat16 [32, 512, 1024], P('rep', 'shard'), may hold values from -6 to 6
- lengths: int32 [8, 4], P('rep'), may hold values from 1 to 512, 1280 in all within a row
- owner: int32 [8, 4], P('rep'), may hold values from 0 to 3, each once within a row
- attn_in: bfloat16 [6, 1024, 1024], P(None, 'shard'), may hold values from -0.1875 to 0.1875
- attn_out: bfloat16 [2, 1024, 1024], P(None, 'shard'), may hold values from -2 to 2
- attn_bias: bfloat16 [6, 1024], P(None, 'shard'), may hold values from -3 to 3
- norm_gain: bfloat16 [3, 1024], P(None, 'shard'), may hold values from 0.25 to 1.75
- norm_bias: bfloat16 [3, 1024], P(None, 'shard'), may hold values from -3 to 3
- mlp_in: bfloat16 [1024, 4096], P('shard'), may hold values from -0.1875 to 0.1875
- mlp_bias_in: bfloat16 [4096], P('shard'), may hold values from -3 to 3
- mlp_out: bfloat16 [4096, 1024], P('shard'), may hold values from -0.09375 to 0.09375
- mlp_bias_out: bfloat16 [1024], P('shard'), may hold values from -3 to 3
Outputs:
- out: bfloat16 [32, 512, 1024], P('rep', 'shard')
- grad_tokens: bfloat16 [32, 512, 1024], P('rep', 'shard')
- grad_enc: bfloat16 [32, 256, 1024], P(('rep', 'shard'))
- grad_attn_in: float32 [6, 1024, 1024], P(None, 'shard')
- grad_attn_out: float32 [2, 1024, 1024], P(None, 'shard')
- grad_attn_bias: float32 [6, 1024], P(None, 'shard')
- grad_norm_gain: float32 [3, 1024], P(None, 'shard')
- grad_norm_bias: float32 [3, 1024], P(None, 'shard')
- grad_mlp_in: float32 [1024, 4096], P('shard')
- grad_mlp_bias_in: float32 [4096], P('shard')
- grad_mlp_out: float32 [4096, 1024], P('shard')
- grad_mlp_bias_out: float32 [1024], P('shard')
The draws below stay inside these ranges and needn't reach their ends.
Inputs may be any that keep to these rules, and one draw needn't show every extreme that they name: Row r holds the lengths of the 4 sequences of group r; they sum to 1280, and the longest of each row is 512. Each row is a permutation: sequence i of group r is handled at index owner[r, i] of shard, and its encoder states are block r * 4 + owner[r, i] of enc_states.
All inputs are finite; a program needn't handle non-finite values.
Results may differ from the reference program's by a relative error of at most 0.024.
The reference program's roundings to bfloat16 on the way count: a program that leaves them out, or rounds other values in their place, can miss the bound.
Values may be sent and summed in bfloat16 or wider, within the bound.
A program may use at most 256 MiB of HBM per device.

```python
import math
import jax
import jax.numpy as jnp
import numpy as np
from jax import lax

D = 1024
HEADS = 16
HEAD_DIM = 64
FF = 4096
CAP = 512
ENC = 256
GROUP_SEQS = 4
GROUP_TOK = 1280
SEQS = 32
N_REP = 8


def levels(rng, dims, split, least, largest):
    loudness, own = 1.0, jax.random.fold_in(rng, 6)
    for dim, blocks in split:
        heights = jnp.exp(jax.random.uniform(jax.random.fold_in(own, dim), (blocks,), jnp.float32, least / len(split), largest / len(split)))
        loudness = loudness * jnp.repeat(heights, dims[dim] // blocks).reshape([-1 if axis == dim else 1 for axis in range(len(dims))])
    return loudness


def length_profile(number_of, total, bound, slope):
    loads = [(1 << 20) // math.isqrt(grade ** slope) + 1 for grade in range(2, number_of + 1)]
    rest, counts = total - bound - (number_of - 1), [1] * (number_of - 1)
    while rest > 0:
        movable = [i for i in range(number_of - 1) if counts[i] < bound]
        whole, left = sum([loads[i] for i in movable]), rest
        for i in movable:
            extra = min(bound - counts[i], max(1, left * loads[i] // whole), rest)
            counts[i] = counts[i] + extra
            rest = rest - extra
    return np.array([bound] + counts)


def ragged_sizes(own_key, number_of, total, bound, lean):
    if number_of == 2:
        one = jax.random.randint(own_key, (), max(1, total - bound), min(bound, total - 1) + 1)
        return jnp.stack([one, total - one])
    sizes = jnp.asarray(length_profile(number_of, total, bound, lean), jnp.int32)
    couples = (number_of - 1) // 2
    donor, sink = sizes[1:1 + 2 * couples:2], sizes[2:2 + 2 * couples:2]
    margin = jnp.minimum(donor - 1, bound - sink)
    moved = jax.random.randint(jax.random.fold_in(own_key, 1), (couples,), 0, 1 << 20) % (margin + 1)
    sizes = sizes.at[1:1 + 2 * couples:2].set(donor - moved).at[2:2 + 2 * couples:2].set(sink + moved)
    return sizes[jax.random.permutation(jax.random.fold_in(own_key, 2), number_of)]


def centred(own_key, dims, deviation, reach, split=(), held_as=jnp.bfloat16):
    array = jax.random.normal(own_key, dims, jnp.float32) * deviation
    if len(split) > 0:
        array = levels(own_key, dims, split, -0.22, 0.18) * array
    return jnp.clip(array, min=-reach, max=reach).astype(held_as)


def setup_inputs(seed: int = 0) -> dict:
    streams_of = jax.random.split(jax.random.key(seed), 15)
    return {
        "tokens": centred(streams_of[0], (SEQS, CAP, D), 1.0, 6.0, ((0, 8), (1, 4))),
        "enc_states": centred(streams_of[1], (SEQS, ENC, D), 1.0, 6.0, ((0, 32),)),
        "cotangent": centred(streams_of[2], (SEQS, CAP, D), 1.0, 6.0, ((0, 8), (1, 4))),
        "lengths": jax.vmap(lambda own: ragged_sizes(own, GROUP_SEQS, GROUP_TOK, CAP, 1))(jax.random.split(streams_of[3], N_REP)).reshape((N_REP, GROUP_SEQS)).astype(jnp.int32),
        "owner": jax.vmap(lambda own: jax.random.permutation(own, GROUP_SEQS))(jax.random.split(streams_of[4], N_REP)).reshape((N_REP, GROUP_SEQS)).astype(jnp.int32),
        "attn_in": centred(streams_of[5], (6, D, D), D ** -0.5, 0.1875, ((1, 4),)),
        "attn_out": centred(streams_of[6], (2, D, D), (max(1, 4 * D // CAP)) ** -0.5, 2.0, ((1, 4),)),
        "attn_bias": centred(streams_of[7], (6, D), 0.5, 3.0, ((1, 4),)),
        "norm_gain": jnp.clip(1.0 + 0.15 * jax.random.normal(streams_of[8], (3, D), jnp.float32), 0.25, 1.75).astype(jnp.bfloat16),
        "norm_bias": centred(streams_of[9], (3, D), 0.5, 3.0, ((1, 4),)),
        "mlp_in": centred(streams_of[10], (D, FF), D ** -0.5, 0.1875, ((0, 4),)),
        "mlp_bias_in": centred(streams_of[11], (FF,), 0.5, 3.0, ((0, 4),)),
        "mlp_out": centred(streams_of[12], (FF, D), FF ** -0.5, 0.09375, ((0, 4),)),
        "mlp_bias_out": centred(streams_of[13], (D,), 0.5, 3.0, ((0, 4),)),
    }


@jax.custom_vjp
def low(v):
    return lax.optimization_barrier(v.astype(jnp.bfloat16)).astype(jnp.float32)

@jax.custom_vjp
def low_back(v):
    return v

def low_keep(v):
    return (low(v), None)

def low_pass(kept, grad):
    return (grad,)

def back_keep(v):
    return (v, None)

def back_low(kept, grad):
    return (low(grad),)
low.defvjp(low_keep, low_pass)
low_back.defvjp(back_keep, back_low)
highest_precision = lax.Precision.HIGHEST

def matmul_high(left, right):
    return jnp.dot(left, right, precision=highest_precision, preferred_element_type=jnp.float32)

def layer_norm(features, norm_scale, norm_shift):
    center = features - lax.optimization_barrier(jnp.mean(features, axis=-1, keepdims=True))
    spread = lax.optimization_barrier(jnp.mean(center * center, axis=-1, keepdims=True))
    return center * lax.rsqrt(spread + 1e-05) * norm_scale + norm_shift

def attend(queries, keys, values, causal):
    row_count = queries.shape[0]
    block_rows = min(512, row_count)
    block_count = row_count // block_rows
    query_heads = queries.reshape(block_count, block_rows, HEADS, HEAD_DIM)
    key_heads = keys.reshape(keys.shape[0], HEADS, HEAD_DIM)
    value_heads = values.reshape(values.shape[0], HEADS, HEAD_DIM)
    key_pos = jnp.arange(keys.shape[0], dtype=jnp.int32)
    offsets = jnp.arange(block_count, dtype=jnp.int32) * block_rows

    def one_block(block_items):
        query_block, offset = block_items
        scores = jnp.einsum('qhd,khd->hqk', query_block, key_heads, precision=highest_precision) * HEAD_DIM ** (-0.5)
        scores = low_back(scores)
        if causal:
            query_pos = offset + jnp.arange(block_rows, dtype=jnp.int32)
            scores = jnp.where(key_pos[None, None, :] <= query_pos[None, :, None], scores, -jnp.inf)
        peak = lax.optimization_barrier(jnp.max(scores, axis=-1, keepdims=True))
        log_total = peak + jnp.log(lax.optimization_barrier(jnp.sum(jnp.exp(scores - peak), axis=-1, keepdims=True)))
        weights_low = low(jnp.exp(scores - log_total))
        return jnp.einsum('hqk,khd->qhd', weights_low, value_heads, precision=highest_precision)
    context = lax.map(jax.checkpoint(one_block), (query_heads, offsets))
    return context.reshape(row_count, HEADS * HEAD_DIM)

def forward(inputs, encoder, row_mask, params):
    attn_in, attn_out, attn_bias, norm_gain, norm_bias, mlp_in, mlp_bias_in, mlp_out, mlp_bias_out = params
    queries = low_back(low(matmul_high(inputs, attn_in[0]) + attn_bias[0]))
    keys = low_back(low(matmul_high(inputs, attn_in[1])))
    values = low_back(low(matmul_high(inputs, attn_in[2]) + attn_bias[1]))
    context = low_back(low(attend(queries, keys, values, True)))
    first_sum = inputs + low_back(matmul_high(context, attn_out[0]) + attn_bias[2])
    first_norm = layer_norm(first_sum, norm_gain[0], norm_bias[0])
    first_low = low(first_norm)
    cross_queries = low_back(low(matmul_high(first_low, attn_in[3]) + attn_bias[3]))
    cross_keys = low_back(low(matmul_high(encoder, attn_in[4])))
    cross_values = low_back(low(matmul_high(encoder, attn_in[5]) + attn_bias[4]))
    cross_context = low_back(low(attend(cross_queries, cross_keys, cross_values, False)))
    second_sum = first_norm + low_back(matmul_high(cross_context, attn_out[1]) + attn_bias[5])
    second_norm = layer_norm(second_sum, norm_gain[1], norm_bias[1])
    second_low = low(second_norm)
    hidden_pre = low_back(matmul_high(second_low, mlp_in) + mlp_bias_in)
    hidden_low = low(jax.nn.gelu(hidden_pre, approximate=False))
    third_sum = second_norm + low_back(matmul_high(hidden_low, mlp_out) + mlp_bias_out)
    return layer_norm(third_sum, norm_gain[2], norm_bias[2]) * row_mask

def reference(tokens, enc_states, cotangent, lengths, owner, attn_in, attn_out, attn_bias, norm_gain, norm_bias, mlp_in, mlp_bias_in, mlp_out, mlp_bias_out):
    params = (attn_in.astype(jnp.float32), attn_out.astype(jnp.float32), attn_bias.astype(jnp.float32), norm_gain.astype(jnp.float32), norm_bias.astype(jnp.float32), mlp_in.astype(jnp.float32), mlp_bias_in.astype(jnp.float32), mlp_out.astype(jnp.float32), mlp_bias_out.astype(jnp.float32))
    sequence_ids = jnp.arange(SEQS, dtype=jnp.int32)
    slot_of = (sequence_ids // GROUP_SEQS * GROUP_SEQS + owner.reshape(SEQS)).astype(jnp.int32)
    flat_lengths = lengths.reshape(SEQS).astype(jnp.int32)
    positions = jnp.arange(CAP, dtype=jnp.int32)

    def one_sequence(totals, scan_items):
        seq_tokens, seq_grad, seq_length, slot_index = scan_items
        encoder = lax.dynamic_index_in_dim(enc_states, slot_index, 0, keepdims=False).astype(jnp.float32)
        row_mask = (positions < seq_length).astype(jnp.float32)[:, None]

        def layer_call(inputs, encoder_rows, weights):
            return forward(inputs, encoder_rows, row_mask, weights)
        result, pullback = jax.vjp(layer_call, seq_tokens.astype(jnp.float32), encoder, params)
        grad_inputs, grad_encoder, grad_weights = pullback(seq_grad.astype(jnp.float32))
        totals = jax.tree.map(jnp.add, totals, grad_weights)
        return (totals, (result.astype(jnp.bfloat16), grad_inputs.astype(jnp.bfloat16), grad_encoder.astype(jnp.bfloat16)))
    zeros_tree = jax.tree.map(jnp.zeros_like, params)
    totals, (output, grad_tokens, encoder_grads) = lax.scan(one_sequence, zeros_tree, (tokens, cotangent, flat_lengths, slot_of))
    grad_enc = jnp.zeros_like(encoder_grads).at[slot_of].set(encoder_grads)
    return (output, grad_tokens, grad_enc, totals[0], totals[1], totals[2], totals[3], totals[4], totals[5], totals[6], totals[7], totals[8])
```

```python
import types

import jax
import jax.numpy as jnp
from jax import lax
from jax.experimental import pallas as pl
from jax.experimental.pallas import tpu as pltpu
from jax.sharding import PartitionSpec as P

HEADS = 16
HEAD_DIM = 64


epsilon = 1e-05


def matmul(left, right):
    return jnp.dot(left, right, preferred_element_type=jnp.float32)


def contract_rows(left, right):
    return lax.dot_general(
        left, right, (((0,), (0,)), ((), ())), preferred_element_type=jnp.float32
    )


def contract_cols(left, right):
    return lax.dot_general(
        left, right, (((1,), (1,)), ((), ())), preferred_element_type=jnp.float32
    )


def layer_norm(features, norm_scale, norm_shift):
    center = features - jnp.mean(features, axis=-1, keepdims=True)
    spread = jnp.mean(center * center, axis=-1, keepdims=True)
    return center * lax.rsqrt(spread + epsilon) * norm_scale + norm_shift


def gelu_exact(features):
    return jax.nn.gelu(features, approximate=False)


def column_sum(matrix):
    return jnp.sum(matrix.astype(jnp.float32), axis=0)


def split_heads(matrix):
    width = min(4, HEADS)
    return jnp.moveaxis(matrix.reshape(matrix.shape[0], HEADS // width, width, HEAD_DIM), 1, 0)


def merge_heads(stacked):
    return jnp.moveaxis(stacked, 0, 1).reshape(stacked.shape[1], HEADS * HEAD_DIM)


def block_scores(query_block, key_group, offset, causal):
    scores = jnp.einsum(
        "qgd,kgd->gqk", query_block, key_group, preferred_element_type=jnp.float32
    ) * HEAD_DIM ** (-0.5)
    if causal:
        query_pos = offset + jnp.arange(query_block.shape[0], dtype=jnp.int32)
        key_pos = jnp.arange(key_group.shape[0], dtype=jnp.int32)
        scores = jnp.where(key_pos[None, None, :] <= query_pos[None, :, None], scores, -jnp.inf)
    return scores


def attention_forward(queries, keys, values, causal):
    row_count = queries.shape[0]
    block_rows = min(512, row_count)
    block_count = row_count // block_rows
    offsets = jnp.arange(block_count, dtype=jnp.int32) * block_rows

    def per_group(operands):
        query_group, key_group, value_group = operands
        width = query_group.shape[1]
        query_blocks = query_group.reshape(block_count, block_rows, width, HEAD_DIM)

        def per_block(block_items):
            query_block, offset = block_items
            scores = block_scores(query_block, key_group, offset, causal)
            peak = jnp.max(scores, axis=-1, keepdims=True)
            log_total = peak + jnp.log(jnp.sum(jnp.exp(scores - peak), axis=-1, keepdims=True))
            weights_low = jnp.exp(scores - log_total).astype(jnp.bfloat16)
            context = jnp.einsum(
                "gqk,kgd->qgd", weights_low, value_group, preferred_element_type=jnp.float32
            )
            return (context.astype(jnp.bfloat16), log_total)

        context, log_totals = lax.map(per_block, (query_blocks, offsets))
        return (context.reshape(row_count, width, HEAD_DIM), log_totals)

    context, log_totals = lax.map(
        per_group, (split_heads(queries), split_heads(keys), split_heads(values))
    )
    return (merge_heads(context), log_totals)


def attention_backward(queries, keys, values, log_totals, context_grad, causal):
    row_count = queries.shape[0]
    block_rows = min(512, row_count)
    block_count = row_count // block_rows
    offsets = jnp.arange(block_count, dtype=jnp.int32) * block_rows
    scale = HEAD_DIM ** (-0.5)

    def per_group(operands):
        query_group, key_group, value_group, grad_group, total_group = operands
        width = query_group.shape[1]
        query_blocks = query_group.reshape(block_count, block_rows, width, HEAD_DIM)
        grad_blocks = grad_group.reshape(block_count, block_rows, width, HEAD_DIM)

        def per_block(accumulated, block_items):
            key_grad, value_grad = accumulated
            query_block, grad_block, log_total, offset = block_items
            scores = block_scores(query_block, key_group, offset, causal)
            weights_full = jnp.exp(scores - log_total)
            weights_low = weights_full.astype(jnp.bfloat16)
            value_grad = value_grad + jnp.einsum(
                "gqk,qgd->kgd", weights_low, grad_block, preferred_element_type=jnp.float32
            )
            weight_grad = jnp.einsum(
                "qgd,kgd->gqk", grad_block, value_group, preferred_element_type=jnp.float32
            )
            row_dot = jnp.sum(weights_full * weight_grad, axis=-1, keepdims=True)
            score_grad = (weights_full * (weight_grad - row_dot)).astype(jnp.bfloat16)
            query_grad = (
                jnp.einsum(
                    "gqk,kgd->qgd", score_grad, key_group, preferred_element_type=jnp.float32
                )
                * scale
            )
            key_grad = (
                key_grad
                + jnp.einsum(
                    "gqk,qgd->kgd", score_grad, query_block, preferred_element_type=jnp.float32
                )
                * scale
            )
            return ((key_grad, value_grad), query_grad)

        empty_grad = jnp.zeros(key_group.shape, jnp.float32)
        (key_grad, value_grad), query_grad = lax.scan(
            per_block, (empty_grad, empty_grad), (query_blocks, grad_blocks, total_group, offsets)
        )
        return (query_grad.reshape(row_count, width, HEAD_DIM), key_grad, value_grad)

    query_grad, key_grad, value_grad = lax.map(
        per_group,
        (
            split_heads(queries),
            split_heads(keys),
            split_heads(values),
            split_heads(context_grad),
            log_totals,
        ),
    )
    return (merge_heads(query_grad), merge_heads(key_grad), merge_heads(value_grad))


def pick_blocks(blocks, order):
    count = blocks.shape[0]
    return jnp.concatenate(
        [lax.dynamic_slice_in_dim(blocks, order[i], 1, axis=0) for i in range(count)], axis=0
    )


MESH = pl.DeviceIdType.MESH
ROWS = 128
CHUNKS = 32


def place():
    rep, shard = lax.axis_index("rep"), lax.axis_index("shard")
    return rep // 2, lax.rem(rep, 2), shard // 2, lax.rem(shard, 2)


def device(z, y, x, c):
    return (z * 2 + y, x * 2 + c)


def greet(peers):
    barrier = pltpu.get_barrier_semaphore()
    for peer in peers:
        pl.semaphore_signal(barrier, inc=1, device_id=peer, device_id_type=MESH)
    pl.semaphore_wait(barrier, len(peers))


def rows_at(base, size, align):
    return pl.ds(pl.multiple_of(base, align), size)


F32, BF16 = jnp.float32, jnp.bfloat16
RING = 8
LAGS = (0, 2, 3, 4, 5, 6, 7)


def dot_over(left, right, a, b):
    return lax.dot_general(left, right, (((a,), (b,)), ((), ())), preferred_element_type=F32)


def dot_nn(left, right):
    return dot_over(left, right, 1, 0)


def dot_nt(left, right):
    return dot_over(left, right, 1, 1)


def dot_tn(left, right):
    return dot_over(left, right, 0, 0)


def remote(src, dst, send, recv, peer):
    return pltpu.make_async_remote_copy(
        src_ref=src, dst_ref=dst, send_sem=send, recv_sem=recv, device_id=peer, device_id_type=MESH
    )


def loop(count, body):
    def step(i, carry):
        body(i)
        return carry

    lax.fori_loop(0, count, step, 0)


ERF_TOP = (
    -2.72614225801306e-10, 2.77068142495902e-08, -2.10102402082508e-06, -5.69250639462346e-05,
    -7.34990630326855e-04, -2.95459980854025e-03, -1.60960333262415e-02,
)
ERF_BOTTOM = (
    -1.45660718464996e-05, -2.13374055278905e-04, -1.68282697438203e-03, -7.37332916720468e-03,
    -1.42647390514189e-02,
)


def normal_cdf(value):
    arg = jnp.clip(value * 0.7071067811865476, -3.832506856900711, 3.832506856900711)
    square = arg * arg
    top, bottom = jnp.full_like(arg, ERF_TOP[0]), jnp.full_like(arg, ERF_BOTTOM[0])
    for factor in ERF_TOP[1:]:
        top = top * square + factor
    for factor in ERF_BOTTOM[1:]:
        bottom = bottom * square + factor
    return 0.5 + 0.5 * (arg * top / bottom)


BACK_SCRATCH = dict(
    mine=pltpu.VMEM((4, 2, ROWS, 1024), BF16),
    r0=pltpu.VMEM((RING, 2, ROWS, 1024), BF16),
    r1=pltpu.VMEM((RING, ROWS, 1024), BF16),
    r2=pltpu.VMEM((RING, ROWS // 2, 1024), BF16),
    r3=pltpu.VMEM((RING, 3, ROWS // 8, 1024), BF16),
    held=pltpu.VMEM((RING, ROWS // 8, 1024), BF16),
    small=pltpu.VMEM((4, 24, 256), F32),
    s0=pltpu.VMEM((2, 24, 256), F32),
    s1=pltpu.VMEM((24, 256), F32),
    s2=pltpu.VMEM((24, 256), F32),
    s3=pltpu.VMEM((3, 24, 256), F32),
    own_sem=pltpu.SemaphoreType.DMA((4, 2)),
    c_send=pltpu.SemaphoreType.DMA((CHUNKS, 2)),
    c_recv=pltpu.SemaphoreType.DMA((CHUNKS, 2)),
    x_send=pltpu.SemaphoreType.DMA((CHUNKS,)),
    x_recv=pltpu.SemaphoreType.DMA((CHUNKS,)),
    y_send=pltpu.SemaphoreType.DMA((CHUNKS,)),
    y_recv=pltpu.SemaphoreType.DMA((CHUNKS,)),
    z_send=pltpu.SemaphoreType.DMA((CHUNKS, 3)),
    z_recv=pltpu.SemaphoreType.DMA((CHUNKS, 3)),
    a_send=pltpu.SemaphoreType.DMA((CHUNKS, 3)),
    a_recv=pltpu.SemaphoreType.DMA((CHUNKS, 3)),
    a_own=pltpu.SemaphoreType.DMA((CHUNKS,)),
    b_send=pltpu.SemaphoreType.DMA((CHUNKS,)),
    b_recv=pltpu.SemaphoreType.DMA((CHUNKS,)),
    t_send=pltpu.SemaphoreType.DMA((7,)),
    t_recv=pltpu.SemaphoreType.DMA((7,)),
    o_send=pltpu.SemaphoreType.DMA((2, 3)),
    o_recv=pltpu.SemaphoreType.DMA((2, 3)),
    o_own=pltpu.SemaphoreType.DMA((2,)),
    load_sem=pltpu.SemaphoreType.DMA((16,)),
    tile_sem=pltpu.SemaphoreType.DMA((2, 16)),
    weight_sem=pltpu.SemaphoreType.DMA((2,)),
    grad_sem=pltpu.SemaphoreType.DMA((2,)),
    x1=pltpu.VMEM((512, 1024), BF16),
    q1=pltpu.VMEM((512, 1024), BF16),
    k1=pltpu.VMEM((512, 1024), BF16),
    v1=pltpu.VMEM((512, 1024), BF16),
    o1=pltpu.VMEM((512, 1024), BF16),
    h1=pltpu.VMEM((512, 1024), BF16),
    q2=pltpu.VMEM((512, 1024), BF16),
    k2=pltpu.VMEM((256, 1024), BF16),
    v2=pltpu.VMEM((256, 1024), BF16),
    o2=pltpu.VMEM((512, 1024), BF16),
    h2=pltpu.VMEM((512, 1024), BF16),
    e1=pltpu.VMEM((256, 1024), BF16),
    cot=pltpu.VMEM((512, 1024), BF16),
    sum1=pltpu.VMEM((512, 1024), F32),
    sum2=pltpu.VMEM((512, 1024), F32),
    sum3=pltpu.VMEM((512, 1024), F32),
    dz=pltpu.VMEM((512, 1024), F32),
    low=pltpu.VMEM((512, 1024), BF16),
    dob=pltpu.VMEM((512, 1024), BF16),
    dqb=pltpu.VMEM((512, 1024), BF16),
    dkb=pltpu.VMEM((512, 1024), BF16),
    dvb=pltpu.VMEM((512, 1024), BF16),
    dka=pltpu.VMEM((512, 128), F32),
    dva=pltpu.VMEM((512, 128), F32),
    ut=pltpu.VMEM((2, 512, 512), F32),
    wd=pltpu.VMEM((2, 512, 1024), BF16),
    wu=pltpu.VMEM((2, 1024, 512), BF16),
    wb=pltpu.VMEM((2, 1024, 1024), BF16),
    gt=pltpu.VMEM((2, 512, 512), BF16),
    dut=pltpu.VMEM((512, 512), BF16),
    stage=pltpu.VMEM((2, 4, ROWS, 1024), BF16),
    sums=pltpu.VMEM((8, 1024), F32),
    ub=pltpu.VMEM((8, 1, 512), F32),
)
BACK_LOADS = (
    "x1", "q1", "k1", "v1", "o1", "h1", "q2", "k2", "v2", "o2", "h2", "e1", "cot", "sum1", "sum2", "sum3",
)


class Reducer:
    def __init__(self, s, parts, total, small_total):
        self.s, self.parts, self.total, self.small_total = s, parts, total, small_total
        z, y, x, c = self.at = place()
        self.core = device(z, y, x, 1 - c)
        self.xmate = device(z, y, 1 - x, c)
        self.diag = device(z, y, 1 - x, 1 - c)
        self.ymate = device(z, 1 - y, x, c)
        self.others = [device(lax.rem(z + i, 4), y, x, c) for i in (1, 2, 3)]

    def greet(self):
        greet([self.core, self.xmate, self.diag, self.ymate] + self.others)

    def core_copy(self, k, side):
        s, (_, _, _, c) = self.s, self.at
        return remote(
            self.parts.at[k, side * 2 + 1 - c], s.r0.at[lax.rem(k, RING), side],
            s.c_send.at[k, side], s.c_recv.at[k, side], self.core,
        )

    def own_copy(self, k, side):
        s, (_, _, _, c) = self.s, self.at
        slot = lax.rem(k, 4)
        return pltpu.make_async_copy(
            self.parts.at[k, side * 2 + c], s.mine.at[slot, side], s.own_sem.at[slot, side]
        )

    def fetch(self, k):
        for side in (0, 1):
            self.core_copy(k, side).start()
            self.own_copy(k, side).start()

    def x_copy(self, k):
        s, (_, _, x, _) = self.s, self.at
        slot = lax.rem(k, RING)
        return remote(s.r0.at[slot, 1 - x], s.r1.at[slot], s.x_send.at[k], s.x_recv.at[k], self.xmate)

    def core_sum(self, k):
        s, slot, near = self.s, lax.rem(k, RING), lax.rem(k, 4)
        for side in (0, 1):
            self.core_copy(k, side).wait()
            self.own_copy(k, side).wait()

        def add(i):
            piece = rows_at(i * 32, 32, 32)
            for side in (0, 1):
                s.r0[slot, side, piece, :] = s.r0[slot, side, piece, :] + s.mine[near, side, piece, :]

        loop(ROWS // 32, add)
        self.x_copy(k).start()

    def y_copy(self, k):
        s, (_, y, _, _) = self.s, self.at
        slot, half = lax.rem(k, RING), ROWS // 2
        return remote(
            s.r1.at[slot, rows_at((1 - y) * half, half, half), :], s.r2.at[slot],
            s.y_send.at[k], s.y_recv.at[k], self.ymate,
        )

    def x_sum(self, k):
        s, (_, _, x, _) = self.s, self.at
        slot = lax.rem(k, RING)
        self.x_copy(k).wait()

        def add(i):
            piece = rows_at(i * 32, 32, 32)
            s.r1[slot, piece, :] = s.r0[slot, x, piece, :] + s.r1[slot, piece, :]

        loop(ROWS // 32, add)
        self.y_copy(k).start()

    def z_copies(self, k):
        s, (z, _, _, _) = self.s, self.at
        slot, quarter = lax.rem(k, RING), ROWS // 8
        return [
            remote(
                s.r2.at[slot, rows_at(lax.rem(z + i + 1, 4) * quarter, quarter, quarter), :], s.r3.at[slot, i],
                s.z_send.at[k, i], s.z_recv.at[k, i], self.others[i],
            )
            for i in (0, 1, 2)
        ]

    def y_sum(self, k):
        s, (_, y, _, _) = self.s, self.at
        slot, half = lax.rem(k, RING), ROWS // 2
        self.y_copy(k).wait()

        def add(i):
            piece = rows_at(i * 32, 32, 32)
            s.r2[slot, piece, :] = s.r1[slot, rows_at(y * half + i * 32, 32, 32), :] + s.r2[slot, piece, :]

        loop(half // 32, add)
        for copy in self.z_copies(k):
            copy.start()

    def out_piece(self, k):
        z, y, _, _ = self.at
        return self.total.at[k, rows_at(y * (ROWS // 2) + z * (ROWS // 8), ROWS // 8, ROWS // 8), :]

    def spread_copies(self, k):
        s, slot = self.s, lax.rem(k, RING)
        return [
            remote(s.held.at[slot], self.out_piece(k), s.a_send.at[k, i], s.a_recv.at[k, i], self.others[i])
            for i in (0, 1, 2)
        ]

    def held_copy(self, k):
        return pltpu.make_async_copy(self.s.held.at[lax.rem(k, RING)], self.out_piece(k), self.s.a_own.at[k])

    def z_sum(self, k):
        s, (z, _, _, _) = self.s, self.at
        slot, quarter = lax.rem(k, RING), ROWS // 8
        for copy in self.z_copies(k):
            copy.wait()
        added = s.r2[slot, rows_at(z * quarter, quarter, quarter), :].astype(F32)
        for i in (0, 1, 2):
            added = added + s.r3[slot, i].astype(F32)
        s.held[slot] = added.astype(BF16)
        for copy in self.spread_copies(k):
            copy.start()
        self.held_copy(k).start()

    def half_copy(self, k):
        s, (_, y, _, _) = self.s, self.at
        half = ROWS // 2
        part = self.total.at[k, rows_at(y * half, half, half), :]
        return remote(part, part, s.b_send.at[k], s.b_recv.at[k], self.ymate)

    def spread_y(self, k):
        for copy in self.spread_copies(k):
            copy.wait()
        self.held_copy(k).wait()
        self.half_copy(k).start()

    def finish(self, k):
        self.half_copy(k).wait()

    def tick(self, t):
        stages = (self.fetch, self.core_sum, self.x_sum, self.y_sum, self.z_sum, self.spread_y, self.finish)
        for lag, act in zip(LAGS, stages):
            k = t - lag

            @pl.when((k >= 0) & (k < CHUNKS))
            def _(k=k, act=act):
                act(k)

    def small_steps(self, t):
        s, (_, _, x, c) = self.s, self.at
        send, recv = s.t_send, s.t_recv
        firsts = [
            remote(s.small.at[side * 2 + 1 - c], s.s0.at[side], send.at[side], recv.at[side], self.core)
            for side in (0, 1)
        ]
        across = remote(s.s0.at[1 - x], s.s1, send.at[2], recv.at[2], self.xmate)
        along = remote(s.s1, s.s2, send.at[3], recv.at[3], self.ymate)
        lasts = [
            remote(s.s2, s.s3.at[i], send.at[4 + i], recv.at[4 + i], self.others[i]) for i in (0, 1, 2)
        ]

        @pl.when(t == 0)
        def _():
            for copy in firsts:
                copy.start()

        @pl.when(t == 2)
        def _():
            for side in (0, 1):
                firsts[side].wait()
                s.s0[side] = s.s0[side] + s.small[side * 2 + c]
            across.start()

        @pl.when(t == 4)
        def _():
            across.wait()
            s.s1[...] = s.s1[...] + s.s0[x]
            along.start()

        @pl.when(t == 6)
        def _():
            along.wait()
            s.s2[...] = s.s2[...] + s.s1[...]
            for copy in lasts:
                copy.start()

        @pl.when(t == 8)
        def _():
            for copy in lasts:
                copy.wait()
            self.small_total[...] = s.s2[...] + s.s3[0] + s.s3[1] + s.s3[2]


def back_kernel(*refs):
    loads = dict(zip(BACK_LOADS, refs[:16]))
    d_all, g_all, f_in, f_out, f_up, f_down, gains, out_rows, mask = refs[16:25]
    total, small_total, grad_enc, out_back, grad_back, parts = refs[25:31]
    s = types.SimpleNamespace(**dict(zip(BACK_SCRATCH, refs[31:])))
    reducer = Reducer(s, parts, total, small_total)
    z, y, x, c = reducer.at
    mine = x * 2 + c
    peers = ((reducer.core, x * 2 + 1 - c), (reducer.xmate, (1 - x) * 2 + c), (reducer.diag, (1 - x) * 2 + 1 - c))

    def row_copies(which, src, dst):
        return [
            remote(
                src.at[rows_at(slot * 128, 128, 128), :], dst.at[mine],
                s.o_send.at[which, i], s.o_recv.at[which, i], peer,
            )
            for i, (peer, slot) in enumerate(peers)
        ] + [pltpu.make_async_copy(src.at[rows_at(mine * 128, 128, 128), :], dst.at[mine], s.o_own.at[which])]

    def load(name):
        return pltpu.make_async_copy(loads[name], getattr(s, name), s.load_sem.at[BACK_LOADS.index(name)])

    for name in ("sum3", "cot", "h2"):
        load(name).start()

    def tile_copies(j, slot):
        copies = []
        for i in range(4):
            columns = rows_at(i * 1024 + j * 128, 128, 128)
            copies += [
                pltpu.make_async_copy(
                    d_all.at[:, columns], s.ut.at[slot, :, pl.ds(i * 128, 128)], s.tile_sem.at[slot, i]
                ),
                pltpu.make_async_copy(
                    g_all.at[:, columns], s.gt.at[slot, :, pl.ds(i * 128, 128)], s.tile_sem.at[slot, 12 + i]
                ),
                pltpu.make_async_copy(
                    f_down.at[columns, :], s.wd.at[slot, pl.ds(i * 128, 128), :], s.tile_sem.at[slot, 4 + i]
                ),
                pltpu.make_async_copy(
                    f_up.at[:, columns], s.wu.at[slot, :, pl.ds(i * 128, 128)], s.tile_sem.at[slot, 8 + i]
                ),
            ]
        return copies

    for copy in tile_copies(0, 0):
        copy.start()
    weights = (
        f_out.at[1], f_in.at[4], f_in.at[5], f_in.at[3], f_out.at[0], f_in.at[0], f_in.at[1], f_in.at[2],
    )

    def weight(i):
        return pltpu.make_async_copy(weights[i], s.wb.at[i % 2], s.weight_sem.at[i % 2])

    reducer.greet()
    for copy in row_copies(0, out_rows, out_back):
        copy.start()
    for name in ("sum2", "o2", "q2", "k2", "v2", "h1", "e1", "sum1", "o1", "q1", "k1", "v1", "x1"):
        load(name).start()
    weight(0).start()
    weight(1).start()
    s.small[...] = jnp.zeros_like(s.small)

    def put(row, value):
        for i in range(4):
            s.small[i, row:row + 1, :] = value[:, i * 256:(i + 1) * 256]

    def norm_back(sum_ref, index, first, bias_row):
        s.sums[...] = jnp.zeros_like(s.sums)
        gain = gains[6 + index:7 + index, :]

        def block(i):
            p = rows_at(i * 32, 32, 32)
            value = sum_ref[p, :]
            grad = s.cot[p, :].astype(F32) * mask[p, 0:1] if first else s.dz[p, :]
            center = value - jnp.mean(value, axis=1, keepdims=True)
            scale = lax.rsqrt(jnp.mean(center * center, axis=1, keepdims=True) + epsilon)
            normal = center * scale
            scaled = grad * gain
            back = scale * (
                scaled - jnp.mean(scaled, axis=1, keepdims=True)
                - normal * jnp.mean(scaled * normal, axis=1, keepdims=True)
            )
            rounded = back.astype(BF16)
            s.dz[p, :] = back
            s.low[p, :] = rounded
            s.sums[0:1, :] += jnp.sum(grad * normal, axis=0, keepdims=True)
            s.sums[1:2, :] += jnp.sum(grad, axis=0, keepdims=True)
            s.sums[2:3, :] += jnp.sum(rounded.astype(F32), axis=0, keepdims=True)

        loop(16, block)
        put(6 + index, s.sums[0:1, :])
        put(9 + index, s.sums[1:2, :])
        put(bias_row, s.sums[2:3, :])

    def column_sums(ref, count, row):
        s.sums[...] = jnp.zeros_like(s.sums)

        def block(i):
            p = rows_at(i * 64, 64, 64)
            s.sums[0:1, :] += jnp.sum(ref[p, :].astype(F32), axis=0, keepdims=True)

        loop(count // 64, block)
        put(row, s.sums[0:1, :])

    pending = []

    def flush():
        if pending:
            pending.pop().wait()

    def store_grad(chunk, left, right):
        count = left.shape[0]
        flush()

        def block(i):
            product = dot_tn(left[:, rows_at(i * 256, 256, 256)], right[0:count, :]).astype(BF16)
            s.stage[0, i] = product[:128]
            s.stage[1, i] = product[128:]

        loop(4, block)
        pending.append(pltpu.make_async_copy(s.stage, parts.at[pl.ds(chunk, 2)], s.grad_sem.at[0]))
        pending[-1].start()

    load("sum3").wait()
    load("cot").wait()
    norm_back(s.sum3, 2, True, 16)
    load("h2").wait()

    def down_save(j):
        return pltpu.make_async_copy(s.stage.at[0], parts.at[2 * j], s.grad_sem.at[0])

    def up_save(j):
        return pltpu.make_async_copy(s.stage.at[1], parts.at[2 * j + 1], s.grad_sem.at[1])

    def tile(j):
        slot = lax.rem(j, 2)
        for copy in tile_copies(j, slot):
            copy.wait()

        @pl.when(j < 7)
        def _():
            for copy in tile_copies(j + 1, 1 - slot):
                copy.start()

        def hidden(i):
            p = rows_at(i * 256, 256, 256)
            grad = dot_nt(s.low[...], s.wd[slot, p, :])
            rounded = (grad * s.ut[slot, :, p]).astype(BF16)
            s.dut[:, p] = rounded
            s.ub[j, :, p] = jnp.sum(rounded.astype(F32), axis=0, keepdims=True)

        loop(2, hidden)

        def down(i):
            product = dot_tn(s.gt[slot, :, rows_at(i * 256, 256, 256)], s.low[...]).astype(BF16)
            s.stage[0, 2 * i] = product[:128]
            s.stage[0, 2 * i + 1] = product[128:]

        loop(2, down)
        down_save(j).start()

        def up(i):
            product = dot_tn(s.h2[:, rows_at(i * 256, 256, 256)], s.dut[...]).astype(BF16)
            s.stage[1, i, :, 0:512] = product[:128]
            s.stage[1, i, :, 512:1024] = product[128:]

        loop(4, up)
        up_save(j).start()

        def back(i):
            p = rows_at(i * 256, 256, 256)
            s.dz[:, p] += dot_nt(s.dut[...], s.wu[slot, p, :])

        loop(4, back)
        down_save(j).wait()
        up_save(j).wait()
        loop(2 - lax.rem(j, 2), lambda i: reducer.tick((3 * j + 1) // 2 + i))

    loop(8, tile)
    for j in range(8):
        for i in range(4):
            s.small[i, 12 + j // 2:13 + j // 2, (j % 2) * 128:(j % 2) * 128 + 128] = s.ub[j, :, i * 128:(i + 1) * 128]
    load("sum2").wait()
    norm_back(s.sum2, 1, False, 5)
    reducer.tick(12)
    load("o2").wait()
    store_grad(16, s.o2, s.low)

    def times_weight(dst, left, count, slot):
        def block(i):
            p = rows_at(i * 256, 256, 256)
            dst[:, p] = dot_nt(left[...], s.wb[slot, p, :]).astype(BF16)

        loop(count, block)

    def add_weight(left, slot):
        def block(i):
            p = rows_at(i * 256, 256, 256)
            s.dz[:, p] += dot_nt(left[...], s.wb[slot, p, :])

        loop(4, block)

    weight(0).wait()
    times_weight(s.dob, s.low, 4, 0)
    weight(2).start()
    flush()
    reducer.tick(13)
    for name in ("q2", "k2", "v2"):
        load(name).wait()

    lane = lax.broadcasted_iota(jnp.int32, (1, 128), 1)
    head_masks = [(lane < 64).astype(F32).astype(BF16), (lane >= 64).astype(F32).astype(BF16)]

    def attention_pair(i, q_ref, k_ref, v_ref, key_count, causal):
        lanes = rows_at(i * 128, 128, 128)
        s.dka[...] = jnp.zeros_like(s.dka)
        s.dva[...] = jnp.zeros_like(s.dva)
        for block in (0, 1):
            rows = pl.ds(block * 256, 256)
            reach = (block + 1) * 256 if causal else key_count
            query, grad = q_ref[rows, lanes], s.dob[rows, lanes]
            key, value = k_ref[0:reach, lanes], v_ref[0:reach, lanes]
            query_grad = jnp.zeros((256, 128), F32)
            for mask in head_masks:
                query_one, grad_one = query * mask, grad * mask
                scores = dot_nt(key, query_one) * 0.125
                if causal:
                    key_at = lax.broadcasted_iota(jnp.int32, (reach, 256), 0)
                    query_at = lax.broadcasted_iota(jnp.int32, (reach, 256), 1) + block * 256
                    scores = jnp.where(key_at <= query_at, scores, -1e30)
                peak = jnp.max(scores, axis=0, keepdims=True)
                full = jnp.exp(scores - peak)
                full = full * (1.0 / jnp.sum(full, axis=0, keepdims=True))
                full_grad = dot_nt(value, grad_one)
                row_dot = jnp.sum(full * full_grad, axis=0, keepdims=True)
                score_grad = (full * (full_grad - row_dot)).astype(BF16)
                s.dva[0:reach, :] += dot_nn(full.astype(BF16), grad_one)
                s.dka[0:reach, :] += dot_nn(score_grad, query_one)
                query_grad = query_grad + dot_tn(score_grad, key * mask)
            s.dqb[rows, lanes] = (query_grad * 0.125).astype(BF16)
        s.dkb[0:key_count, lanes] = (s.dka[0:key_count, :] * 0.125).astype(BF16)
        s.dvb[0:key_count, lanes] = s.dva[0:key_count, :].astype(BF16)

    def cross(i):
        attention_pair(i, s.q2, s.k2, s.v2, 256, False)

        @pl.when((lax.rem(i, 2) == 1) & (i < 7))
        def _():
            reducer.tick(14 + i // 2)

    loop(8, cross)
    load("h1").wait()
    load("e1").wait()
    store_grad(18, s.h1, s.dqb)
    reducer.tick(17)
    store_grad(20, s.e1, s.dkb)
    reducer.tick(18)
    store_grad(22, s.e1, s.dvb)
    reducer.tick(19)
    column_sums(s.dqb, 512, 3)
    column_sums(s.dvb, 256, 4)
    weight(1).wait()
    weight(2).wait()

    def enc_block(i):
        p = rows_at(i * 256, 256, 256)
        grad_enc[:, p] = (
            dot_nt(s.dkb[0:256, :], s.wb[1, p, :]) + dot_nt(s.dvb[0:256, :], s.wb[0, p, :])
        ).astype(BF16)

    loop(4, enc_block)
    flush()
    reducer.tick(20)
    weight(3).start()
    weight(4).start()
    weight(3).wait()
    add_weight(s.dqb, 1)
    weight(5).start()
    reducer.tick(21)
    load("sum1").wait()
    norm_back(s.sum1, 0, False, 2)
    load("o1").wait()
    store_grad(24, s.o1, s.low)
    reducer.tick(22)
    weight(4).wait()
    times_weight(s.dob, s.low, 4, 0)
    weight(6).start()
    flush()
    reducer.tick(23)
    for name in ("q1", "k1", "v1"):
        load(name).wait()

    def own(i):
        attention_pair(i, s.q1, s.k1, s.v1, 512, True)

        @pl.when(lax.rem(i, 3) == 2)
        def _():
            reducer.tick(24 + i // 3)

    loop(8, own)
    load("x1").wait()
    store_grad(26, s.x1, s.dqb)
    store_grad(28, s.x1, s.dkb)
    reducer.tick(26)
    store_grad(30, s.x1, s.dvb)
    reducer.tick(27)
    column_sums(s.dqb, 512, 0)
    column_sums(s.dvb, 512, 1)
    flush()
    reducer.tick(28)
    weight(5).wait()
    add_weight(s.dqb, 1)
    weight(7).start()
    reducer.tick(29)
    weight(6).wait()
    add_weight(s.dkb, 0)
    reducer.tick(30)
    weight(7).wait()

    def last(i):
        p = rows_at(i * 256, 256, 256)
        s.low[:, p] = (s.dz[:, p] + dot_nt(s.dvb[...], s.wb[1, p, :])).astype(BF16)

    loop(4, last)
    for copy in row_copies(1, s.low, grad_back):
        copy.start()

    def drain(i):
        reducer.tick(31 + i)
        reducer.small_steps(i)

    loop(max(9, CHUNKS + LAGS[-1] - 31), drain)
    for copy in row_copies(0, out_rows, out_back) + row_copies(1, s.low, grad_back):
        copy.wait()


def backward(loads, *rest):
    any_space = pl.BlockSpec(memory_space=pl.ANY)
    in_vmem = pl.BlockSpec(memory_space=pltpu.VMEM)
    return pl.pallas_call(
        back_kernel,
        out_shape=(
            jax.ShapeDtypeStruct((CHUNKS, ROWS, 1024), BF16),
            jax.ShapeDtypeStruct((24, 256), F32),
            jax.ShapeDtypeStruct((256, 1024), BF16),
            jax.ShapeDtypeStruct((4, 128, 1024), BF16),
            jax.ShapeDtypeStruct((4, 128, 1024), BF16),
            jax.ShapeDtypeStruct((CHUNKS, 4, ROWS, 1024), BF16),
        ),
        in_specs=[any_space] * 22 + [in_vmem] * 3,
        out_specs=(any_space, in_vmem, in_vmem, any_space, any_space, any_space),
        scratch_shapes=list(BACK_SCRATCH.values()),
        compiler_params=pltpu.CompilerParams(
            collective_id=1, has_side_effects=True, vmem_limit_bytes=62 << 20
        ),
    )(*[loads[name] for name in BACK_LOADS], *rest)


FORWARD_SCRATCH = dict(
    v_in=pltpu.VMEM((6, 1024, 1024), BF16),
    v_out=pltpu.VMEM((2, 1024, 1024), BF16),
    v_up=pltpu.VMEM((1024, 4096), BF16),
    v_down=pltpu.VMEM((4096, 1024), BF16),
    v_small=pltpu.VMEM((4, 24, 256), F32),
    vec=pltpu.VMEM((24, 1024), F32),
    x=pltpu.VMEM((512, 1024), BF16),
    e=pltpu.VMEM((256, 1024), BF16),
    q=pltpu.VMEM((512, 1024), BF16),
    k=pltpu.VMEM((512, 1024), BF16),
    v=pltpu.VMEM((512, 1024), BF16),
    o=pltpu.VMEM((512, 1024), BF16),
    h1=pltpu.VMEM((512, 1024), BF16),
    q2=pltpu.VMEM((512, 1024), BF16),
    k2=pltpu.VMEM((256, 1024), BF16),
    v2=pltpu.VMEM((256, 1024), BF16),
    o2=pltpu.VMEM((512, 1024), BF16),
    h2=pltpu.VMEM((512, 1024), BF16),
    y=pltpu.VMEM((512, 1024), BF16),
    hf=pltpu.VMEM((512, 1024), F32),
    sum_a=pltpu.VMEM((512, 1024), F32),
    sum_b=pltpu.VMEM((512, 1024), F32),
    ublock=pltpu.VMEM((512, 256), F32),
    gblock=pltpu.VMEM((2, 512, 256), BF16),
    dblock=pltpu.VMEM((2, 512, 256), F32),
    own_sem=pltpu.SemaphoreType.DMA((16,)),
    x_send=pltpu.SemaphoreType.DMA((16,)),
    x_recv=pltpu.SemaphoreType.DMA((16,)),
    y_send=pltpu.SemaphoreType.DMA((16, 2)),
    y_recv=pltpu.SemaphoreType.DMA((16, 2)),
    z_send=pltpu.SemaphoreType.DMA((16, 2)),
    z_recv=pltpu.SemaphoreType.DMA((16, 2)),
    c_send=pltpu.SemaphoreType.DMA((16, 2)),
    c_recv=pltpu.SemaphoreType.DMA((16, 2)),
    t_send=pltpu.SemaphoreType.DMA((3, 3)),
    t_recv=pltpu.SemaphoreType.DMA((3, 3)),
    t_own=pltpu.SemaphoreType.DMA((4,)),
    save_sem=pltpu.SemaphoreType.DMA((16,)),
    weight_sem=pltpu.SemaphoreType.DMA((16,)),
    block_sem=pltpu.SemaphoreType.DMA((2, 2)),
)
SAVED = ("x", "q", "k", "v", "o", "h1", "q2", "k2", "v2", "o2", "h2", "sum1", "sum2", "sum3", "y")
GATHER_ORDER = (0, 1, 2, 6, 4, 5, 3, 7, 8, 9, 10, 11, 12, 13, 14, 15)


def weight_rows(refs, k, shard, start, size):
    if k < 6:
        return refs[0].at[k, rows_at(shard * 256 + start, size, 8), :]
    if k < 8:
        return refs[1].at[k - 6, rows_at(shard * 256 + start, size, 8), :]
    if k < 12:
        return refs[2].at[rows_at(shard * 256 + (k - 8) * 64 + start, size, 8), :]
    return refs[3].at[rows_at(shard * 1024 + (k - 12) * 256 + start, size, 8), :]


class Gatherer:
    def __init__(self, s, shards, full):
        self.s, self.shards, self.full, self.done = s, shards, full, -4
        z, y, x, c = self.at = place()
        self.side = lax.rem(z, 2)
        self.core = device(z, y, x, 1 - c)
        self.xmate = device(z, y, 1 - x, c)
        self.diag = device(z, y, 1 - x, 1 - c)
        self.ymate = device(z, 1 - y, x, c)
        self.zmate = device(z + 1 - 2 * self.side, y, x, c)
        self.mine, self.other = x * 2 + c, (1 - x) * 2 + c

    def greet(self):
        greet([self.core, self.xmate, self.diag, self.ymate, self.zmate])

    def size(self, k):
        return 64 if 8 <= k < 12 else 256

    def x_copy(self, k):
        n = self.size(k) // 4
        q = (self.at[1] * 2 + self.side) * n
        return remote(
            weight_rows(self.shards, k, 0, q, n), weight_rows(self.full, k, self.mine, q, n),
            self.s.x_send.at[k], self.s.x_recv.at[k], self.xmate,
        )

    def core_copy(self, k):
        return remote(
            weight_rows(self.shards, k, 0, 0, self.size(k)), weight_rows(self.full, k, self.mine, 0, self.size(k)),
            self.s.c_send.at[k, 0], self.s.c_recv.at[k, 0], self.core,
        )

    def own_copy(self, k):
        return pltpu.make_async_copy(
            weight_rows(self.shards, k, 0, 0, self.size(k)), weight_rows(self.full, k, self.mine, 0, self.size(k)),
            self.s.own_sem.at[k],
        )

    def relay(self, k, start, n, send, recv, peer):
        view = weight_rows(self.full, k, self.other, start, n)
        return remote(view, view, send, recv, peer)

    def first_hops(self, k):
        s, n = self.s, self.size(k) // 4
        q = (self.at[1] * 2 + self.side) * n
        return [
            self.relay(k, q, n, s.y_send.at[k, 0], s.y_recv.at[k, 0], self.ymate),
            self.relay(k, q, n, s.z_send.at[k, 0], s.z_recv.at[k, 0], self.zmate),
        ]

    def second_hops(self, k):
        s, n, y = self.s, self.size(k) // 4, self.at[1]
        return [
            self.relay(k, (y * 2 + 1 - self.side) * n, n // 2, s.y_send.at[k, 1], s.y_recv.at[k, 1], self.ymate),
            self.relay(
                k, ((1 - y) * 2 + self.side) * n + n // 2, n // 2, s.z_send.at[k, 1], s.z_recv.at[k, 1], self.zmate
            ),
        ]

    def last_hop(self, k):
        return self.relay(k, 0, self.size(k), self.s.c_send.at[k, 1], self.s.c_recv.at[k, 1], self.core)

    def step(self, t):
        def chunk(lag):
            return GATHER_ORDER[t - lag] if 0 <= t - lag < 16 else None

        if (k := chunk(-3)) is not None:
            self.x_copy(k).start()
            self.core_copy(k).start()
            self.own_copy(k).start()
        if (k := chunk(0)) is not None:
            self.x_copy(k).wait()
            for copy in self.first_hops(k):
                copy.start()
        if (k := chunk(1)) is not None:
            for copy in self.first_hops(k):
                copy.wait()
            for copy in self.second_hops(k):
                copy.start()
        if (k := chunk(2)) is not None:
            for copy in self.second_hops(k):
                copy.wait()
            self.last_hop(k).start()
        if (k := chunk(3)) is not None:
            self.last_hop(k).wait()
            self.core_copy(k).wait()
            self.own_copy(k).wait()

    def advance(self, t):
        while self.done < t:
            self.done += 1
            self.step(self.done)

    def ready(self, index):
        self.advance(index + 3)


def forward_kernel(*refs):
    w_in, w_out, w_up, w_down, small, tok, cot, enc, mask = refs[:9]
    f_in, f_out, f_up, f_down, f_cot, gains, g_all, d_all = refs[9:17]
    saved = dict(zip(SAVED, refs[17:32]))
    s = types.SimpleNamespace(**dict(zip(FORWARD_SCRATCH, refs[32:])))
    full = (s.v_in, s.v_out, s.v_up, s.v_down)
    gather = Gatherer(s, (w_in, w_out, w_up, w_down), full)
    mine, (_, _, x, c) = gather.mine, gather.at
    peers = ((gather.core, x * 2 + 1 - c), (gather.xmate, gather.other), (gather.diag, (1 - x) * 2 + 1 - c))

    def rows_of(index):
        return rows_at(index * 128, 128, 128)

    def token_copies():
        return [
            remote(tok.at[slot], s.x.at[rows_of(mine), :], s.t_send.at[0, i], s.t_recv.at[0, i], peer)
            for i, (peer, slot) in enumerate(peers)
        ] + [
            remote(small, s.v_small.at[mine], s.t_send.at[2, i], s.t_recv.at[2, i], peer)
            for i, (peer, slot) in enumerate(peers)
        ] + [
            pltpu.make_async_copy(tok.at[mine], s.x.at[rows_of(mine), :], s.t_own.at[0]),
            pltpu.make_async_copy(small, s.v_small.at[mine], s.t_own.at[1]),
        ]

    def cot_copies():
        return [
            remote(cot.at[slot], f_cot.at[mine], s.t_send.at[1, i], s.t_recv.at[1, i], peer)
            for i, (peer, slot) in enumerate(peers)
        ] + [pltpu.make_async_copy(cot.at[mine], f_cot.at[mine], s.t_own.at[2])]

    enc_copy = pltpu.make_async_copy(enc, s.e, s.t_own.at[3])
    gather.greet()
    enc_copy.start()
    gather.advance(-2)
    for copy in token_copies():
        copy.start()

    def save(name, ref):
        return pltpu.make_async_copy(ref, saved[name], s.save_sem.at[SAVED.index(name)])

    def weight_saves(k):
        if k < 6:
            return [pltpu.make_async_copy(s.v_in.at[k], f_in.at[k], s.weight_sem.at[k])]
        if k < 8:
            return [pltpu.make_async_copy(s.v_out.at[k - 6], f_out.at[k - 6], s.weight_sem.at[k])]
        if k == 11:
            return [pltpu.make_async_copy(s.v_up, f_up, s.weight_sem.at[k])]
        if k == 15:
            return [pltpu.make_async_copy(s.v_down, f_down, s.weight_sem.at[k])]
        return []

    def ready(index):
        gather.ready(index)
        for copy in weight_saves(GATHER_ORDER[index]):
            copy.start()

    def project(dst, left, weight, count, bias):
        def block(i):
            columns = rows_at(i * 256, 256, 256)
            product = dot_nn(left[0:count, :], weight[:, columns])
            if bias is not None:
                product = product + s.vec[bias:bias + 1, columns]
            dst[0:count, columns] = product.astype(BF16)

        loop(4, block)

    def join(dst, base, left, weight, bias):
        def block(i):
            columns = rows_at(i * 256, 256, 256)
            dst[:, columns] = base[:, columns].astype(F32) + (
                dot_nn(left[...], weight[:, columns]) + s.vec[bias:bias + 1, columns]
            )

        loop(4, block)

    def normalize(sum_ref, index, low, last):
        gain, shift = s.vec[6 + index:7 + index, :], s.vec[9 + index:10 + index, :]

        def block(i):
            p = rows_at(i * 32, 32, 32)
            value = sum_ref[p, :]
            center = value - jnp.mean(value, axis=1, keepdims=True)
            scale = lax.rsqrt(jnp.mean(center * center, axis=1, keepdims=True) + epsilon)
            result = center * scale * gain + shift
            if last:
                low[p, :] = (result * mask[p, 0:1]).astype(BF16)
            else:
                s.hf[p, :] = result
                low[p, :] = result.astype(BF16)

        loop(16, block)

    lane = lax.broadcasted_iota(jnp.int32, (1, 128), 1)
    head_masks = [(lane < 64).astype(F32).astype(BF16), (lane >= 64).astype(F32).astype(BF16)]

    def attend_pair(i, q_ref, k_ref, v_ref, o_ref, key_count, causal):
        lanes = rows_at(i * 128, 128, 128)
        for block in (0, 1):
            rows = pl.ds(block * 256, 256)
            reach = (block + 1) * 256 if causal else key_count
            query = q_ref[rows, lanes]
            key, value = k_ref[0:reach, lanes], v_ref[0:reach, lanes]
            context = jnp.zeros((256, 128), F32)
            for head_mask in head_masks:
                scores = dot_nt(query * head_mask, key) * 0.125
                if causal:
                    query_at = lax.broadcasted_iota(jnp.int32, (256, reach), 0) + block * 256
                    key_at = lax.broadcasted_iota(jnp.int32, (256, reach), 1)
                    scores = jnp.where(key_at <= query_at, scores, -1e30)
                weights = jnp.exp(scores - jnp.max(scores, axis=1, keepdims=True))
                weights = weights * (1.0 / jnp.sum(weights, axis=1, keepdims=True))
                context = context + dot_nn(weights.astype(BF16), value * head_mask)
            o_ref[rows, lanes] = context.astype(BF16)

    ready(0)
    for copy in token_copies():
        copy.wait()
    for i in range(4):
        s.vec[:, i * 256:(i + 1) * 256] = s.v_small[i]
    gains[...] = s.vec[0:16, :]
    save("x", s.x).start()
    project(s.q, s.x, s.v_in.at[0], 512, 0)
    save("q", s.q).start()
    ready(1)
    project(s.k, s.x, s.v_in.at[1], 512, None)
    save("k", s.k).start()
    ready(2)
    project(s.v, s.x, s.v_in.at[2], 512, 1)
    save("v", s.v).start()
    for part in range(4):
        loop(2, lambda i, part=part: attend_pair(part * 2 + i, s.q, s.k, s.v, s.o, 512, True))
        gather.advance(6 + part)
    save("o", s.o).start()
    ready(3)
    join(s.sum_a, s.x, s.o, s.v_out.at[0], 2)
    save("sum1", s.sum_a).start()
    ready(4)
    normalize(s.sum_a, 0, s.h1, False)
    save("h1", s.h1).start()
    enc_copy.wait()
    project(s.k2, s.e, s.v_in.at[4], 256, None)
    save("k2", s.k2).start()
    ready(5)
    project(s.v2, s.e, s.v_in.at[5], 256, 4)
    save("v2", s.v2).start()
    ready(6)
    project(s.q2, s.h1, s.v_in.at[3], 512, 3)
    save("q2", s.q2).start()
    ready(7)
    for part in range(4):
        loop(2, lambda i, part=part: attend_pair(part * 2 + i, s.q2, s.k2, s.v2, s.o2, 256, False))
        gather.advance(11 + part // 2)
    save("o2", s.o2).start()
    join(s.sum_b, s.hf, s.o2, s.v_out.at[1], 5)
    save("sum2", s.sum_b).start()
    ready(10)
    normalize(s.sum_b, 1, s.h2, False)
    save("h2", s.h2).start()
    for copy in cot_copies():
        copy.start()
    save("sum1", s.sum_a).wait()

    def widen(i):
        p = rows_at(i * 64, 64, 64)
        s.sum_a[p, :] = s.hf[p, :] + s.vec[16:17, :]

    loop(8, widen)
    ready(11)

    def block_copies(j, i, slot):
        columns = rows_at(i * 1024 + j * 256, 256, 256)
        return [
            pltpu.make_async_copy(s.gblock.at[slot], g_all.at[:, columns], s.block_sem.at[slot, 0]),
            pltpu.make_async_copy(s.dblock.at[slot], d_all.at[:, columns], s.block_sem.at[slot, 1]),
        ]

    for j in range(4):
        ready(12 + j)

        def mlp(i, j=j):
            slot = lax.rem(i, 2)
            columns = rows_at(i * 1024 + j * 256, 256, 256)
            if j > 0:
                for copy in block_copies(j, i, slot):
                    copy.wait()
            else:
                @pl.when(i >= 2)
                def _():
                    for copy in block_copies(j, i, slot):
                        copy.wait()

            s.ublock[...] = dot_nn(s.h2[...], s.v_up[:, columns])
            bias = s.v_small[i, 12 + j:13 + j, :]

            def hidden(r):
                p = rows_at(r * 64, 64, 64)
                value = s.ublock[p, :] + bias
                cdf = normal_cdf(value)
                pdf = jnp.exp(-0.5 * value * value) * 0.3989422804014327
                s.gblock[slot, p, :] = (value * cdf).astype(BF16)
                s.dblock[slot, p, :] = cdf + value * pdf

            loop(8, hidden)
            for copy in block_copies(j, i, slot):
                copy.start()

            def out(n):
                wide = rows_at(n * 256, 256, 256)
                s.sum_a[:, wide] += dot_nn(s.gblock[slot], s.v_down[columns, wide])

            loop(4, out)

        loop(4, mlp)

    save("sum3", s.sum_a).start()
    normalize(s.sum_a, 2, s.y, True)
    save("y", s.y).start()
    for copy in block_copies(3, 2, 0) + block_copies(3, 3, 1) + cot_copies():
        copy.wait()
    for k in range(16):
        for copy in weight_saves(k):
            copy.wait()
    ends = dict(
        x=s.x, q=s.q, k=s.k, v=s.v, o=s.o, h1=s.h1, q2=s.q2, k2=s.k2, v2=s.v2, o2=s.o2, h2=s.h2,
        sum2=s.sum_b, sum3=s.sum_a, y=s.y,
    )
    for name, ref in ends.items():
        save(name, ref).wait()


def forward(w_in, w_out, w_up, w_down, small, tok, cot, enc, mask):
    any_space = pl.BlockSpec(memory_space=pl.ANY)
    in_vmem = pl.BlockSpec(memory_space=pltpu.VMEM)
    wide = {"sum1", "sum2", "sum3"}
    return pl.pallas_call(
        forward_kernel,
        out_shape=(
            jax.ShapeDtypeStruct((6, 1024, 1024), BF16),
            jax.ShapeDtypeStruct((2, 1024, 1024), BF16),
            jax.ShapeDtypeStruct((1024, 4096), BF16),
            jax.ShapeDtypeStruct((4096, 1024), BF16),
            jax.ShapeDtypeStruct((4, 128, 1024), BF16),
            jax.ShapeDtypeStruct((16, 1024), F32),
            jax.ShapeDtypeStruct((512, 4096), BF16),
            jax.ShapeDtypeStruct((512, 4096), F32),
        ) + tuple(
            jax.ShapeDtypeStruct((256 if name in ("k2", "v2") else 512, 1024), F32 if name in wide else BF16)
            for name in SAVED
        ),
        in_specs=[any_space] * 8 + [in_vmem],
        out_specs=(any_space,) * 5 + (in_vmem,) + (any_space,) * 17,
        scratch_shapes=list(FORWARD_SCRATCH.values()),
        compiler_params=pltpu.CompilerParams(
            collective_id=2, has_side_effects=True, vmem_limit_bytes=62 << 20
        ),
    )(w_in, w_out, w_up, w_down, small, tok, cot, enc, mask)


def sum_plain(*parts):
    dims = (1, 1, 1, 1, 1, 0, 0, 0, 0)
    scattered = [
        lax.psum_scatter(part.astype(jnp.bfloat16), "shard", scatter_dimension=dim, tiled=True)
        for part, dim in zip(parts, dims)
    ]
    return tuple(lax.psum(part, "rep").astype(jnp.float32) for part in scattered)


def fast_layer(
    sent_tokens, sent_grads, encoder, length, owner_row, attn_in, attn_out, attn_bias,
    norm_gain, norm_bias, mlp_in, mlp_bias_in, mlp_out, mlp_bias_out,
):
    packed = jnp.concatenate(
        [attn_bias, norm_gain, norm_bias, mlp_bias_in.reshape(4, 256), mlp_bias_out[None],
         jnp.zeros((7, 256), BF16)], axis=0,
    ).astype(F32)
    mask = jnp.broadcast_to(
        (jnp.arange(512, dtype=jnp.int32) < length).astype(F32)[:, None], (512, 128)
    )
    full_in, full_out, up_full, down_full, cot, vectors, g_all, d_all, *saved = forward(
        attn_in, attn_out, mlp_in, mlp_out, packed, sent_tokens, sent_grads, encoder, mask
    )
    saved = dict(zip(SAVED, saved))
    loads = dict(
        x1=saved["x"], q1=saved["q"], k1=saved["k"], v1=saved["v"], o1=saved["o"], h1=saved["h1"],
        q2=saved["q2"], k2=saved["k2"], v2=saved["v2"], o2=saved["o2"], h2=saved["h2"], e1=encoder,
        cot=cot.reshape(512, 1024), sum1=saved["sum1"], sum2=saved["sum2"], sum3=saved["sum3"],
    )
    total, small_total, encoder_grad, back_blocks, grad_blocks, _ = backward(
        loads, d_all, g_all, full_in, full_out, up_full, down_full, vectors, saved["y"], mask
    )
    total = total.astype(F32)
    pairs = total[:16].reshape(8, 2, 128, 1024)
    return (
        pick_blocks(back_blocks, owner_row),
        pick_blocks(grad_blocks, owner_row),
        encoder_grad[None],
        jnp.concatenate([total[26:], total[18:24]]).reshape(6, 256, 1024),
        jnp.concatenate([total[24:26], total[16:18]]).reshape(2, 256, 1024),
        small_total[:6],
        small_total[6:9],
        small_total[9:12],
        pairs[:, 1].reshape(8, 128, 2, 4, 128).transpose(2, 1, 3, 0, 4).reshape(256, 4096),
        small_total[12:16].reshape(1024),
        pairs[:, 0].reshape(1024, 1024),
        small_total[16],
    )


def local(
    tokens,
    enc_states,
    cotangent,
    lengths,
    owner,
    attn_in,
    attn_out,
    attn_bias,
    norm_gain,
    norm_bias,
    mlp_in,
    mlp_bias_in,
    mlp_out,
    mlp_bias_out,
):
    groups = lax.axis_size("shard")
    my_index = lax.axis_index("shard")
    owner_row = owner[0]
    slot_ids = jnp.arange(groups, dtype=jnp.int32)
    matches = owner_row[None, :] == slot_ids[:, None]
    sequence_at = jnp.sum(jnp.where(matches, slot_ids[None, :], 0), axis=1)
    my_sequence = jnp.sum(jnp.where(slot_ids == my_index, sequence_at, 0))
    my_length = jnp.sum(jnp.where(slot_ids == my_sequence, lengths[0], 0))
    sent_tokens = pick_blocks(tokens, sequence_at)
    sent_grads = pick_blocks(cotangent, sequence_at)
    if (lax.axis_size("rep"), groups) == (8, 4):
        return fast_layer(
            sent_tokens, sent_grads, enc_states[0], my_length, owner_row, attn_in, attn_out, attn_bias,
            norm_gain, norm_bias, mlp_in, mlp_bias_in, mlp_out, mlp_bias_out,
        )
    got_tokens, got_grads = (
        lax.all_to_all(sent_tokens, "shard", split_axis=0, concat_axis=1, tiled=True),
        lax.all_to_all(sent_grads, "shard", split_axis=0, concat_axis=1, tiled=True),
    )
    full_in, full_out, full_bias, full_gain, full_shift = (
        lax.all_gather(attn_in, "shard", axis=1, tiled=True),
        lax.all_gather(attn_out, "shard", axis=1, tiled=True),
        lax.all_gather(attn_bias, "shard", axis=1, tiled=True),
        lax.all_gather(norm_gain, "shard", axis=1, tiled=True),
        lax.all_gather(norm_bias, "shard", axis=1, tiled=True),
    )
    bias_rows = full_bias.astype(jnp.float32)
    gain_rows = full_gain.astype(jnp.float32)
    shift_rows = full_shift.astype(jnp.float32)
    up_full, up_bias, down_full, down_bias = (
        lax.all_gather(mlp_in, "shard", axis=0, tiled=True),
        lax.all_gather(mlp_bias_in, "shard", axis=0, tiled=True),
        lax.all_gather(mlp_out, "shard", axis=0, tiled=True),
        lax.all_gather(mlp_bias_out, "shard", axis=0, tiled=True),
    )
    in_back, out_back, up_back, down_back = full_in, full_out, up_full, down_full
    inputs = got_tokens[0]
    row_count = inputs.shape[0]
    row_mask = (jnp.arange(row_count, dtype=jnp.int32) < my_length).astype(jnp.float32)[:, None]
    encoder = enc_states[0]
    projected = jnp.einsum("rd,wde->wre", inputs, full_in[:3], preferred_element_type=jnp.float32)
    queries = (projected[0] + bias_rows[0]).astype(jnp.bfloat16)
    keys = projected[1].astype(jnp.bfloat16)
    values = (projected[2] + bias_rows[1]).astype(jnp.bfloat16)
    context, log_totals = attention_forward(queries, keys, values, True)
    first_sum = inputs.astype(jnp.float32) + (matmul(context, full_out[0]) + bias_rows[2])
    first_norm = layer_norm(first_sum, gain_rows[0], shift_rows[0])
    first_low = first_norm.astype(jnp.bfloat16)
    cross_queries = (matmul(first_low, full_in[3]) + bias_rows[3]).astype(jnp.bfloat16)
    cross_projected = jnp.einsum(
        "rd,wde->wre", encoder, full_in[4:6], preferred_element_type=jnp.float32
    )
    cross_keys = cross_projected[0].astype(jnp.bfloat16)
    cross_values = (cross_projected[1] + bias_rows[4]).astype(jnp.bfloat16)
    cross_context, cross_totals = attention_forward(cross_queries, cross_keys, cross_values, False)
    second_sum = first_norm + (matmul(cross_context, full_out[1]) + bias_rows[5])
    second_norm = layer_norm(second_sum, gain_rows[1], shift_rows[1])
    second_low = second_norm.astype(jnp.bfloat16)
    hidden_pre = matmul(second_low, up_full) + up_bias.astype(jnp.float32)
    hidden_low = gelu_exact(hidden_pre).astype(jnp.bfloat16)
    third_sum = second_norm + (matmul(hidden_low, down_full) + down_bias.astype(jnp.float32))
    result = (layer_norm(third_sum, gain_rows[2], shift_rows[2]) * row_mask).astype(jnp.bfloat16)
    back_blocks = lax.all_to_all(result[None], "shard", split_axis=1, concat_axis=0, tiled=True)
    output = pick_blocks(back_blocks, owner_row)
    out_grad = got_grads[0].astype(jnp.float32) * row_mask
    third_grad, third_gain_grad, third_shift_grad = jax.vjp(
        layer_norm, third_sum, gain_rows[2], shift_rows[2]
    )[1](out_grad)
    down_grad_in = third_grad.astype(jnp.bfloat16)
    grad_down = contract_rows(hidden_low, down_grad_in)
    grad_down_bias = column_sum(down_grad_in)
    hidden_grad = contract_cols(down_grad_in, down_back)
    hidden_pre_grad = jax.vjp(gelu_exact, hidden_pre)[1](hidden_grad)[0].astype(jnp.bfloat16)
    grad_up = contract_rows(second_low, hidden_pre_grad)
    grad_up_bias = column_sum(hidden_pre_grad)
    second_norm_grad = third_grad + contract_cols(hidden_pre_grad, up_back)
    second_grad, second_gain_grad, second_shift_grad = jax.vjp(
        layer_norm, second_sum, gain_rows[1], shift_rows[1]
    )[1](second_norm_grad)
    cross_out_grad = second_grad.astype(jnp.bfloat16)
    grad_cross_out = contract_rows(cross_context, cross_out_grad)
    grad_cross_out_bias = column_sum(cross_out_grad)
    cross_context_grad = contract_cols(cross_out_grad, out_back[1]).astype(jnp.bfloat16)
    cross_query_grad, cross_key_grad, cross_value_grad = attention_backward(
        cross_queries, cross_keys, cross_values, cross_totals, cross_context_grad, False
    )
    cross_query_low = cross_query_grad.astype(jnp.bfloat16)
    cross_key_low = cross_key_grad.astype(jnp.bfloat16)
    cross_value_low = cross_value_grad.astype(jnp.bfloat16)
    grad_cross_query = contract_rows(first_low, cross_query_low)
    grad_cross_query_bias = column_sum(cross_query_low)
    grad_cross_key = contract_rows(encoder, cross_key_low)
    grad_cross_value = contract_rows(encoder, cross_value_low)
    grad_cross_value_bias = column_sum(cross_value_low)
    encoder_grad = (
        contract_cols(cross_key_low, in_back[4]) + contract_cols(cross_value_low, in_back[5])
    ).astype(jnp.bfloat16)
    first_norm_grad = second_grad + contract_cols(cross_query_low, in_back[3])
    first_grad, first_gain_grad, first_shift_grad = jax.vjp(
        layer_norm, first_sum, gain_rows[0], shift_rows[0]
    )[1](first_norm_grad)
    self_out_grad = first_grad.astype(jnp.bfloat16)
    grad_self_out = contract_rows(context, self_out_grad)
    grad_self_out_bias = column_sum(self_out_grad)
    context_grad = contract_cols(self_out_grad, out_back[0]).astype(jnp.bfloat16)
    query_grad, key_grad, value_grad = attention_backward(
        queries, keys, values, log_totals, context_grad, True
    )
    query_low = query_grad.astype(jnp.bfloat16)
    key_low = key_grad.astype(jnp.bfloat16)
    value_low = value_grad.astype(jnp.bfloat16)
    grad_query = contract_rows(inputs, query_low)
    grad_query_bias = column_sum(query_low)
    grad_key = contract_rows(inputs, key_low)
    grad_value = contract_rows(inputs, value_low)
    grad_value_bias = column_sum(value_low)
    input_grad = (
        first_grad
        + contract_cols(query_low, in_back[0])
        + contract_cols(key_low, in_back[1])
        + contract_cols(value_low, in_back[2])
    ).astype(jnp.bfloat16)
    grad_blocks = lax.all_to_all(input_grad[None], "shard", split_axis=1, concat_axis=0, tiled=True)
    grad_tokens = pick_blocks(grad_blocks, owner_row)
    grad_in_full = jnp.stack(
        [grad_query, grad_key, grad_value, grad_cross_query, grad_cross_key, grad_cross_value]
    )
    grad_out_full = jnp.stack([grad_self_out, grad_cross_out])
    grad_bias_full = jnp.stack(
        [
            grad_query_bias,
            grad_value_bias,
            grad_self_out_bias,
            grad_cross_query_bias,
            grad_cross_value_bias,
            grad_cross_out_bias,
        ]
    )
    grad_gain_full = jnp.stack([first_gain_grad, second_gain_grad, third_gain_grad])
    grad_shift_full = jnp.stack([first_shift_grad, second_shift_grad, third_shift_grad])
    summed = sum_plain(
        grad_in_full, grad_out_full, grad_bias_full, grad_gain_full, grad_shift_full,
        grad_up, grad_up_bias, grad_down, grad_down_bias,
    )
    return (
        output,
        grad_tokens,
        encoder_grad[None],
        summed[0],
        summed[1],
        summed[2],
        summed[3],
        summed[4],
        summed[5],
        summed[6],
        summed[7],
        summed[8],
    )


def solution(mesh):
    placed = (
        P("rep", "shard", None),
        P(("rep", "shard"), None, None),
        P("rep", "shard", None),
        P("rep", None),
        P("rep", None),
        P(None, "shard", None),
        P(None, "shard", None),
        P(None, "shard"),
        P(None, "shard"),
        P(None, "shard"),
        P("shard", None),
        P("shard"),
        P("shard", None),
        P("shard"),
    )
    return jax.shard_map(
        local,
        mesh=mesh,
        in_specs=placed,
        out_specs=(
            P("rep", "shard", None),
            P("rep", "shard", None),
            P(("rep", "shard"), None, None),
            P(None, "shard", None),
            P(None, "shard", None),
            P(None, "shard"),
            P(None, "shard"),
            P(None, "shard"),
            P("shard", None),
            P("shard"),
            P("shard", None),
            P("shard"),
        ),
        check_vma=False,
    )
```

```python
import types

import jax
import jax.numpy as jnp
from jax import lax
from jax.experimental import pallas as pl
from jax.experimental.pallas import tpu as pltpu
from jax.sharding import PartitionSpec as P

HEADS = 16
HEAD_DIM = 64


epsilon = 1e-05


def matmul(left, right):
    return jnp.dot(left, right, preferred_element_type=jnp.float32)


def contract_rows(left, right):
    return lax.dot_general(
        left, right, (((0,), (0,)), ((), ())), preferred_element_type=jnp.float32
    )


def contract_cols(left, right):
    return lax.dot_general(
        left, right, (((1,), (1,)), ((), ())), preferred_element_type=jnp.float32
    )


def layer_norm(features, norm_scale, norm_shift):
    center = features - jnp.mean(features, axis=-1, keepdims=True)
    spread = jnp.mean(center * center, axis=-1, keepdims=True)
    return center * lax.rsqrt(spread + epsilon) * norm_scale + norm_shift


def gelu_exact(features):
    return jax.nn.gelu(features, approximate=False)


def column_sum(matrix):
    return jnp.sum(matrix.astype(jnp.float32), axis=0)


def split_heads(matrix):
    width = min(4, HEADS)
    return jnp.moveaxis(matrix.reshape(matrix.shape[0], HEADS // width, width, HEAD_DIM), 1, 0)


def merge_heads(stacked):
    return jnp.moveaxis(stacked, 0, 1).reshape(stacked.shape[1], HEADS * HEAD_DIM)


def block_scores(query_block, key_group, offset, causal):
    scores = jnp.einsum(
        "qgd,kgd->gqk", query_block, key_group, preferred_element_type=jnp.float32
    ) * HEAD_DIM ** (-0.5)
    if causal:
        query_pos = offset + jnp.arange(query_block.shape[0], dtype=jnp.int32)
        key_pos = jnp.arange(key_group.shape[0], dtype=jnp.int32)
        scores = jnp.where(key_pos[None, None, :] <= query_pos[None, :, None], scores, -jnp.inf)
    return scores


def attention_forward(queries, keys, values, causal):
    row_count = queries.shape[0]
    block_rows = min(512, row_count)
    block_count = row_count // block_rows
    offsets = jnp.arange(block_count, dtype=jnp.int32) * block_rows

    def per_group(operands):
        query_group, key_group, value_group = operands
        width = query_group.shape[1]
        query_blocks = query_group.reshape(block_count, block_rows, width, HEAD_DIM)

        def per_block(block_items):
            query_block, offset = block_items
            scores = block_scores(query_block, key_group, offset, causal)
            peak = jnp.max(scores, axis=-1, keepdims=True)
            log_total = peak + jnp.log(jnp.sum(jnp.exp(scores - peak), axis=-1, keepdims=True))
            weights_low = jnp.exp(scores - log_total).astype(jnp.bfloat16)
            context = jnp.einsum(
                "gqk,kgd->qgd", weights_low, value_group, preferred_element_type=jnp.float32
            )
            return (context.astype(jnp.bfloat16), log_total)

        context, log_totals = lax.map(per_block, (query_blocks, offsets))
        return (context.reshape(row_count, width, HEAD_DIM), log_totals)

    context, log_totals = lax.map(
        per_group, (split_heads(queries), split_heads(keys), split_heads(values))
    )
    return (merge_heads(context), log_totals)


def attention_backward(queries, keys, values, log_totals, context_grad, causal):
    row_count = queries.shape[0]
    block_rows = min(512, row_count)
    block_count = row_count // block_rows
    offsets = jnp.arange(block_count, dtype=jnp.int32) * block_rows
    scale = HEAD_DIM ** (-0.5)

    def per_group(operands):
        query_group, key_group, value_group, grad_group, total_group = operands
        width = query_group.shape[1]
        query_blocks = query_group.reshape(block_count, block_rows, width, HEAD_DIM)
        grad_blocks = grad_group.reshape(block_count, block_rows, width, HEAD_DIM)

        def per_block(accumulated, block_items):
            key_grad, value_grad = accumulated
            query_block, grad_block, log_total, offset = block_items
            scores = block_scores(query_block, key_group, offset, causal)
            weights_full = jnp.exp(scores - log_total)
            weights_low = weights_full.astype(jnp.bfloat16)
            value_grad = value_grad + jnp.einsum(
                "gqk,qgd->kgd", weights_low, grad_block, preferred_element_type=jnp.float32
            )
            weight_grad = jnp.einsum(
                "qgd,kgd->gqk", grad_block, value_group, preferred_element_type=jnp.float32
            )
            row_dot = jnp.sum(weights_full * weight_grad, axis=-1, keepdims=True)
            score_grad = (weights_full * (weight_grad - row_dot)).astype(jnp.bfloat16)
            query_grad = (
                jnp.einsum(
                    "gqk,kgd->qgd", score_grad, key_group, preferred_element_type=jnp.float32
                )
                * scale
            )
            key_grad = (
                key_grad
                + jnp.einsum(
                    "gqk,qgd->kgd", score_grad, query_block, preferred_element_type=jnp.float32
                )
                * scale
            )
            return ((key_grad, value_grad), query_grad)

        empty_grad = jnp.zeros(key_group.shape, jnp.float32)
        (key_grad, value_grad), query_grad = lax.scan(
            per_block, (empty_grad, empty_grad), (query_blocks, grad_blocks, total_group, offsets)
        )
        return (query_grad.reshape(row_count, width, HEAD_DIM), key_grad, value_grad)

    query_grad, key_grad, value_grad = lax.map(
        per_group,
        (
            split_heads(queries),
            split_heads(keys),
            split_heads(values),
            split_heads(context_grad),
            log_totals,
        ),
    )
    return (merge_heads(query_grad), merge_heads(key_grad), merge_heads(value_grad))


def pick_blocks(blocks, order):
    count = blocks.shape[0]
    return jnp.concatenate(
        [lax.dynamic_slice_in_dim(blocks, order[i], 1, axis=0) for i in range(count)], axis=0
    )


MESH = pl.DeviceIdType.MESH
ROWS = 128
CHUNKS = 32


def place():
    rep, shard = lax.axis_index("rep"), lax.axis_index("shard")
    return rep // 2, lax.rem(rep, 2), shard // 2, lax.rem(shard, 2)


def device(z, y, x, c):
    return (z * 2 + y, x * 2 + c)


def greet(peers):
    barrier = pltpu.get_barrier_semaphore()
    for peer in peers:
        pl.semaphore_signal(barrier, inc=1, device_id=peer, device_id_type=MESH)
    pl.semaphore_wait(barrier, len(peers))


def rows_at(base, size, align):
    return pl.ds(pl.multiple_of(base, align), size)


F32, BF16 = jnp.float32, jnp.bfloat16
RING = 8
LAGS = (0, 1, 3, 4, 5, 6, 7)


def dot_over(left, right, a, b):
    return lax.dot_general(left, right, (((a,), (b,)), ((), ())), preferred_element_type=F32)


def dot_nn(left, right):
    return dot_over(left, right, 1, 0)


def dot_nt(left, right):
    return dot_over(left, right, 1, 1)


def dot_tn(left, right):
    return dot_over(left, right, 0, 0)


def remote(src, dst, send, recv, peer):
    return pltpu.make_async_remote_copy(
        src_ref=src, dst_ref=dst, send_sem=send, recv_sem=recv, device_id=peer, device_id_type=MESH
    )


def loop(count, body):
    def step(i, carry):
        body(i)
        return carry

    lax.fori_loop(0, count, step, 0)


ERF_TOP = (
    -2.72614225801306e-10, 2.77068142495902e-08, -2.10102402082508e-06, -5.69250639462346e-05,
    -7.34990630326855e-04, -2.95459980854025e-03, -1.60960333262415e-02,
)
ERF_BOTTOM = (
    -1.45660718464996e-05, -2.13374055278905e-04, -1.68282697438203e-03, -7.37332916720468e-03,
    -1.42647390514189e-02,
)


def normal_cdf(value):
    arg = jnp.clip(value * 0.7071067811865476, -3.832506856900711, 3.832506856900711)
    square = arg * arg
    top, bottom = jnp.full_like(arg, ERF_TOP[0]), jnp.full_like(arg, ERF_BOTTOM[0])
    for factor in ERF_TOP[1:]:
        top = top * square + factor
    for factor in ERF_BOTTOM[1:]:
        bottom = bottom * square + factor
    return 0.5 + 0.5 * (arg * top / bottom)


BACK_SCRATCH = dict(
    mine=pltpu.VMEM((4, 2, ROWS, 1024), BF16),
    r0=pltpu.VMEM((RING, 2, ROWS, 1024), BF16),
    r1=pltpu.VMEM((RING, ROWS, 1024), BF16),
    r2=pltpu.VMEM((RING, ROWS // 2, 1024), BF16),
    r3=pltpu.VMEM((RING, 3, ROWS // 8, 1024), BF16),
    held=pltpu.VMEM((RING, ROWS // 8, 1024), BF16),
    small=pltpu.VMEM((4, 24, 256), F32),
    s0=pltpu.VMEM((2, 24, 256), F32),
    s1=pltpu.VMEM((24, 256), F32),
    s2=pltpu.VMEM((24, 256), F32),
    s3=pltpu.VMEM((3, 24, 256), F32),
    own_sem=pltpu.SemaphoreType.DMA((4, 2)),
    c_send=pltpu.SemaphoreType.DMA((CHUNKS, 2)),
    c_recv=pltpu.SemaphoreType.DMA((CHUNKS, 2)),
    x_send=pltpu.SemaphoreType.DMA((CHUNKS,)),
    x_recv=pltpu.SemaphoreType.DMA((CHUNKS,)),
    y_send=pltpu.SemaphoreType.DMA((CHUNKS,)),
    y_recv=pltpu.SemaphoreType.DMA((CHUNKS,)),
    z_send=pltpu.SemaphoreType.DMA((CHUNKS, 3)),
    z_recv=pltpu.SemaphoreType.DMA((CHUNKS, 3)),
    a_send=pltpu.SemaphoreType.DMA((CHUNKS, 3)),
    a_recv=pltpu.SemaphoreType.DMA((CHUNKS, 3)),
    a_own=pltpu.SemaphoreType.DMA((CHUNKS,)),
    b_send=pltpu.SemaphoreType.DMA((CHUNKS,)),
    b_recv=pltpu.SemaphoreType.DMA((CHUNKS,)),
    t_send=pltpu.SemaphoreType.DMA((7,)),
    t_recv=pltpu.SemaphoreType.DMA((7,)),
    o_send=pltpu.SemaphoreType.DMA((2, 3)),
    o_recv=pltpu.SemaphoreType.DMA((2, 3)),
    o_own=pltpu.SemaphoreType.DMA((2,)),
    load_sem=pltpu.SemaphoreType.DMA((16,)),
    tile_sem=pltpu.SemaphoreType.DMA((2, 16)),
    weight_sem=pltpu.SemaphoreType.DMA((2,)),
    grad_sem=pltpu.SemaphoreType.DMA((2,)),
    x1=pltpu.VMEM((512, 1024), BF16),
    q1=pltpu.VMEM((512, 1024), BF16),
    k1=pltpu.VMEM((512, 1024), BF16),
    v1=pltpu.VMEM((512, 1024), BF16),
    o1=pltpu.VMEM((512, 1024), BF16),
    h1=pltpu.VMEM((512, 1024), BF16),
    q2=pltpu.VMEM((512, 1024), BF16),
    k2=pltpu.VMEM((256, 1024), BF16),
    v2=pltpu.VMEM((256, 1024), BF16),
    o2=pltpu.VMEM((512, 1024), BF16),
    h2=pltpu.VMEM((512, 1024), BF16),
    e1=pltpu.VMEM((256, 1024), BF16),
    cot=pltpu.VMEM((512, 1024), BF16),
    sum1=pltpu.VMEM((512, 1024), F32),
    sum2=pltpu.VMEM((512, 1024), F32),
    sum3=pltpu.VMEM((512, 1024), F32),
    dz=pltpu.VMEM((512, 1024), F32),
    low=pltpu.VMEM((512, 1024), BF16),
    dob=pltpu.VMEM((512, 1024), BF16),
    dqb=pltpu.VMEM((512, 1024), BF16),
    dkb=pltpu.VMEM((512, 1024), BF16),
    dvb=pltpu.VMEM((512, 1024), BF16),
    dka=pltpu.VMEM((512, 128), F32),
    dva=pltpu.VMEM((512, 128), F32),
    ut=pltpu.VMEM((2, 512, 512), F32),
    wd=pltpu.VMEM((2, 512, 1024), BF16),
    wu=pltpu.VMEM((2, 1024, 512), BF16),
    wb=pltpu.VMEM((2, 1024, 1024), BF16),
    gt=pltpu.VMEM((2, 512, 512), BF16),
    dut=pltpu.VMEM((512, 512), BF16),
    stage=pltpu.VMEM((2, 4, ROWS, 1024), BF16),
    sums=pltpu.VMEM((8, 1024), F32),
    ub=pltpu.VMEM((8, 1, 512), F32),
)
BACK_LOADS = (
    "x1", "q1", "k1", "v1", "o1", "h1", "q2", "k2", "v2", "o2", "h2", "e1", "cot", "sum1", "sum2", "sum3",
)


class Reducer:
    def __init__(self, s, parts, total, small_total):
        self.s, self.parts, self.total, self.small_total = s, parts, total, small_total
        z, y, x, c = self.at = place()
        self.core = device(z, y, x, 1 - c)
        self.xmate = device(z, y, 1 - x, c)
        self.diag = device(z, y, 1 - x, 1 - c)
        self.ymate = device(z, 1 - y, x, c)
        self.others = [device(lax.rem(z + i, 4), y, x, c) for i in (1, 2, 3)]

    def greet(self):
        greet([self.core, self.xmate, self.diag, self.ymate] + self.others)

    def core_copy(self, k, side):
        s, (_, _, _, c) = self.s, self.at
        return remote(
            self.parts.at[k, side * 2 + 1 - c], s.r0.at[lax.rem(k, RING), side],
            s.c_send.at[k, side], s.c_recv.at[k, side], self.core,
        )

    def own_copy(self, k, side):
        s, (_, _, _, c) = self.s, self.at
        slot = lax.rem(k, 4)
        return pltpu.make_async_copy(
            self.parts.at[k, side * 2 + c], s.mine.at[slot, side], s.own_sem.at[slot, side]
        )

    def fetch(self, k):
        for side in (0, 1):
            self.core_copy(k, side).start()
            self.own_copy(k, side).start()

    def x_copy(self, k):
        s, (_, _, x, _) = self.s, self.at
        slot = lax.rem(k, RING)
        return remote(s.r0.at[slot, 1 - x], s.r1.at[slot], s.x_send.at[k], s.x_recv.at[k], self.xmate)

    def core_sum(self, k):
        s, slot, near = self.s, lax.rem(k, RING), lax.rem(k, 4)
        for side in (0, 1):
            self.core_copy(k, side).wait()
            self.own_copy(k, side).wait()

        def add(i):
            piece = rows_at(i * 32, 32, 32)
            for side in (0, 1):
                s.r0[slot, side, piece, :] = s.r0[slot, side, piece, :] + s.mine[near, side, piece, :]

        loop(ROWS // 32, add)
        self.x_copy(k).start()

    def y_copy(self, k):
        s, (_, y, _, _) = self.s, self.at
        slot, half = lax.rem(k, RING), ROWS // 2
        return remote(
            s.r1.at[slot, rows_at((1 - y) * half, half, half), :], s.r2.at[slot],
            s.y_send.at[k], s.y_recv.at[k], self.ymate,
        )

    def x_sum(self, k):
        s, (_, _, x, _) = self.s, self.at
        slot = lax.rem(k, RING)
        self.x_copy(k).wait()

        def add(i):
            piece = rows_at(i * 32, 32, 32)
            s.r1[slot, piece, :] = s.r0[slot, x, piece, :] + s.r1[slot, piece, :]

        loop(ROWS // 32, add)
        self.y_copy(k).start()

    def z_copies(self, k):
        s, (z, _, _, _) = self.s, self.at
        slot, quarter = lax.rem(k, RING), ROWS // 8
        return [
            remote(
                s.r2.at[slot, rows_at(lax.rem(z + i + 1, 4) * quarter, quarter, quarter), :], s.r3.at[slot, i],
                s.z_send.at[k, i], s.z_recv.at[k, i], self.others[i],
            )
            for i in (0, 1, 2)
        ]

    def y_sum(self, k):
        s, (_, y, _, _) = self.s, self.at
        slot, half = lax.rem(k, RING), ROWS // 2
        self.y_copy(k).wait()

        def add(i):
            piece = rows_at(i * 32, 32, 32)
            s.r2[slot, piece, :] = s.r1[slot, rows_at(y * half + i * 32, 32, 32), :] + s.r2[slot, piece, :]

        loop(half // 32, add)
        for copy in self.z_copies(k):
            copy.start()

    def out_piece(self, k):
        z, y, _, _ = self.at
        return self.total.at[k, rows_at(y * (ROWS // 2) + z * (ROWS // 8), ROWS // 8, ROWS // 8), :]

    def spread_copies(self, k):
        s, slot = self.s, lax.rem(k, RING)
        return [
            remote(s.held.at[slot], self.out_piece(k), s.a_send.at[k, i], s.a_recv.at[k, i], self.others[i])
            for i in (0, 1, 2)
        ]

    def held_copy(self, k):
        return pltpu.make_async_copy(self.s.held.at[lax.rem(k, RING)], self.out_piece(k), self.s.a_own.at[k])

    def z_sum(self, k):
        s, (z, _, _, _) = self.s, self.at
        slot, quarter = lax.rem(k, RING), ROWS // 8
        for copy in self.z_copies(k):
            copy.wait()
        added = s.r2[slot, rows_at(z * quarter, quarter, quarter), :].astype(F32)
        for i in (0, 1, 2):
            added = added + s.r3[slot, i].astype(F32)
        s.held[slot] = added.astype(BF16)
        for copy in self.spread_copies(k):
            copy.start()
        self.held_copy(k).start()

    def half_copy(self, k):
        s, (_, y, _, _) = self.s, self.at
        half = ROWS // 2
        part = self.total.at[k, rows_at(y * half, half, half), :]
        return remote(part, part, s.b_send.at[k], s.b_recv.at[k], self.ymate)

    def spread_y(self, k):
        for copy in self.spread_copies(k):
            copy.wait()
        self.held_copy(k).wait()
        self.half_copy(k).start()

    def finish(self, k):
        self.half_copy(k).wait()

    def tick(self, t):
        stages = (self.fetch, self.core_sum, self.x_sum, self.y_sum, self.z_sum, self.spread_y, self.finish)
        for lag, act in zip(LAGS, stages):
            k = t - lag

            @pl.when((k >= 0) & (k < CHUNKS))
            def _(k=k, act=act):
                act(k)

    def small_steps(self, t):
        s, (_, _, x, c) = self.s, self.at
        send, recv = s.t_send, s.t_recv
        firsts = [
            remote(s.small.at[side * 2 + 1 - c], s.s0.at[side], send.at[side], recv.at[side], self.core)
            for side in (0, 1)
        ]
        across = remote(s.s0.at[1 - x], s.s1, send.at[2], recv.at[2], self.xmate)
        along = remote(s.s1, s.s2, send.at[3], recv.at[3], self.ymate)
        lasts = [
            remote(s.s2, s.s3.at[i], send.at[4 + i], recv.at[4 + i], self.others[i]) for i in (0, 1, 2)
        ]

        @pl.when(t == 0)
        def _():
            for copy in firsts:
                copy.start()

        @pl.when(t == 2)
        def _():
            for side in (0, 1):
                firsts[side].wait()
                s.s0[side] = s.s0[side] + s.small[side * 2 + c]
            across.start()

        @pl.when(t == 4)
        def _():
            across.wait()
            s.s1[...] = s.s1[...] + s.s0[x]
            along.start()

        @pl.when(t == 6)
        def _():
            along.wait()
            s.s2[...] = s.s2[...] + s.s1[...]
            for copy in lasts:
                copy.start()

        @pl.when(t == 8)
        def _():
            for copy in lasts:
                copy.wait()
            self.small_total[...] = s.s2[...] + s.s3[0] + s.s3[1] + s.s3[2]


def back_kernel(*refs):
    loads = dict(zip(BACK_LOADS, refs[:16]))
    d_all, g_all, f_in, f_out, f_up, f_down, gains, out_rows, mask = refs[16:25]
    total, small_total, grad_enc, out_back, grad_back, parts = refs[25:31]
    s = types.SimpleNamespace(**dict(zip(BACK_SCRATCH, refs[31:])))
    reducer = Reducer(s, parts, total, small_total)
    z, y, x, c = reducer.at
    mine = x * 2 + c
    peers = ((reducer.core, x * 2 + 1 - c), (reducer.xmate, (1 - x) * 2 + c), (reducer.diag, (1 - x) * 2 + 1 - c))

    def row_copies(which, src, dst):
        return [
            remote(
                src.at[rows_at(slot * 128, 128, 128), :], dst.at[mine],
                s.o_send.at[which, i], s.o_recv.at[which, i], peer,
            )
            for i, (peer, slot) in enumerate(peers)
        ] + [pltpu.make_async_copy(src.at[rows_at(mine * 128, 128, 128), :], dst.at[mine], s.o_own.at[which])]

    def load(name):
        return pltpu.make_async_copy(loads[name], getattr(s, name), s.load_sem.at[BACK_LOADS.index(name)])

    for name in ("sum3", "cot", "h2"):
        load(name).start()

    def tile_copies(j, slot):
        copies = []
        for i in range(4):
            columns = rows_at(i * 1024 + j * 128, 128, 128)
            copies += [
                pltpu.make_async_copy(
                    d_all.at[:, columns], s.ut.at[slot, :, pl.ds(i * 128, 128)], s.tile_sem.at[slot, i]
                ),
                pltpu.make_async_copy(
                    g_all.at[:, columns], s.gt.at[slot, :, pl.ds(i * 128, 128)], s.tile_sem.at[slot, 12 + i]
                ),
                pltpu.make_async_copy(
                    f_down.at[columns, :], s.wd.at[slot, pl.ds(i * 128, 128), :], s.tile_sem.at[slot, 4 + i]
                ),
                pltpu.make_async_copy(
                    f_up.at[:, columns], s.wu.at[slot, :, pl.ds(i * 128, 128)], s.tile_sem.at[slot, 8 + i]
                ),
            ]
        return copies

    for copy in tile_copies(0, 0):
        copy.start()
    weights = (
        f_out.at[1], f_in.at[4], f_in.at[5], f_in.at[3], f_out.at[0], f_in.at[0], f_in.at[1], f_in.at[2],
    )

    def weight(i):
        return pltpu.make_async_copy(weights[i], s.wb.at[i % 2], s.weight_sem.at[i % 2])

    reducer.greet()
    for copy in row_copies(0, out_rows, out_back):
        copy.start()
    for name in ("sum2", "o2", "q2", "k2", "v2", "h1", "e1", "sum1", "o1", "q1", "k1", "v1", "x1"):
        load(name).start()
    weight(0).start()
    weight(1).start()
    s.small[...] = jnp.zeros_like(s.small)

    def put(row, value):
        for i in range(4):
            s.small[i, row:row + 1, :] = value[:, i * 256:(i + 1) * 256]

    def norm_back(sum_ref, index, first, bias_row):
        s.sums[...] = jnp.zeros_like(s.sums)
        gain = gains[6 + index:7 + index, :]

        def block(i):
            p = rows_at(i * 32, 32, 32)
            value = sum_ref[p, :]
            grad = s.cot[p, :].astype(F32) * mask[p, 0:1] if first else s.dz[p, :]
            center = value - jnp.mean(value, axis=1, keepdims=True)
            scale = lax.rsqrt(jnp.mean(center * center, axis=1, keepdims=True) + epsilon)
            normal = center * scale
            scaled = grad * gain
            back = scale * (
                scaled - jnp.mean(scaled, axis=1, keepdims=True)
                - normal * jnp.mean(scaled * normal, axis=1, keepdims=True)
            )
            rounded = back.astype(BF16)
            s.dz[p, :] = back
            s.low[p, :] = rounded
            s.sums[0:1, :] += jnp.sum(grad * normal, axis=0, keepdims=True)
            s.sums[1:2, :] += jnp.sum(grad, axis=0, keepdims=True)
            s.sums[2:3, :] += jnp.sum(rounded.astype(F32), axis=0, keepdims=True)

        loop(16, block)
        put(6 + index, s.sums[0:1, :])
        put(9 + index, s.sums[1:2, :])
        put(bias_row, s.sums[2:3, :])

    def column_sums(ref, count, row):
        s.sums[...] = jnp.zeros_like(s.sums)

        def block(i):
            p = rows_at(i * 64, 64, 64)
            s.sums[0:1, :] += jnp.sum(ref[p, :].astype(F32), axis=0, keepdims=True)

        loop(count // 64, block)
        put(row, s.sums[0:1, :])

    pending = []

    def flush():
        if pending:
            pending.pop().wait()

    def store_grad(chunk, left, right):
        count = left.shape[0]
        flush()

        def block(i):
            product = dot_tn(left[:, rows_at(i * 256, 256, 256)], right[0:count, :]).astype(BF16)
            s.stage[0, i] = product[:128]
            s.stage[1, i] = product[128:]

        loop(4, block)
        pending.append(pltpu.make_async_copy(s.stage, parts.at[pl.ds(chunk, 2)], s.grad_sem.at[0]))
        pending[-1].start()

    load("sum3").wait()
    load("cot").wait()
    norm_back(s.sum3, 2, True, 16)
    load("h2").wait()

    def down_save(j):
        return pltpu.make_async_copy(s.stage.at[0], parts.at[2 * j], s.grad_sem.at[0])

    def up_save(j):
        return pltpu.make_async_copy(s.stage.at[1], parts.at[2 * j + 1], s.grad_sem.at[1])

    def tile(j):
        slot = lax.rem(j, 2)
        for copy in tile_copies(j, slot):
            copy.wait()

        @pl.when(j < 7)
        def _():
            for copy in tile_copies(j + 1, 1 - slot):
                copy.start()

        def hidden(i):
            p = rows_at(i * 256, 256, 256)
            grad = dot_nt(s.low[...], s.wd[slot, p, :])
            rounded = (grad * s.ut[slot, :, p]).astype(BF16)
            s.dut[:, p] = rounded
            s.ub[j, :, p] = jnp.sum(rounded.astype(F32), axis=0, keepdims=True)

        loop(2, hidden)

        def down(i):
            product = dot_tn(s.gt[slot, :, rows_at(i * 256, 256, 256)], s.low[...]).astype(BF16)
            s.stage[0, 2 * i] = product[:128]
            s.stage[0, 2 * i + 1] = product[128:]

        loop(2, down)
        down_save(j).start()

        def up(i):
            product = dot_tn(s.h2[:, rows_at(i * 256, 256, 256)], s.dut[...]).astype(BF16)
            s.stage[1, i, :, 0:512] = product[:128]
            s.stage[1, i, :, 512:1024] = product[128:]

        loop(4, up)
        up_save(j).start()

        def back(i):
            p = rows_at(i * 256, 256, 256)
            s.dz[:, p] += dot_nt(s.dut[...], s.wu[slot, p, :])

        loop(4, back)
        down_save(j).wait()
        up_save(j).wait()
        loop(2 - lax.rem(j, 2), lambda i: reducer.tick((3 * j + 1) // 2 + i))

    loop(8, tile)
    for j in range(8):
        for i in range(4):
            s.small[i, 12 + j // 2:13 + j // 2, (j % 2) * 128:(j % 2) * 128 + 128] = s.ub[j, :, i * 128:(i + 1) * 128]
    load("sum2").wait()
    norm_back(s.sum2, 1, False, 5)
    reducer.tick(12)
    load("o2").wait()
    store_grad(16, s.o2, s.low)

    def times_weight(dst, left, count, slot):
        def block(i):
            p = rows_at(i * 256, 256, 256)
            dst[:, p] = dot_nt(left[...], s.wb[slot, p, :]).astype(BF16)

        loop(count, block)

    def add_weight(left, slot):
        def block(i):
            p = rows_at(i * 256, 256, 256)
            s.dz[:, p] += dot_nt(left[...], s.wb[slot, p, :])

        loop(4, block)

    weight(0).wait()
    times_weight(s.dob, s.low, 4, 0)
    weight(2).start()
    flush()
    reducer.tick(13)
    for name in ("q2", "k2", "v2"):
        load(name).wait()

    lane = lax.broadcasted_iota(jnp.int32, (1, 128), 1)
    head_masks = [(lane < 64).astype(F32).astype(BF16), (lane >= 64).astype(F32).astype(BF16)]

    def attention_pair(i, q_ref, k_ref, v_ref, key_count, causal):
        lanes = rows_at(i * 128, 128, 128)
        s.dka[...] = jnp.zeros_like(s.dka)
        s.dva[...] = jnp.zeros_like(s.dva)
        for block in (0, 1):
            rows = pl.ds(block * 256, 256)
            reach = (block + 1) * 256 if causal else key_count
            query, grad = q_ref[rows, lanes], s.dob[rows, lanes]
            key, value = k_ref[0:reach, lanes], v_ref[0:reach, lanes]
            query_grad = jnp.zeros((256, 128), F32)
            for mask in head_masks:
                query_one, grad_one = query * mask, grad * mask
                scores = dot_nt(key, query_one) * 0.125
                if causal:
                    key_at = lax.broadcasted_iota(jnp.int32, (reach, 256), 0)
                    query_at = lax.broadcasted_iota(jnp.int32, (reach, 256), 1) + block * 256
                    scores = jnp.where(key_at <= query_at, scores, -1e30)
                peak = jnp.max(scores, axis=0, keepdims=True)
                full = jnp.exp(scores - peak)
                full = full * (1.0 / jnp.sum(full, axis=0, keepdims=True))
                full_grad = dot_nt(value, grad_one)
                row_dot = jnp.sum(full * full_grad, axis=0, keepdims=True)
                score_grad = (full * (full_grad - row_dot)).astype(BF16)
                s.dva[0:reach, :] += dot_nn(full.astype(BF16), grad_one)
                s.dka[0:reach, :] += dot_nn(score_grad, query_one)
                query_grad = query_grad + dot_tn(score_grad, key * mask)
            s.dqb[rows, lanes] = (query_grad * 0.125).astype(BF16)
        s.dkb[0:key_count, lanes] = (s.dka[0:key_count, :] * 0.125).astype(BF16)
        s.dvb[0:key_count, lanes] = s.dva[0:key_count, :].astype(BF16)

    def cross(i):
        attention_pair(i, s.q2, s.k2, s.v2, 256, False)

        @pl.when((lax.rem(i, 2) == 1) & (i < 7))
        def _():
            reducer.tick(14 + i // 2)

    loop(8, cross)
    load("h1").wait()
    load("e1").wait()
    store_grad(18, s.h1, s.dqb)
    reducer.tick(17)
    store_grad(20, s.e1, s.dkb)
    reducer.tick(18)
    store_grad(22, s.e1, s.dvb)
    reducer.tick(19)
    column_sums(s.dqb, 512, 3)
    column_sums(s.dvb, 256, 4)
    weight(1).wait()
    weight(2).wait()

    def enc_block(i):
        p = rows_at(i * 256, 256, 256)
        grad_enc[:, p] = (
            dot_nt(s.dkb[0:256, :], s.wb[1, p, :]) + dot_nt(s.dvb[0:256, :], s.wb[0, p, :])
        ).astype(BF16)

    loop(4, enc_block)
    flush()
    reducer.tick(20)
    weight(3).start()
    weight(4).start()
    weight(3).wait()
    add_weight(s.dqb, 1)
    weight(5).start()
    reducer.tick(21)
    load("sum1").wait()
    norm_back(s.sum1, 0, False, 2)
    load("o1").wait()
    store_grad(24, s.o1, s.low)
    reducer.tick(22)
    weight(4).wait()
    times_weight(s.dob, s.low, 4, 0)
    weight(6).start()
    flush()
    reducer.tick(23)
    for name in ("q1", "k1", "v1"):
        load(name).wait()

    def own(i):
        attention_pair(i, s.q1, s.k1, s.v1, 512, True)

        @pl.when(lax.rem(i, 3) == 2)
        def _():
            reducer.tick(24 + i // 3)

    loop(8, own)
    load("x1").wait()
    store_grad(26, s.x1, s.dqb)
    store_grad(28, s.x1, s.dkb)
    reducer.tick(26)
    store_grad(30, s.x1, s.dvb)
    reducer.tick(27)
    column_sums(s.dqb, 512, 0)
    column_sums(s.dvb, 512, 1)
    flush()
    reducer.tick(28)
    weight(5).wait()
    add_weight(s.dqb, 1)
    weight(7).start()
    reducer.tick(29)
    weight(6).wait()
    add_weight(s.dkb, 0)
    reducer.tick(30)
    weight(7).wait()

    def last(i):
        p = rows_at(i * 256, 256, 256)
        s.low[:, p] = (s.dz[:, p] + dot_nt(s.dvb[...], s.wb[1, p, :])).astype(BF16)

    loop(4, last)
    def drain(i):
        reducer.tick(31 + i)

        @pl.when(i == LAGS[1])
        def _():
            for copy in row_copies(1, s.low, grad_back):
                copy.start()

        reducer.small_steps(i)

    loop(max(9, CHUNKS + LAGS[-1] - 31), drain)
    for copy in row_copies(0, out_rows, out_back) + row_copies(1, s.low, grad_back):
        copy.wait()


def backward(loads, *rest):
    any_space = pl.BlockSpec(memory_space=pl.ANY)
    in_vmem = pl.BlockSpec(memory_space=pltpu.VMEM)
    return pl.pallas_call(
        back_kernel,
        out_shape=(
            jax.ShapeDtypeStruct((CHUNKS, ROWS, 1024), BF16),
            jax.ShapeDtypeStruct((24, 256), F32),
            jax.ShapeDtypeStruct((256, 1024), BF16),
            jax.ShapeDtypeStruct((4, 128, 1024), BF16),
            jax.ShapeDtypeStruct((4, 128, 1024), BF16),
            jax.ShapeDtypeStruct((CHUNKS, 4, ROWS, 1024), BF16),
        ),
        in_specs=[any_space] * 22 + [in_vmem] * 3,
        out_specs=(any_space, in_vmem, in_vmem, any_space, any_space, any_space),
        scratch_shapes=list(BACK_SCRATCH.values()),
        compiler_params=pltpu.CompilerParams(
            collective_id=1, has_side_effects=True, vmem_limit_bytes=62 << 20
        ),
    )(*[loads[name] for name in BACK_LOADS], *rest)


FORWARD_SCRATCH = dict(
    v_in=pltpu.VMEM((6, 1024, 1024), BF16),
    v_out=pltpu.VMEM((2, 1024, 1024), BF16),
    v_up=pltpu.VMEM((1024, 4096), BF16),
    v_down=pltpu.VMEM((4096, 1024), BF16),
    small=pltpu.VMEM((24, 256), F32),
    s_tok=pltpu.VMEM((4, 128, 1024), BF16),
    v_small=pltpu.VMEM((4, 24, 256), F32),
    vec=pltpu.VMEM((24, 1024), F32),
    x=pltpu.VMEM((512, 1024), BF16),
    e=pltpu.VMEM((256, 1024), BF16),
    q=pltpu.VMEM((512, 1024), BF16),
    k=pltpu.VMEM((512, 1024), BF16),
    v=pltpu.VMEM((512, 1024), BF16),
    o=pltpu.VMEM((512, 1024), BF16),
    h1=pltpu.VMEM((512, 1024), BF16),
    q2=pltpu.VMEM((512, 1024), BF16),
    k2=pltpu.VMEM((256, 1024), BF16),
    v2=pltpu.VMEM((256, 1024), BF16),
    o2=pltpu.VMEM((512, 1024), BF16),
    h2=pltpu.VMEM((512, 1024), BF16),
    y=pltpu.VMEM((512, 1024), BF16),
    hf=pltpu.VMEM((512, 1024), F32),
    sum_a=pltpu.VMEM((512, 1024), F32),
    sum_b=pltpu.VMEM((512, 1024), F32),
    ublock=pltpu.VMEM((512, 256), F32),
    gblock=pltpu.VMEM((2, 512, 256), BF16),
    dblock=pltpu.VMEM((2, 512, 256), F32),
    own_sem=pltpu.SemaphoreType.DMA((16,)),
    x_send=pltpu.SemaphoreType.DMA((16,)),
    x_recv=pltpu.SemaphoreType.DMA((16,)),
    y_send=pltpu.SemaphoreType.DMA((16, 2)),
    y_recv=pltpu.SemaphoreType.DMA((16, 2)),
    z_send=pltpu.SemaphoreType.DMA((16, 2)),
    z_recv=pltpu.SemaphoreType.DMA((16, 2)),
    c_send=pltpu.SemaphoreType.DMA((16, 2)),
    c_recv=pltpu.SemaphoreType.DMA((16, 2)),
    t_send=pltpu.SemaphoreType.DMA((3, 3)),
    t_recv=pltpu.SemaphoreType.DMA((3, 3)),
    t_own=pltpu.SemaphoreType.DMA((4,)),
    save_sem=pltpu.SemaphoreType.DMA((16,)),
    weight_sem=pltpu.SemaphoreType.DMA((16,)),
    block_sem=pltpu.SemaphoreType.DMA((2, 2)),
)
SAVED = ("x", "q", "k", "v", "o", "h1", "q2", "k2", "v2", "o2", "h2", "sum1", "sum2", "sum3", "y")
GATHER_ORDER = (0, 1, 2, 6, 4, 5, 3, 7, 8, 9, 10, 11, 12, 13, 14, 15)


def weight_rows(refs, k, shard, start, size):
    if k < 6:
        return refs[0].at[k, rows_at(shard * 256 + start, size, 8), :]
    if k < 8:
        return refs[1].at[k - 6, rows_at(shard * 256 + start, size, 8), :]
    if k < 12:
        return refs[2].at[rows_at(shard * 256 + (k - 8) * 64 + start, size, 8), :]
    return refs[3].at[rows_at(shard * 1024 + (k - 12) * 256 + start, size, 8), :]


class Gatherer:
    def __init__(self, s, shards, full):
        self.s, self.shards, self.full, self.done = s, shards, full, -4
        z, y, x, c = self.at = place()
        self.side = lax.rem(z, 2)
        self.core = device(z, y, x, 1 - c)
        self.xmate = device(z, y, 1 - x, c)
        self.diag = device(z, y, 1 - x, 1 - c)
        self.ymate = device(z, 1 - y, x, c)
        self.zmate = device(z + 1 - 2 * self.side, y, x, c)
        self.mine, self.other = x * 2 + c, (1 - x) * 2 + c

    def greet(self):
        greet([self.core, self.xmate, self.diag, self.ymate, self.zmate])

    def size(self, k):
        return 64 if 8 <= k < 12 else 256

    def x_copy(self, k):
        n = self.size(k) // 4
        q = (self.at[1] * 2 + self.side) * n
        return remote(
            weight_rows(self.shards, k, 0, q, n), weight_rows(self.full, k, self.mine, q, n),
            self.s.x_send.at[k], self.s.x_recv.at[k], self.xmate,
        )

    def core_copy(self, k):
        return remote(
            weight_rows(self.shards, k, 0, 0, self.size(k)), weight_rows(self.full, k, self.mine, 0, self.size(k)),
            self.s.c_send.at[k, 0], self.s.c_recv.at[k, 0], self.core,
        )

    def own_copy(self, k):
        return pltpu.make_async_copy(
            weight_rows(self.shards, k, 0, 0, self.size(k)), weight_rows(self.full, k, self.mine, 0, self.size(k)),
            self.s.own_sem.at[k],
        )

    def relay(self, k, start, n, send, recv, peer):
        view = weight_rows(self.full, k, self.other, start, n)
        return remote(view, view, send, recv, peer)

    def first_hops(self, k):
        s, n = self.s, self.size(k) // 4
        q = (self.at[1] * 2 + self.side) * n
        return [
            self.relay(k, q, n, s.y_send.at[k, 0], s.y_recv.at[k, 0], self.ymate),
            self.relay(k, q, n, s.z_send.at[k, 0], s.z_recv.at[k, 0], self.zmate),
        ]

    def second_hops(self, k):
        s, n, y = self.s, self.size(k) // 4, self.at[1]
        return [
            self.relay(k, (y * 2 + 1 - self.side) * n, n // 2, s.y_send.at[k, 1], s.y_recv.at[k, 1], self.ymate),
            self.relay(
                k, ((1 - y) * 2 + self.side) * n + n // 2, n // 2, s.z_send.at[k, 1], s.z_recv.at[k, 1], self.zmate
            ),
        ]

    def last_hop(self, k):
        return self.relay(k, 0, self.size(k), self.s.c_send.at[k, 1], self.s.c_recv.at[k, 1], self.core)

    def step(self, t):
        def chunk(lag):
            return GATHER_ORDER[t - lag] if 0 <= t - lag < 16 else None

        if (k := chunk(-3)) is not None:
            self.x_copy(k).start()
            self.core_copy(k).start()
            self.own_copy(k).start()
        if (k := chunk(0)) is not None:
            self.x_copy(k).wait()
            for copy in self.first_hops(k):
                copy.start()
        if (k := chunk(1)) is not None:
            for copy in self.first_hops(k):
                copy.wait()
            for copy in self.second_hops(k):
                copy.start()
        if (k := chunk(2)) is not None:
            for copy in self.second_hops(k):
                copy.wait()
            self.last_hop(k).start()
        if (k := chunk(3)) is not None:
            self.last_hop(k).wait()
            self.core_copy(k).wait()
            self.own_copy(k).wait()

    def advance(self, t):
        while self.done < t:
            self.done += 1
            self.step(self.done)

    def ready(self, index):
        self.advance(index + 3)


def forward_kernel(*refs):
    owner, lengths, bias, gain_in, shift_in, up_bias, down_bias, tok_in, cot_in = refs[:9]
    w_in, w_out, w_up, w_down, enc = refs[9:14]
    f_in, f_out, f_up, f_down, f_cot, gains, mask, g_all, d_all = refs[14:23]
    saved = dict(zip(SAVED, refs[23:38]))
    s = types.SimpleNamespace(**dict(zip(FORWARD_SCRATCH, refs[38:])))
    sequence_at = [
        jnp.clip(sum(jnp.where(owner[0, j] == i, j, 0) for j in range(4)), 0, 3) for i in range(4)
    ]
    small, tok = s.small, s.s_tok
    full = (s.v_in, s.v_out, s.v_up, s.v_down)
    gather = Gatherer(s, (w_in, w_out, w_up, w_down), full)
    mine, (_, _, x, c) = gather.mine, gather.at
    peers = ((gather.core, x * 2 + 1 - c), (gather.xmate, gather.other), (gather.diag, (1 - x) * 2 + 1 - c))

    def rows_of(index):
        return rows_at(index * 128, 128, 128)

    def arrange(source, target):
        for i in range(4):
            def block(n, i=i):
                p = rows_at(n * 32, 32, 32)
                target[i, p, :] = source[sequence_at[i], p, :]

            loop(4, block)

    def token_copies():
        return [
            remote(tok.at[slot], s.x.at[rows_of(mine), :], s.t_send.at[0, i], s.t_recv.at[0, i], peer)
            for i, (peer, slot) in enumerate(peers)
        ] + [
            remote(small, s.v_small.at[mine], s.t_send.at[2, i], s.t_recv.at[2, i], peer)
            for i, (peer, slot) in enumerate(peers)
        ] + [
            pltpu.make_async_copy(tok.at[mine], s.x.at[rows_of(mine), :], s.t_own.at[0]),
            pltpu.make_async_copy(small, s.v_small.at[mine], s.t_own.at[1]),
        ]

    def cot_copies():
        return [
            remote(tok.at[slot], f_cot.at[mine], s.t_send.at[1, i], s.t_recv.at[1, i], peer)
            for i, (peer, slot) in enumerate(peers)
        ] + [pltpu.make_async_copy(tok.at[mine], f_cot.at[mine], s.t_own.at[2])]

    enc_copy = pltpu.make_async_copy(enc, s.e, s.t_own.at[3])
    enc_copy.start()
    arrange(tok_in, s.s_tok)
    small[...] = jnp.zeros_like(small)
    small[0:6, :] = bias[...].astype(F32)
    small[6:9, :] = gain_in[...].astype(F32)
    small[9:12, :] = shift_in[...].astype(F32)
    for i in range(4):
        small[12 + i:13 + i, :] = up_bias[:, i * 256:(i + 1) * 256].astype(F32)
    small[16:17, :] = down_bias[...].astype(F32)
    gather.greet()
    gather.advance(-2)
    for copy in token_copies():
        copy.start()

    def save(name, ref):
        return pltpu.make_async_copy(ref, saved[name], s.save_sem.at[SAVED.index(name)])

    def weight_saves(k):
        if k < 6:
            return [pltpu.make_async_copy(s.v_in.at[k], f_in.at[k], s.weight_sem.at[k])]
        if k < 8:
            return [pltpu.make_async_copy(s.v_out.at[k - 6], f_out.at[k - 6], s.weight_sem.at[k])]
        if k == 11:
            return [pltpu.make_async_copy(s.v_up, f_up, s.weight_sem.at[k])]
        if k == 15:
            return [pltpu.make_async_copy(s.v_down, f_down, s.weight_sem.at[k])]
        return []

    def ready(index):
        gather.ready(index)
        for copy in weight_saves(GATHER_ORDER[index]):
            copy.start()

    def project(dst, left, weight, count, bias):
        def block(i):
            columns = rows_at(i * 256, 256, 256)
            product = dot_nn(left[0:count, :], weight[:, columns])
            if bias is not None:
                product = product + s.vec[bias:bias + 1, columns]
            dst[0:count, columns] = product.astype(BF16)

        loop(4, block)

    def join(dst, base, left, weight, bias):
        def block(i):
            columns = rows_at(i * 256, 256, 256)
            dst[:, columns] = base[:, columns].astype(F32) + (
                dot_nn(left[...], weight[:, columns]) + s.vec[bias:bias + 1, columns]
            )

        loop(4, block)

    def normalize(sum_ref, index, low, last):
        gain, shift = s.vec[6 + index:7 + index, :], s.vec[9 + index:10 + index, :]

        def block(i):
            p = rows_at(i * 32, 32, 32)
            value = sum_ref[p, :]
            center = value - jnp.mean(value, axis=1, keepdims=True)
            scale = lax.rsqrt(jnp.mean(center * center, axis=1, keepdims=True) + epsilon)
            result = center * scale * gain + shift
            if last:
                low[p, :] = (result * mask[p, 0:1]).astype(BF16)
            else:
                s.hf[p, :] = result
                low[p, :] = result.astype(BF16)

        loop(16, block)

    lane = lax.broadcasted_iota(jnp.int32, (1, 128), 1)
    head_masks = [(lane < 64).astype(F32).astype(BF16), (lane >= 64).astype(F32).astype(BF16)]

    def attend_pair(i, q_ref, k_ref, v_ref, o_ref, key_count, causal):
        lanes = rows_at(i * 128, 128, 128)
        for block in (0, 1):
            rows = pl.ds(block * 256, 256)
            reach = (block + 1) * 256 if causal else key_count
            query = q_ref[rows, lanes]
            key, value = k_ref[0:reach, lanes], v_ref[0:reach, lanes]
            context = jnp.zeros((256, 128), F32)
            for head_mask in head_masks:
                scores = dot_nt(query * head_mask, key) * 0.125
                if causal:
                    query_at = lax.broadcasted_iota(jnp.int32, (256, reach), 0) + block * 256
                    key_at = lax.broadcasted_iota(jnp.int32, (256, reach), 1)
                    scores = jnp.where(key_at <= query_at, scores, -1e30)
                weights = jnp.exp(scores - jnp.max(scores, axis=1, keepdims=True))
                weights = weights * (1.0 / jnp.sum(weights, axis=1, keepdims=True))
                context = context + dot_nn(weights.astype(BF16), value * head_mask)
            o_ref[rows, lanes] = context.astype(BF16)

    length = jnp.int32(0)
    for i in range(4):
        here = sum(jnp.where(sequence_at[i] == j, lengths[0, j], 0) for j in range(4))
        length = length + jnp.where(mine == i, here, 0)
    mask[...] = (lax.broadcasted_iota(jnp.int32, (512, 128), 0) < length).astype(F32)
    ready(0)
    for copy in token_copies():
        copy.wait()
    for i in range(4):
        s.vec[:, i * 256:(i + 1) * 256] = s.v_small[i]
    gains[...] = s.vec[0:16, :]
    save("x", s.x).start()
    project(s.q, s.x, s.v_in.at[0], 512, 0)
    save("q", s.q).start()
    ready(1)
    project(s.k, s.x, s.v_in.at[1], 512, None)
    save("k", s.k).start()
    ready(2)
    project(s.v, s.x, s.v_in.at[2], 512, 1)
    save("v", s.v).start()
    for part in range(4):
        loop(2, lambda i, part=part: attend_pair(part * 2 + i, s.q, s.k, s.v, s.o, 512, True))
        gather.advance(6 + part)
    save("o", s.o).start()
    ready(3)
    join(s.sum_a, s.x, s.o, s.v_out.at[0], 2)
    save("sum1", s.sum_a).start()
    ready(4)
    normalize(s.sum_a, 0, s.h1, False)
    save("h1", s.h1).start()
    enc_copy.wait()
    project(s.k2, s.e, s.v_in.at[4], 256, None)
    save("k2", s.k2).start()
    ready(5)
    project(s.v2, s.e, s.v_in.at[5], 256, 4)
    save("v2", s.v2).start()
    ready(6)
    project(s.q2, s.h1, s.v_in.at[3], 512, 3)
    save("q2", s.q2).start()
    ready(7)
    for part in range(4):
        loop(2, lambda i, part=part: attend_pair(part * 2 + i, s.q2, s.k2, s.v2, s.o2, 256, False))
        gather.advance(11 + part // 2)
    save("o2", s.o2).start()
    join(s.sum_b, s.hf, s.o2, s.v_out.at[1], 5)
    save("sum2", s.sum_b).start()
    ready(10)
    normalize(s.sum_b, 1, s.h2, False)
    save("h2", s.h2).start()
    arrange(cot_in, s.s_tok)
    for copy in cot_copies():
        copy.start()
    save("sum1", s.sum_a).wait()

    def widen(i):
        p = rows_at(i * 64, 64, 64)
        s.sum_a[p, :] = s.hf[p, :] + s.vec[16:17, :]

    loop(8, widen)
    ready(11)

    def block_copies(j, i, slot):
        columns = rows_at(i * 1024 + j * 256, 256, 256)
        return [
            pltpu.make_async_copy(s.gblock.at[slot], g_all.at[:, columns], s.block_sem.at[slot, 0]),
            pltpu.make_async_copy(s.dblock.at[slot], d_all.at[:, columns], s.block_sem.at[slot, 1]),
        ]

    for j in range(4):
        ready(12 + j)

        def mlp(i, j=j):
            slot = lax.rem(i, 2)
            columns = rows_at(i * 1024 + j * 256, 256, 256)
            if j > 0:
                for copy in block_copies(j, i, slot):
                    copy.wait()
            else:
                @pl.when(i >= 2)
                def _():
                    for copy in block_copies(j, i, slot):
                        copy.wait()

            s.ublock[...] = dot_nn(s.h2[...], s.v_up[:, columns])
            bias = s.v_small[i, 12 + j:13 + j, :]

            def hidden(r):
                p = rows_at(r * 64, 64, 64)
                value = s.ublock[p, :] + bias
                cdf = normal_cdf(value)
                pdf = jnp.exp(-0.5 * value * value) * 0.3989422804014327
                s.gblock[slot, p, :] = (value * cdf).astype(BF16)
                s.dblock[slot, p, :] = cdf + value * pdf

            loop(8, hidden)
            for copy in block_copies(j, i, slot):
                copy.start()

            def out(n):
                wide = rows_at(n * 256, 256, 256)
                s.sum_a[:, wide] += dot_nn(s.gblock[slot], s.v_down[columns, wide])

            loop(4, out)

        loop(4, mlp)

    save("sum3", s.sum_a).start()
    normalize(s.sum_a, 2, s.y, True)
    save("y", s.y).start()
    for copy in block_copies(3, 2, 0) + block_copies(3, 3, 1) + cot_copies():
        copy.wait()
    for k in range(16):
        for copy in weight_saves(k):
            copy.wait()
    ends = dict(
        x=s.x, q=s.q, k=s.k, v=s.v, o=s.o, h1=s.h1, q2=s.q2, k2=s.k2, v2=s.v2, o2=s.o2, h2=s.h2,
        sum2=s.sum_b, sum3=s.sum_a, y=s.y,
    )
    for name, ref in ends.items():
        save(name, ref).wait()


def forward(*operands):
    any_space = pl.BlockSpec(memory_space=pl.ANY)
    in_vmem = pl.BlockSpec(memory_space=pltpu.VMEM)
    in_smem = pl.BlockSpec(memory_space=pltpu.SMEM)
    wide = {"sum1", "sum2", "sum3"}
    return pl.pallas_call(
        forward_kernel,
        out_shape=(
            jax.ShapeDtypeStruct((6, 1024, 1024), BF16),
            jax.ShapeDtypeStruct((2, 1024, 1024), BF16),
            jax.ShapeDtypeStruct((1024, 4096), BF16),
            jax.ShapeDtypeStruct((4096, 1024), BF16),
            jax.ShapeDtypeStruct((4, 128, 1024), BF16),
            jax.ShapeDtypeStruct((16, 1024), F32),
            jax.ShapeDtypeStruct((512, 128), F32),
            jax.ShapeDtypeStruct((512, 4096), BF16),
            jax.ShapeDtypeStruct((512, 4096), F32),
        ) + tuple(
            jax.ShapeDtypeStruct((256 if name in ("k2", "v2") else 512, 1024), F32 if name in wide else BF16)
            for name in SAVED
        ),
        in_specs=[in_smem] * 2 + [in_vmem] * 7 + [any_space] * 5,
        out_specs=(any_space,) * 5 + (in_vmem,) * 2 + (any_space,) * 17,
        scratch_shapes=list(FORWARD_SCRATCH.values()),
        compiler_params=pltpu.CompilerParams(
            collective_id=2, has_side_effects=True, vmem_limit_bytes=62 << 20
        ),
    )(*operands)


def sum_plain(*parts):
    dims = (1, 1, 1, 1, 1, 0, 0, 0, 0)
    scattered = [
        lax.psum_scatter(part.astype(jnp.bfloat16), "shard", scatter_dimension=dim, tiled=True)
        for part, dim in zip(parts, dims)
    ]
    return tuple(lax.psum(part, "rep").astype(jnp.float32) for part in scattered)


def finish_kernel(owner, total, small_total, out_back, grad_back, *refs):
    out, grad_tok, g_in, g_out, g_up, g_down, g_bias, g_gain, g_shift, g_up_bias, g_down_bias, w_in, w_out, w_up, w_down, sem, row_sem = refs
    copies = []
    for i in range(4):
        for j, (src, dst) in enumerate(((out_back, out), (grad_back, grad_tok))):
            copies.append(pltpu.make_async_copy(src.at[jnp.clip(owner[0, i], 0, 3)], dst.at[i], row_sem.at[i, j]))
            copies[-1].start()
    g_bias[...] = small_total[0:6, :]
    g_gain[...] = small_total[6:9, :]
    g_shift[...] = small_total[9:12, :]
    for i in range(4):
        g_up_bias[:, i * 256:(i + 1) * 256] = small_total[12 + i:13 + i, :]
    g_down_bias[...] = small_total[16:17, :]

    def widen(k, dst):
        def block(i):
            p = rows_at(i * 32, 32, 32)
            dst(p, total[k, p, :].astype(F32))

        loop(4, block)

    def send(src, dst, index):
        copies.append(pltpu.make_async_copy(src, dst, sem.at[index]))
        copies[-1].start()

    for j in range(8):
        def up(p, value):
            for half in (0, 1):
                rows = rows_at(p.start + half * 128, 32, 32)
                for c in range(4):
                    w_up[rows, c * 1024 + j * 128:c * 1024 + j * 128 + 128] = (
                        value[:, half * 512 + c * 128:half * 512 + c * 128 + 128]
                    )

        widen(2 * j + 1, up)
        rows = pl.ds(j * 128, 128)

        def down(p, value):
            w_down[rows_at(j * 128 + p.start, 32, 32), :] = value

        widen(2 * j, down)
        send(w_down.at[rows, :], g_down.at[rows, :], j)
    send(w_up, g_up, 8)
    order = [(g_out, w_out, 1, 16), (g_in, w_in, 3, 18), (g_in, w_in, 4, 20), (g_in, w_in, 5, 22),
             (g_out, w_out, 0, 24), (g_in, w_in, 0, 26), (g_in, w_in, 1, 28), (g_in, w_in, 2, 30)]
    for n, (dst, held, index, chunk) in enumerate(order):
        for half in (0, 1):
            def place_rows(p, value):
                held[index, rows_at(half * 128 + p.start, 32, 32), :] = value

            widen(chunk + half, place_rows)
        send(held.at[index], dst.at[index], 9 + n)
    for copy in copies:
        copy.wait()


def finish(owner, total, small_total, out_back, grad_back):
    any_space = pl.BlockSpec(memory_space=pl.ANY)
    in_vmem = pl.BlockSpec(memory_space=pltpu.VMEM)
    narrow = [(6, 256), (3, 256), (3, 256), (1, 1024), (1, 256)]
    wide = [(6, 256, 1024), (2, 256, 1024), (256, 4096), (1024, 1024)]
    return pl.pallas_call(
        finish_kernel,
        out_shape=tuple(
            [jax.ShapeDtypeStruct((4, 128, 1024), BF16)] * 2
            + [jax.ShapeDtypeStruct(shape, F32) for shape in wide]
            + [jax.ShapeDtypeStruct(shape, F32) for shape in narrow]
        ),
        in_specs=[pl.BlockSpec(memory_space=pltpu.SMEM)] + [in_vmem] * 4,
        out_specs=tuple([any_space] * 6 + [in_vmem] * 5),
        scratch_shapes=[pltpu.VMEM(shape, F32) for shape in wide]
        + [pltpu.SemaphoreType.DMA((17,)), pltpu.SemaphoreType.DMA((4, 2))],
        compiler_params=pltpu.CompilerParams(vmem_limit_bytes=60 << 20),
    )(owner, total, small_total, out_back, grad_back)


def fast_layer(
    tokens, enc_states, cotangent, lengths, owner, attn_in, attn_out, attn_bias,
    norm_gain, norm_bias, mlp_in, mlp_bias_in, mlp_out, mlp_bias_out,
):
    encoder = enc_states[0]
    full_in, full_out, up_full, down_full, cot, vectors, mask, g_all, d_all, *saved = forward(
        owner, lengths, attn_bias, norm_gain, norm_bias, mlp_bias_in.reshape(1, 1024),
        mlp_bias_out.reshape(1, 256), tokens, cotangent, attn_in, attn_out, mlp_in, mlp_out, encoder,
    )
    saved = dict(zip(SAVED, saved))
    loads = dict(
        x1=saved["x"], q1=saved["q"], k1=saved["k"], v1=saved["v"], o1=saved["o"], h1=saved["h1"],
        q2=saved["q2"], k2=saved["k2"], v2=saved["v2"], o2=saved["o2"], h2=saved["h2"], e1=encoder,
        cot=cot.reshape(512, 1024), sum1=saved["sum1"], sum2=saved["sum2"], sum3=saved["sum3"],
    )
    total, small_total, encoder_grad, back_blocks, grad_blocks, _ = backward(
        loads, d_all, g_all, full_in, full_out, up_full, down_full, vectors, saved["y"], mask
    )
    out, grad_tokens, g_in, g_out, g_up, g_down, *small = finish(
        owner, total, small_total, back_blocks, grad_blocks
    )
    return (
        out, grad_tokens, encoder_grad[None], g_in, g_out, small[0], small[1], small[2],
        g_up, small[3].reshape(1024), g_down, small[4].reshape(256),
    )


def local(
    tokens,
    enc_states,
    cotangent,
    lengths,
    owner,
    attn_in,
    attn_out,
    attn_bias,
    norm_gain,
    norm_bias,
    mlp_in,
    mlp_bias_in,
    mlp_out,
    mlp_bias_out,
):
    groups = lax.axis_size("shard")
    if (lax.axis_size("rep"), groups) == (8, 4):
        return fast_layer(
            tokens, enc_states, cotangent, lengths, owner, attn_in, attn_out, attn_bias,
            norm_gain, norm_bias, mlp_in, mlp_bias_in, mlp_out, mlp_bias_out,
        )
    my_index = lax.axis_index("shard")
    owner_row = owner[0]
    slot_ids = jnp.arange(groups, dtype=jnp.int32)
    matches = owner_row[None, :] == slot_ids[:, None]
    sequence_at = jnp.sum(jnp.where(matches, slot_ids[None, :], 0), axis=1)
    my_sequence = jnp.sum(jnp.where(slot_ids == my_index, sequence_at, 0))
    my_length = jnp.sum(jnp.where(slot_ids == my_sequence, lengths[0], 0))
    sent_tokens = pick_blocks(tokens, sequence_at)
    sent_grads = pick_blocks(cotangent, sequence_at)
    got_tokens, got_grads = (
        lax.all_to_all(sent_tokens, "shard", split_axis=0, concat_axis=1, tiled=True),
        lax.all_to_all(sent_grads, "shard", split_axis=0, concat_axis=1, tiled=True),
    )
    full_in, full_out, full_bias, full_gain, full_shift = (
        lax.all_gather(attn_in, "shard", axis=1, tiled=True),
        lax.all_gather(attn_out, "shard", axis=1, tiled=True),
        lax.all_gather(attn_bias, "shard", axis=1, tiled=True),
        lax.all_gather(norm_gain, "shard", axis=1, tiled=True),
        lax.all_gather(norm_bias, "shard", axis=1, tiled=True),
    )
    bias_rows = full_bias.astype(jnp.float32)
    gain_rows = full_gain.astype(jnp.float32)
    shift_rows = full_shift.astype(jnp.float32)
    up_full, up_bias, down_full, down_bias = (
        lax.all_gather(mlp_in, "shard", axis=0, tiled=True),
        lax.all_gather(mlp_bias_in, "shard", axis=0, tiled=True),
        lax.all_gather(mlp_out, "shard", axis=0, tiled=True),
        lax.all_gather(mlp_bias_out, "shard", axis=0, tiled=True),
    )
    in_back, out_back, up_back, down_back = full_in, full_out, up_full, down_full
    inputs = got_tokens[0]
    row_count = inputs.shape[0]
    row_mask = (jnp.arange(row_count, dtype=jnp.int32) < my_length).astype(jnp.float32)[:, None]
    encoder = enc_states[0]
    projected = jnp.einsum("rd,wde->wre", inputs, full_in[:3], preferred_element_type=jnp.float32)
    queries = (projected[0] + bias_rows[0]).astype(jnp.bfloat16)
    keys = projected[1].astype(jnp.bfloat16)
    values = (projected[2] + bias_rows[1]).astype(jnp.bfloat16)
    context, log_totals = attention_forward(queries, keys, values, True)
    first_sum = inputs.astype(jnp.float32) + (matmul(context, full_out[0]) + bias_rows[2])
    first_norm = layer_norm(first_sum, gain_rows[0], shift_rows[0])
    first_low = first_norm.astype(jnp.bfloat16)
    cross_queries = (matmul(first_low, full_in[3]) + bias_rows[3]).astype(jnp.bfloat16)
    cross_projected = jnp.einsum(
        "rd,wde->wre", encoder, full_in[4:6], preferred_element_type=jnp.float32
    )
    cross_keys = cross_projected[0].astype(jnp.bfloat16)
    cross_values = (cross_projected[1] + bias_rows[4]).astype(jnp.bfloat16)
    cross_context, cross_totals = attention_forward(cross_queries, cross_keys, cross_values, False)
    second_sum = first_norm + (matmul(cross_context, full_out[1]) + bias_rows[5])
    second_norm = layer_norm(second_sum, gain_rows[1], shift_rows[1])
    second_low = second_norm.astype(jnp.bfloat16)
    hidden_pre = matmul(second_low, up_full) + up_bias.astype(jnp.float32)
    hidden_low = gelu_exact(hidden_pre).astype(jnp.bfloat16)
    third_sum = second_norm + (matmul(hidden_low, down_full) + down_bias.astype(jnp.float32))
    result = (layer_norm(third_sum, gain_rows[2], shift_rows[2]) * row_mask).astype(jnp.bfloat16)
    back_blocks = lax.all_to_all(result[None], "shard", split_axis=1, concat_axis=0, tiled=True)
    output = pick_blocks(back_blocks, owner_row)
    out_grad = got_grads[0].astype(jnp.float32) * row_mask
    third_grad, third_gain_grad, third_shift_grad = jax.vjp(
        layer_norm, third_sum, gain_rows[2], shift_rows[2]
    )[1](out_grad)
    down_grad_in = third_grad.astype(jnp.bfloat16)
    grad_down = contract_rows(hidden_low, down_grad_in)
    grad_down_bias = column_sum(down_grad_in)
    hidden_grad = contract_cols(down_grad_in, down_back)
    hidden_pre_grad = jax.vjp(gelu_exact, hidden_pre)[1](hidden_grad)[0].astype(jnp.bfloat16)
    grad_up = contract_rows(second_low, hidden_pre_grad)
    grad_up_bias = column_sum(hidden_pre_grad)
    second_norm_grad = third_grad + contract_cols(hidden_pre_grad, up_back)
    second_grad, second_gain_grad, second_shift_grad = jax.vjp(
        layer_norm, second_sum, gain_rows[1], shift_rows[1]
    )[1](second_norm_grad)
    cross_out_grad = second_grad.astype(jnp.bfloat16)
    grad_cross_out = contract_rows(cross_context, cross_out_grad)
    grad_cross_out_bias = column_sum(cross_out_grad)
    cross_context_grad = contract_cols(cross_out_grad, out_back[1]).astype(jnp.bfloat16)
    cross_query_grad, cross_key_grad, cross_value_grad = attention_backward(
        cross_queries, cross_keys, cross_values, cross_totals, cross_context_grad, False
    )
    cross_query_low = cross_query_grad.astype(jnp.bfloat16)
    cross_key_low = cross_key_grad.astype(jnp.bfloat16)
    cross_value_low = cross_value_grad.astype(jnp.bfloat16)
    grad_cross_query = contract_rows(first_low, cross_query_low)
    grad_cross_query_bias = column_sum(cross_query_low)
    grad_cross_key = contract_rows(encoder, cross_key_low)
    grad_cross_value = contract_rows(encoder, cross_value_low)
    grad_cross_value_bias = column_sum(cross_value_low)
    encoder_grad = (
        contract_cols(cross_key_low, in_back[4]) + contract_cols(cross_value_low, in_back[5])
    ).astype(jnp.bfloat16)
    first_norm_grad = second_grad + contract_cols(cross_query_low, in_back[3])
    first_grad, first_gain_grad, first_shift_grad = jax.vjp(
        layer_norm, first_sum, gain_rows[0], shift_rows[0]
    )[1](first_norm_grad)
    self_out_grad = first_grad.astype(jnp.bfloat16)
    grad_self_out = contract_rows(context, self_out_grad)
    grad_self_out_bias = column_sum(self_out_grad)
    context_grad = contract_cols(self_out_grad, out_back[0]).astype(jnp.bfloat16)
    query_grad, key_grad, value_grad = attention_backward(
        queries, keys, values, log_totals, context_grad, True
    )
    query_low = query_grad.astype(jnp.bfloat16)
    key_low = key_grad.astype(jnp.bfloat16)
    value_low = value_grad.astype(jnp.bfloat16)
    grad_query = contract_rows(inputs, query_low)
    grad_query_bias = column_sum(query_low)
    grad_key = contract_rows(inputs, key_low)
    grad_value = contract_rows(inputs, value_low)
    grad_value_bias = column_sum(value_low)
    input_grad = (
        first_grad
        + contract_cols(query_low, in_back[0])
        + contract_cols(key_low, in_back[1])
        + contract_cols(value_low, in_back[2])
    ).astype(jnp.bfloat16)
    grad_blocks = lax.all_to_all(input_grad[None], "shard", split_axis=1, concat_axis=0, tiled=True)
    grad_tokens = pick_blocks(grad_blocks, owner_row)
    grad_in_full = jnp.stack(
        [grad_query, grad_key, grad_value, grad_cross_query, grad_cross_key, grad_cross_value]
    )
    grad_out_full = jnp.stack([grad_self_out, grad_cross_out])
    grad_bias_full = jnp.stack(
        [
            grad_query_bias,
            grad_value_bias,
            grad_self_out_bias,
            grad_cross_query_bias,
            grad_cross_value_bias,
            grad_cross_out_bias,
        ]
    )
    grad_gain_full = jnp.stack([first_gain_grad, second_gain_grad, third_gain_grad])
    grad_shift_full = jnp.stack([first_shift_grad, second_shift_grad, third_shift_grad])
    summed = sum_plain(
        grad_in_full, grad_out_full, grad_bias_full, grad_gain_full, grad_shift_full,
        grad_up, grad_up_bias, grad_down, grad_down_bias,
    )
    return (
        output,
        grad_tokens,
        encoder_grad[None],
        summed[0],
        summed[1],
        summed[2],
        summed[3],
        summed[4],
        summed[5],
        summed[6],
        summed[7],
        summed[8],
    )


def solution(mesh):
    placed = (
        P("rep", "shard", None),
        P(("rep", "shard"), None, None),
        P("rep", "shard", None),
        P("rep", None),
        P("rep", None),
        P(None, "shard", None),
        P(None, "shard", None),
        P(None, "shard"),
        P(None, "shard"),
        P(None, "shard"),
        P("shard", None),
        P("shard"),
        P("shard", None),
        P("shard"),
    )
    return jax.shard_map(
        local,
        mesh=mesh,
        in_specs=placed,
        out_specs=(
            P("rep", "shard", None),
            P("rep", "shard", None),
            P(("rep", "shard"), None, None),
            P(None, "shard", None),
            P(None, "shard", None),
            P(None, "shard"),
            P(None, "shard"),
            P(None, "shard"),
            P("shard", None),
            P("shard"),
            P("shard", None),
            P("shard"),
        ),
        check_vma=False,
    )
```

```python
import types

import jax
import jax.numpy as jnp
from jax import lax
from jax.experimental import pallas as pl
from jax.experimental.pallas import tpu as pltpu
from jax.sharding import PartitionSpec as P

HEADS = 16
HEAD_DIM = 64


epsilon = 1e-05


def matmul(left, right):
    return jnp.dot(left, right, preferred_element_type=jnp.float32)


def contract_rows(left, right):
    return lax.dot_general(
        left, right, (((0,), (0,)), ((), ())), preferred_element_type=jnp.float32
    )


def contract_cols(left, right):
    return lax.dot_general(
        left, right, (((1,), (1,)), ((), ())), preferred_element_type=jnp.float32
    )


def layer_norm(features, norm_scale, norm_shift):
    center = features - jnp.mean(features, axis=-1, keepdims=True)
    spread = jnp.mean(center * center, axis=-1, keepdims=True)
    return center * lax.rsqrt(spread + epsilon) * norm_scale + norm_shift


def gelu_exact(features):
    return jax.nn.gelu(features, approximate=False)


def column_sum(matrix):
    return jnp.sum(matrix.astype(jnp.float32), axis=0)


def split_heads(matrix):
    width = min(4, HEADS)
    return jnp.moveaxis(matrix.reshape(matrix.shape[0], HEADS // width, width, HEAD_DIM), 1, 0)


def merge_heads(stacked):
    return jnp.moveaxis(stacked, 0, 1).reshape(stacked.shape[1], HEADS * HEAD_DIM)


def block_scores(query_block, key_group, offset, causal):
    scores = jnp.einsum(
        "qgd,kgd->gqk", query_block, key_group, preferred_element_type=jnp.float32
    ) * HEAD_DIM ** (-0.5)
    if causal:
        query_pos = offset + jnp.arange(query_block.shape[0], dtype=jnp.int32)
        key_pos = jnp.arange(key_group.shape[0], dtype=jnp.int32)
        scores = jnp.where(key_pos[None, None, :] <= query_pos[None, :, None], scores, -jnp.inf)
    return scores


def attention_forward(queries, keys, values, causal):
    row_count = queries.shape[0]
    block_rows = min(512, row_count)
    block_count = row_count // block_rows
    offsets = jnp.arange(block_count, dtype=jnp.int32) * block_rows

    def per_group(operands):
        query_group, key_group, value_group = operands
        width = query_group.shape[1]
        query_blocks = query_group.reshape(block_count, block_rows, width, HEAD_DIM)

        def per_block(block_items):
            query_block, offset = block_items
            scores = block_scores(query_block, key_group, offset, causal)
            peak = jnp.max(scores, axis=-1, keepdims=True)
            log_total = peak + jnp.log(jnp.sum(jnp.exp(scores - peak), axis=-1, keepdims=True))
            weights_low = jnp.exp(scores - log_total).astype(jnp.bfloat16)
            context = jnp.einsum(
                "gqk,kgd->qgd", weights_low, value_group, preferred_element_type=jnp.float32
            )
            return (context.astype(jnp.bfloat16), log_total)

        context, log_totals = lax.map(per_block, (query_blocks, offsets))
        return (context.reshape(row_count, width, HEAD_DIM), log_totals)

    context, log_totals = lax.map(
        per_group, (split_heads(queries), split_heads(keys), split_heads(values))
    )
    return (merge_heads(context), log_totals)


def attention_backward(queries, keys, values, log_totals, context_grad, causal):
    row_count = queries.shape[0]
    block_rows = min(512, row_count)
    block_count = row_count // block_rows
    offsets = jnp.arange(block_count, dtype=jnp.int32) * block_rows
    scale = HEAD_DIM ** (-0.5)

    def per_group(operands):
        query_group, key_group, value_group, grad_group, total_group = operands
        width = query_group.shape[1]
        query_blocks = query_group.reshape(block_count, block_rows, width, HEAD_DIM)
        grad_blocks = grad_group.reshape(block_count, block_rows, width, HEAD_DIM)

        def per_block(accumulated, block_items):
            key_grad, value_grad = accumulated
            query_block, grad_block, log_total, offset = block_items
            scores = block_scores(query_block, key_group, offset, causal)
            weights_full = jnp.exp(scores - log_total)
            weights_low = weights_full.astype(jnp.bfloat16)
            value_grad = value_grad + jnp.einsum(
                "gqk,qgd->kgd", weights_low, grad_block, preferred_element_type=jnp.float32
            )
            weight_grad = jnp.einsum(
                "qgd,kgd->gqk", grad_block, value_group, preferred_element_type=jnp.float32
            )
            row_dot = jnp.sum(weights_full * weight_grad, axis=-1, keepdims=True)
            score_grad = (weights_full * (weight_grad - row_dot)).astype(jnp.bfloat16)
            query_grad = (
                jnp.einsum(
                    "gqk,kgd->qgd", score_grad, key_group, preferred_element_type=jnp.float32
                )
                * scale
            )
            key_grad = (
                key_grad
                + jnp.einsum(
                    "gqk,qgd->kgd", score_grad, query_block, preferred_element_type=jnp.float32
                )
                * scale
            )
            return ((key_grad, value_grad), query_grad)

        empty_grad = jnp.zeros(key_group.shape, jnp.float32)
        (key_grad, value_grad), query_grad = lax.scan(
            per_block, (empty_grad, empty_grad), (query_blocks, grad_blocks, total_group, offsets)
        )
        return (query_grad.reshape(row_count, width, HEAD_DIM), key_grad, value_grad)

    query_grad, key_grad, value_grad = lax.map(
        per_group,
        (
            split_heads(queries),
            split_heads(keys),
            split_heads(values),
            split_heads(context_grad),
            log_totals,
        ),
    )
    return (merge_heads(query_grad), merge_heads(key_grad), merge_heads(value_grad))


def pick_blocks(blocks, order):
    count = blocks.shape[0]
    return jnp.concatenate(
        [lax.dynamic_slice_in_dim(blocks, order[i], 1, axis=0) for i in range(count)], axis=0
    )


MESH = pl.DeviceIdType.MESH
ROWS = 128
CHUNKS = 32


def place():
    rep, shard = lax.axis_index("rep"), lax.axis_index("shard")
    return rep // 2, lax.rem(rep, 2), shard // 2, lax.rem(shard, 2)


def device(z, y, x, c):
    return (z * 2 + y, x * 2 + c)


def greet(peers):
    barrier = pltpu.get_barrier_semaphore()
    for peer in peers:
        pl.semaphore_signal(barrier, inc=1, device_id=peer, device_id_type=MESH)
    pl.semaphore_wait(barrier, len(peers))


def rows_at(base, size, align):
    return pl.ds(pl.multiple_of(base, align), size)


F32, BF16 = jnp.float32, jnp.bfloat16
RING = 8
LAGS = (0, 1, 3, 4, 5, 6, 7)


def dot_over(left, right, a, b):
    return lax.dot_general(left, right, (((a,), (b,)), ((), ())), preferred_element_type=F32)


def dot_nn(left, right):
    return dot_over(left, right, 1, 0)


def dot_nt(left, right):
    return dot_over(left, right, 1, 1)


def dot_tn(left, right):
    return dot_over(left, right, 0, 0)


def remote(src, dst, send, recv, peer):
    return pltpu.make_async_remote_copy(
        src_ref=src, dst_ref=dst, send_sem=send, recv_sem=recv, device_id=peer, device_id_type=MESH
    )


def loop(count, body):
    def step(i, carry):
        body(i)
        return carry

    lax.fori_loop(0, count, step, 0)


ERF_TOP = (
    -2.72614225801306e-10, 2.77068142495902e-08, -2.10102402082508e-06, -5.69250639462346e-05,
    -7.34990630326855e-04, -2.95459980854025e-03, -1.60960333262415e-02,
)
ERF_BOTTOM = (
    -1.45660718464996e-05, -2.13374055278905e-04, -1.68282697438203e-03, -7.37332916720468e-03,
    -1.42647390514189e-02,
)


def normal_cdf(value):
    arg = jnp.clip(value * 0.7071067811865476, -3.832506856900711, 3.832506856900711)
    square = arg * arg
    top, bottom = jnp.full_like(arg, ERF_TOP[0]), jnp.full_like(arg, ERF_BOTTOM[0])
    for factor in ERF_TOP[1:]:
        top = top * square + factor
    for factor in ERF_BOTTOM[1:]:
        bottom = bottom * square + factor
    return 0.5 + 0.5 * (arg * top / bottom)


BACK_SCRATCH = dict(
    mine=pltpu.VMEM((4, 2, ROWS, 1024), BF16),
    r0=pltpu.VMEM((RING, 2, ROWS, 1024), BF16),
    r1=pltpu.VMEM((RING, ROWS, 1024), BF16),
    r2=pltpu.VMEM((RING, ROWS // 2, 1024), BF16),
    r3=pltpu.VMEM((RING, 3, ROWS // 8, 1024), BF16),
    held=pltpu.VMEM((RING, ROWS // 8, 1024), BF16),
    small=pltpu.VMEM((4, 24, 256), F32),
    s0=pltpu.VMEM((2, 24, 256), F32),
    s1=pltpu.VMEM((24, 256), F32),
    s2=pltpu.VMEM((24, 256), F32),
    s3=pltpu.VMEM((3, 24, 256), F32),
    own_sem=pltpu.SemaphoreType.DMA((4, 2)),
    c_send=pltpu.SemaphoreType.DMA((CHUNKS, 2)),
    c_recv=pltpu.SemaphoreType.DMA((CHUNKS, 2)),
    x_send=pltpu.SemaphoreType.DMA((CHUNKS,)),
    x_recv=pltpu.SemaphoreType.DMA((CHUNKS,)),
    y_send=pltpu.SemaphoreType.DMA((CHUNKS,)),
    y_recv=pltpu.SemaphoreType.DMA((CHUNKS,)),
    z_send=pltpu.SemaphoreType.DMA((CHUNKS, 3)),
    z_recv=pltpu.SemaphoreType.DMA((CHUNKS, 3)),
    a_send=pltpu.SemaphoreType.DMA((CHUNKS, 3)),
    a_recv=pltpu.SemaphoreType.DMA((CHUNKS, 3)),
    a_own=pltpu.SemaphoreType.DMA((CHUNKS,)),
    b_send=pltpu.SemaphoreType.DMA((CHUNKS,)),
    b_recv=pltpu.SemaphoreType.DMA((CHUNKS,)),
    t_send=pltpu.SemaphoreType.DMA((7,)),
    t_recv=pltpu.SemaphoreType.DMA((7,)),
    o_send=pltpu.SemaphoreType.DMA((2, 3)),
    o_recv=pltpu.SemaphoreType.DMA((2, 3)),
    o_own=pltpu.SemaphoreType.DMA((2,)),
    load_sem=pltpu.SemaphoreType.DMA((16,)),
    tile_sem=pltpu.SemaphoreType.DMA((2, 16)),
    weight_sem=pltpu.SemaphoreType.DMA((2,)),
    grad_sem=pltpu.SemaphoreType.DMA((2,)),
    x1=pltpu.VMEM((512, 1024), BF16),
    q1=pltpu.VMEM((512, 1024), BF16),
    k1=pltpu.VMEM((512, 1024), BF16),
    v1=pltpu.VMEM((512, 1024), BF16),
    o1=pltpu.VMEM((512, 1024), BF16),
    h1=pltpu.VMEM((512, 1024), BF16),
    q2=pltpu.VMEM((512, 1024), BF16),
    k2=pltpu.VMEM((256, 1024), BF16),
    v2=pltpu.VMEM((256, 1024), BF16),
    o2=pltpu.VMEM((512, 1024), BF16),
    h2=pltpu.VMEM((512, 1024), BF16),
    e1=pltpu.VMEM((256, 1024), BF16),
    cot=pltpu.VMEM((512, 1024), BF16),
    sum1=pltpu.VMEM((512, 1024), F32),
    sum2=pltpu.VMEM((512, 1024), F32),
    sum3=pltpu.VMEM((512, 1024), F32),
    dz=pltpu.VMEM((512, 1024), F32),
    low=pltpu.VMEM((512, 1024), BF16),
    dob=pltpu.VMEM((512, 1024), BF16),
    dqb=pltpu.VMEM((512, 1024), BF16),
    dkb=pltpu.VMEM((512, 1024), BF16),
    dvb=pltpu.VMEM((512, 1024), BF16),
    dka=pltpu.VMEM((512, 128), F32),
    dva=pltpu.VMEM((512, 128), F32),
    ut=pltpu.VMEM((2, 512, 512), F32),
    wd=pltpu.VMEM((2, 512, 1024), BF16),
    wu=pltpu.VMEM((2, 1024, 512), BF16),
    wb=pltpu.VMEM((2, 1024, 1024), BF16),
    gt=pltpu.VMEM((2, 512, 512), BF16),
    dut=pltpu.VMEM((512, 512), BF16),
    stage=pltpu.VMEM((2, 4, ROWS, 1024), BF16),
    sums=pltpu.VMEM((8, 1024), F32),
    ub=pltpu.VMEM((8, 1, 512), F32),
)
BACK_LOADS = (
    "x1", "q1", "k1", "v1", "o1", "h1", "q2", "k2", "v2", "o2", "h2", "e1", "cot", "sum1", "sum2", "sum3",
)


class Reducer:
    def __init__(self, s, parts, total, small_total):
        self.s, self.parts, self.total, self.small_total = s, parts, total, small_total
        z, y, x, c = self.at = place()
        self.core = device(z, y, x, 1 - c)
        self.xmate = device(z, y, 1 - x, c)
        self.diag = device(z, y, 1 - x, 1 - c)
        self.ymate = device(z, 1 - y, x, c)
        self.others = [device(lax.rem(z + i, 4), y, x, c) for i in (1, 2, 3)]

    def greet(self):
        greet([self.core, self.xmate, self.diag, self.ymate] + self.others)

    def core_copy(self, k, side):
        s, (_, _, _, c) = self.s, self.at
        return remote(
            self.parts.at[k, side * 2 + 1 - c], s.r0.at[lax.rem(k, RING), side],
            s.c_send.at[k, side], s.c_recv.at[k, side], self.core,
        )

    def own_copy(self, k, side):
        s, (_, _, _, c) = self.s, self.at
        slot = lax.rem(k, 4)
        return pltpu.make_async_copy(
            self.parts.at[k, side * 2 + c], s.mine.at[slot, side], s.own_sem.at[slot, side]
        )

    def fetch(self, k):
        for side in (0, 1):
            self.core_copy(k, side).start()
            self.own_copy(k, side).start()

    def x_copy(self, k):
        s, (_, _, x, _) = self.s, self.at
        slot = lax.rem(k, RING)
        return remote(s.r0.at[slot, 1 - x], s.r1.at[slot], s.x_send.at[k], s.x_recv.at[k], self.xmate)

    def core_sum(self, k):
        s, slot, near = self.s, lax.rem(k, RING), lax.rem(k, 4)
        for side in (0, 1):
            self.core_copy(k, side).wait()
            self.own_copy(k, side).wait()

        def add(i):
            piece = rows_at(i * 32, 32, 32)
            for side in (0, 1):
                s.r0[slot, side, piece, :] = s.r0[slot, side, piece, :] + s.mine[near, side, piece, :]

        loop(ROWS // 32, add)
        self.x_copy(k).start()

    def y_copy(self, k):
        s, (_, y, _, _) = self.s, self.at
        slot, half = lax.rem(k, RING), ROWS // 2
        return remote(
            s.r1.at[slot, rows_at((1 - y) * half, half, half), :], s.r2.at[slot],
            s.y_send.at[k], s.y_recv.at[k], self.ymate,
        )

    def x_sum(self, k):
        s, (_, _, x, _) = self.s, self.at
        slot = lax.rem(k, RING)
        self.x_copy(k).wait()

        def add(i):
            piece = rows_at(i * 32, 32, 32)
            s.r1[slot, piece, :] = s.r0[slot, x, piece, :] + s.r1[slot, piece, :]

        loop(ROWS // 32, add)
        self.y_copy(k).start()

    def z_copies(self, k):
        s, (z, _, _, _) = self.s, self.at
        slot, quarter = lax.rem(k, RING), ROWS // 8
        return [
            remote(
                s.r2.at[slot, rows_at(lax.rem(z + i + 1, 4) * quarter, quarter, quarter), :], s.r3.at[slot, i],
                s.z_send.at[k, i], s.z_recv.at[k, i], self.others[i],
            )
            for i in (0, 1, 2)
        ]

    def y_sum(self, k):
        s, (_, y, _, _) = self.s, self.at
        slot, half = lax.rem(k, RING), ROWS // 2
        self.y_copy(k).wait()

        def add(i):
            piece = rows_at(i * 32, 32, 32)
            s.r2[slot, piece, :] = s.r1[slot, rows_at(y * half + i * 32, 32, 32), :] + s.r2[slot, piece, :]

        loop(half // 32, add)
        for copy in self.z_copies(k):
            copy.start()

    def out_piece(self, k):
        z, y, _, _ = self.at
        return self.total.at[k, rows_at(y * (ROWS // 2) + z * (ROWS // 8), ROWS // 8, ROWS // 8), :]

    def spread_copies(self, k):
        s, slot = self.s, lax.rem(k, RING)
        return [
            remote(s.held.at[slot], self.out_piece(k), s.a_send.at[k, i], s.a_recv.at[k, i], self.others[i])
            for i in (0, 1, 2)
        ]

    def held_copy(self, k):
        return pltpu.make_async_copy(self.s.held.at[lax.rem(k, RING)], self.out_piece(k), self.s.a_own.at[k])

    def z_sum(self, k):
        s, (z, _, _, _) = self.s, self.at
        slot, quarter = lax.rem(k, RING), ROWS // 8
        for copy in self.z_copies(k):
            copy.wait()
        added = s.r2[slot, rows_at(z * quarter, quarter, quarter), :].astype(F32)
        for i in (0, 1, 2):
            added = added + s.r3[slot, i].astype(F32)
        s.held[slot] = added.astype(BF16)
        for copy in self.spread_copies(k):
            copy.start()
        self.held_copy(k).start()

    def half_copy(self, k):
        s, (_, y, _, _) = self.s, self.at
        half = ROWS // 2
        part = self.total.at[k, rows_at(y * half, half, half), :]
        return remote(part, part, s.b_send.at[k], s.b_recv.at[k], self.ymate)

    def spread_y(self, k):
        for copy in self.spread_copies(k):
            copy.wait()
        self.held_copy(k).wait()
        self.half_copy(k).start()

    def finish(self, k):
        self.half_copy(k).wait()

    def tick(self, t):
        stages = (self.fetch, self.core_sum, self.x_sum, self.y_sum, self.z_sum, self.spread_y, self.finish)
        for lag, act in zip(LAGS, stages):
            k = t - lag

            @pl.when((k >= 0) & (k < CHUNKS))
            def _(k=k, act=act):
                act(k)

    def small_steps(self, t):
        s, (_, _, x, c) = self.s, self.at
        send, recv = s.t_send, s.t_recv
        firsts = [
            remote(s.small.at[side * 2 + 1 - c], s.s0.at[side], send.at[side], recv.at[side], self.core)
            for side in (0, 1)
        ]
        across = remote(s.s0.at[1 - x], s.s1, send.at[2], recv.at[2], self.xmate)
        along = remote(s.s1, s.s2, send.at[3], recv.at[3], self.ymate)
        lasts = [
            remote(s.s2, s.s3.at[i], send.at[4 + i], recv.at[4 + i], self.others[i]) for i in (0, 1, 2)
        ]

        @pl.when(t == 0)
        def _():
            for copy in firsts:
                copy.start()

        @pl.when(t == 2)
        def _():
            for side in (0, 1):
                firsts[side].wait()
                s.s0[side] = s.s0[side] + s.small[side * 2 + c]
            across.start()

        @pl.when(t == 4)
        def _():
            across.wait()
            s.s1[...] = s.s1[...] + s.s0[x]
            along.start()

        @pl.when(t == 6)
        def _():
            along.wait()
            s.s2[...] = s.s2[...] + s.s1[...]
            for copy in lasts:
                copy.start()

        @pl.when(t == 8)
        def _():
            for copy in lasts:
                copy.wait()
            self.small_total[...] = s.s2[...] + s.s3[0] + s.s3[1] + s.s3[2]


def back_kernel(*refs):
    loads = dict(zip(BACK_LOADS, refs[:16]))
    d_all, g_all, f_in, f_out, f_up, f_down, gains, out_rows, mask = refs[16:25]
    total, small_total, grad_enc, out_back, grad_back, parts = refs[25:31]
    s = types.SimpleNamespace(**dict(zip(BACK_SCRATCH, refs[31:])))
    reducer = Reducer(s, parts, total, small_total)
    z, y, x, c = reducer.at
    mine = x * 2 + c
    peers = ((reducer.core, x * 2 + 1 - c), (reducer.xmate, (1 - x) * 2 + c), (reducer.diag, (1 - x) * 2 + 1 - c))

    def row_copies(which, src, dst):
        return [
            remote(
                src.at[rows_at(slot * 128, 128, 128), :], dst.at[mine],
                s.o_send.at[which, i], s.o_recv.at[which, i], peer,
            )
            for i, (peer, slot) in enumerate(peers)
        ] + [pltpu.make_async_copy(src.at[rows_at(mine * 128, 128, 128), :], dst.at[mine], s.o_own.at[which])]

    def load(name):
        return pltpu.make_async_copy(loads[name], getattr(s, name), s.load_sem.at[BACK_LOADS.index(name)])

    for name in ("sum3", "cot", "h2"):
        load(name).start()

    def tile_copies(j, slot):
        copies = []
        for i in range(4):
            columns = rows_at(i * 1024 + j * 128, 128, 128)
            copies += [
                pltpu.make_async_copy(
                    d_all.at[:, columns], s.ut.at[slot, :, pl.ds(i * 128, 128)], s.tile_sem.at[slot, i]
                ),
                pltpu.make_async_copy(
                    g_all.at[:, columns], s.gt.at[slot, :, pl.ds(i * 128, 128)], s.tile_sem.at[slot, 12 + i]
                ),
                pltpu.make_async_copy(
                    f_down.at[columns, :], s.wd.at[slot, pl.ds(i * 128, 128), :], s.tile_sem.at[slot, 4 + i]
                ),
                pltpu.make_async_copy(
                    f_up.at[:, columns], s.wu.at[slot, :, pl.ds(i * 128, 128)], s.tile_sem.at[slot, 8 + i]
                ),
            ]
        return copies

    for copy in tile_copies(0, 0):
        copy.start()
    weights = (
        f_out.at[1], f_in.at[4], f_in.at[5], f_in.at[3], f_out.at[0], f_in.at[0], f_in.at[1], f_in.at[2],
    )

    def weight(i):
        return pltpu.make_async_copy(weights[i], s.wb.at[i % 2], s.weight_sem.at[i % 2])

    reducer.greet()
    for copy in row_copies(0, out_rows, out_back):
        copy.start()
    for name in ("sum2", "o2", "q2", "k2", "v2", "h1", "e1", "sum1", "o1", "q1", "k1", "v1", "x1"):
        load(name).start()
    weight(0).start()
    weight(1).start()
    s.small[...] = jnp.zeros_like(s.small)

    def put(row, value):
        for i in range(4):
            s.small[i, row:row + 1, :] = value[:, i * 256:(i + 1) * 256]

    def norm_back(sum_ref, index, first, bias_row):
        s.sums[...] = jnp.zeros_like(s.sums)
        gain = gains[6 + index:7 + index, :]

        def block(i):
            p = rows_at(i * 32, 32, 32)
            value = sum_ref[p, :]
            grad = s.cot[p, :].astype(F32) * mask[p, 0:1] if first else s.dz[p, :]
            center = value - jnp.mean(value, axis=1, keepdims=True)
            scale = lax.rsqrt(jnp.mean(center * center, axis=1, keepdims=True) + epsilon)
            normal = center * scale
            scaled = grad * gain
            back = scale * (
                scaled - jnp.mean(scaled, axis=1, keepdims=True)
                - normal * jnp.mean(scaled * normal, axis=1, keepdims=True)
            )
            rounded = back.astype(BF16)
            s.dz[p, :] = back
            s.low[p, :] = rounded
            s.sums[0:1, :] += jnp.sum(grad * normal, axis=0, keepdims=True)
            s.sums[1:2, :] += jnp.sum(grad, axis=0, keepdims=True)
            s.sums[2:3, :] += jnp.sum(rounded.astype(F32), axis=0, keepdims=True)

        loop(16, block)
        put(6 + index, s.sums[0:1, :])
        put(9 + index, s.sums[1:2, :])
        put(bias_row, s.sums[2:3, :])

    def column_sums(ref, count, row):
        s.sums[...] = jnp.zeros_like(s.sums)

        def block(i):
            p = rows_at(i * 64, 64, 64)
            s.sums[0:1, :] += jnp.sum(ref[p, :].astype(F32), axis=0, keepdims=True)

        loop(count // 64, block)
        put(row, s.sums[0:1, :])

    pending = []

    def flush():
        if pending:
            pending.pop().wait()

    def store_grad(chunk, left, right):
        count = left.shape[0]
        flush()

        def block(i):
            product = dot_tn(left[:, rows_at(i * 256, 256, 256)], right[0:count, :]).astype(BF16)
            s.stage[0, i] = product[:128]
            s.stage[1, i] = product[128:]

        loop(4, block)
        pending.append(pltpu.make_async_copy(s.stage, parts.at[pl.ds(chunk, 2)], s.grad_sem.at[0]))
        pending[-1].start()

    load("sum3").wait()
    load("cot").wait()
    norm_back(s.sum3, 2, True, 16)
    load("h2").wait()

    def down_save(j):
        return pltpu.make_async_copy(s.stage.at[0], parts.at[2 * j], s.grad_sem.at[0])

    def up_save(j):
        return pltpu.make_async_copy(s.stage.at[1], parts.at[2 * j + 1], s.grad_sem.at[1])

    def tile(j):
        slot = lax.rem(j, 2)
        for copy in tile_copies(j, slot):
            copy.wait()

        @pl.when(j < 7)
        def _():
            for copy in tile_copies(j + 1, 1 - slot):
                copy.start()

        def down(i):
            product = dot_tn(s.gt[slot, :, rows_at(i * 256, 256, 256)], s.low[...]).astype(BF16)
            s.stage[0, 2 * i] = product[:128]
            s.stage[0, 2 * i + 1] = product[128:]

        loop(2, down)
        down_save(j).start()

        def hidden(i):
            p = rows_at(i * 256, 256, 256)
            grad = dot_nt(s.low[...], s.wd[slot, p, :])
            rounded = (grad * s.ut[slot, :, p]).astype(BF16)
            s.dut[:, p] = rounded
            s.ub[j, :, p] = jnp.sum(rounded.astype(F32), axis=0, keepdims=True)

        loop(2, hidden)
        down_save(j).wait()

        @pl.when(lax.rem(j, 2) == 0)
        def _():
            reducer.tick(3 * j // 2)


        def up(i):
            product = dot_tn(s.h2[:, rows_at(i * 256, 256, 256)], s.dut[...]).astype(BF16)
            s.stage[1, i, :, 0:512] = product[:128]
            s.stage[1, i, :, 512:1024] = product[128:]

        loop(4, up)
        up_save(j).start()

        def back(i):
            p = rows_at(i * 256, 256, 256)
            s.dz[:, p] += dot_nt(s.dut[...], s.wu[slot, p, :])

        loop(4, back)
        up_save(j).wait()
        reducer.tick((3 * j + 2) // 2)

    loop(8, tile)
    for j in range(8):
        for i in range(4):
            s.small[i, 12 + j // 2:13 + j // 2, (j % 2) * 128:(j % 2) * 128 + 128] = s.ub[j, :, i * 128:(i + 1) * 128]
    load("sum2").wait()
    norm_back(s.sum2, 1, False, 5)
    reducer.tick(12)
    load("o2").wait()
    store_grad(16, s.o2, s.low)

    def times_weight(dst, left, count, slot):
        def block(i):
            p = rows_at(i * 256, 256, 256)
            dst[:, p] = dot_nt(left[...], s.wb[slot, p, :]).astype(BF16)

        loop(count, block)

    def add_weight(left, slot):
        def block(i):
            p = rows_at(i * 256, 256, 256)
            s.dz[:, p] += dot_nt(left[...], s.wb[slot, p, :])

        loop(4, block)

    weight(0).wait()
    times_weight(s.dob, s.low, 4, 0)
    weight(2).start()
    flush()
    reducer.tick(13)
    for name in ("q2", "k2", "v2"):
        load(name).wait()

    lane = lax.broadcasted_iota(jnp.int32, (1, 128), 1)
    head_masks = [(lane < 64).astype(F32).astype(BF16), (lane >= 64).astype(F32).astype(BF16)]

    def attention_pair(i, q_ref, k_ref, v_ref, key_count, causal):
        lanes = rows_at(i * 128, 128, 128)
        s.dka[...] = jnp.zeros_like(s.dka)
        s.dva[...] = jnp.zeros_like(s.dva)
        for block in (0, 1):
            rows = pl.ds(block * 256, 256)
            reach = (block + 1) * 256 if causal else key_count
            query, grad = q_ref[rows, lanes], s.dob[rows, lanes]
            key, value = k_ref[0:reach, lanes], v_ref[0:reach, lanes]
            query_grad = jnp.zeros((256, 128), F32)
            for mask in head_masks:
                query_one, grad_one = query * mask, grad * mask
                scores = dot_nt(key, query_one) * 0.125
                if causal:
                    key_at = lax.broadcasted_iota(jnp.int32, (reach, 256), 0)
                    query_at = lax.broadcasted_iota(jnp.int32, (reach, 256), 1) + block * 256
                    scores = jnp.where(key_at <= query_at, scores, -1e30)
                peak = jnp.max(scores, axis=0, keepdims=True)
                full = jnp.exp(scores - peak)
                full = full * (1.0 / jnp.sum(full, axis=0, keepdims=True))
                full_grad = dot_nt(value, grad_one)
                row_dot = jnp.sum(full * full_grad, axis=0, keepdims=True)
                score_grad = (full * (full_grad - row_dot)).astype(BF16)
                s.dva[0:reach, :] += dot_nn(full.astype(BF16), grad_one)
                s.dka[0:reach, :] += dot_nn(score_grad, query_one)
                query_grad = query_grad + dot_tn(score_grad, key * mask)
            s.dqb[rows, lanes] = (query_grad * 0.125).astype(BF16)
        s.dkb[0:key_count, lanes] = (s.dka[0:key_count, :] * 0.125).astype(BF16)
        s.dvb[0:key_count, lanes] = s.dva[0:key_count, :].astype(BF16)

    def cross(i):
        attention_pair(i, s.q2, s.k2, s.v2, 256, False)

        @pl.when((lax.rem(i, 2) == 1) & (i < 7))
        def _():
            reducer.tick(14 + i // 2)

    loop(8, cross)
    load("h1").wait()
    load("e1").wait()
    store_grad(18, s.h1, s.dqb)
    reducer.tick(17)
    store_grad(20, s.e1, s.dkb)
    reducer.tick(18)
    store_grad(22, s.e1, s.dvb)
    reducer.tick(19)
    column_sums(s.dqb, 512, 3)
    column_sums(s.dvb, 256, 4)
    weight(1).wait()
    weight(2).wait()

    def enc_block(i):
        p = rows_at(i * 256, 256, 256)
        grad_enc[:, p] = (
            dot_nt(s.dkb[0:256, :], s.wb[1, p, :]) + dot_nt(s.dvb[0:256, :], s.wb[0, p, :])
        ).astype(BF16)

    loop(4, enc_block)
    flush()
    reducer.tick(20)
    weight(3).start()
    weight(4).start()
    weight(3).wait()
    add_weight(s.dqb, 1)
    weight(5).start()
    reducer.tick(21)
    load("sum1").wait()
    norm_back(s.sum1, 0, False, 2)
    load("o1").wait()
    store_grad(24, s.o1, s.low)
    reducer.tick(22)
    weight(4).wait()
    times_weight(s.dob, s.low, 4, 0)
    weight(6).start()
    flush()
    reducer.tick(23)
    for name in ("q1", "k1", "v1"):
        load(name).wait()

    def own(i):
        attention_pair(i, s.q1, s.k1, s.v1, 512, True)

        @pl.when(lax.rem(i, 3) == 2)
        def _():
            reducer.tick(24 + i // 3)

    loop(8, own)
    load("x1").wait()
    store_grad(26, s.x1, s.dqb)
    store_grad(28, s.x1, s.dkb)
    reducer.tick(26)
    store_grad(30, s.x1, s.dvb)
    reducer.tick(27)
    column_sums(s.dqb, 512, 0)
    column_sums(s.dvb, 512, 1)
    flush()
    reducer.tick(28)
    weight(5).wait()
    add_weight(s.dqb, 1)
    weight(7).start()
    reducer.tick(29)
    weight(6).wait()
    add_weight(s.dkb, 0)
    reducer.tick(30)
    weight(7).wait()

    def last(i):
        p = rows_at(i * 256, 256, 256)
        s.low[:, p] = (s.dz[:, p] + dot_nt(s.dvb[...], s.wb[1, p, :])).astype(BF16)

    loop(4, last)
    def drain(i):
        reducer.tick(31 + i)

        @pl.when(i == LAGS[1])
        def _():
            for copy in row_copies(1, s.low, grad_back):
                copy.start()

        reducer.small_steps(i)

    loop(max(9, CHUNKS + LAGS[-1] - 31), drain)
    for copy in row_copies(0, out_rows, out_back) + row_copies(1, s.low, grad_back):
        copy.wait()


def backward(loads, *rest):
    any_space = pl.BlockSpec(memory_space=pl.ANY)
    in_vmem = pl.BlockSpec(memory_space=pltpu.VMEM)
    return pl.pallas_call(
        back_kernel,
        out_shape=(
            jax.ShapeDtypeStruct((CHUNKS, ROWS, 1024), BF16),
            jax.ShapeDtypeStruct((24, 256), F32),
            jax.ShapeDtypeStruct((256, 1024), BF16),
            jax.ShapeDtypeStruct((4, 128, 1024), BF16),
            jax.ShapeDtypeStruct((4, 128, 1024), BF16),
            jax.ShapeDtypeStruct((CHUNKS, 4, ROWS, 1024), BF16),
        ),
        in_specs=[any_space] * 22 + [in_vmem] * 3,
        out_specs=(any_space, in_vmem, in_vmem, any_space, any_space, any_space),
        scratch_shapes=list(BACK_SCRATCH.values()),
        compiler_params=pltpu.CompilerParams(
            collective_id=1, has_side_effects=True, vmem_limit_bytes=62 << 20
        ),
    )(*[loads[name] for name in BACK_LOADS], *rest)


FORWARD_SCRATCH = dict(
    v_in=pltpu.VMEM((6, 1024, 1024), BF16),
    v_out=pltpu.VMEM((2, 1024, 1024), BF16),
    v_up=pltpu.VMEM((1024, 4096), BF16),
    v_down=pltpu.VMEM((4096, 1024), BF16),
    small=pltpu.VMEM((24, 256), F32),
    s_tok=pltpu.VMEM((4, 128, 1024), BF16),
    v_small=pltpu.VMEM((4, 24, 256), F32),
    vec=pltpu.VMEM((24, 1024), F32),
    x=pltpu.VMEM((512, 1024), BF16),
    e=pltpu.VMEM((256, 1024), BF16),
    q=pltpu.VMEM((512, 1024), BF16),
    k=pltpu.VMEM((512, 1024), BF16),
    v=pltpu.VMEM((512, 1024), BF16),
    o=pltpu.VMEM((512, 1024), BF16),
    h1=pltpu.VMEM((512, 1024), BF16),
    q2=pltpu.VMEM((512, 1024), BF16),
    k2=pltpu.VMEM((256, 1024), BF16),
    v2=pltpu.VMEM((256, 1024), BF16),
    o2=pltpu.VMEM((512, 1024), BF16),
    h2=pltpu.VMEM((512, 1024), BF16),
    y=pltpu.VMEM((512, 1024), BF16),
    hf=pltpu.VMEM((512, 1024), F32),
    sum_a=pltpu.VMEM((512, 1024), F32),
    sum_b=pltpu.VMEM((512, 1024), F32),
    ublock=pltpu.VMEM((512, 512), F32),
    gblock=pltpu.VMEM((2, 512, 512), BF16),
    dblock=pltpu.VMEM((2, 512, 512), F32),
    own_sem=pltpu.SemaphoreType.DMA((16, 4)),
    x_send=pltpu.SemaphoreType.DMA((16, 4)),
    x_recv=pltpu.SemaphoreType.DMA((16, 4)),
    y_send=pltpu.SemaphoreType.DMA((16, 2, 4)),
    y_recv=pltpu.SemaphoreType.DMA((16, 2, 4)),
    z_send=pltpu.SemaphoreType.DMA((16, 2, 4)),
    z_recv=pltpu.SemaphoreType.DMA((16, 2, 4)),
    c_send=pltpu.SemaphoreType.DMA((16, 2, 4)),
    c_recv=pltpu.SemaphoreType.DMA((16, 2, 4)),
    t_send=pltpu.SemaphoreType.DMA((3, 3)),
    t_recv=pltpu.SemaphoreType.DMA((3, 3)),
    t_own=pltpu.SemaphoreType.DMA((4,)),
    save_sem=pltpu.SemaphoreType.DMA((16,)),
    weight_sem=pltpu.SemaphoreType.DMA((16,)),
    late_sem=pltpu.SemaphoreType.DMA((8, 4)),
    block_sem=pltpu.SemaphoreType.DMA((2, 4)),
)
SAVED = ("x", "q", "k", "v", "o", "h1", "q2", "k2", "v2", "o2", "h2", "sum1", "sum2", "sum3", "y")
GATHER_ORDER = (0, 1, 2, 6, 4, 5, 3, 7, 8, 12, 9, 13, 10, 14, 11, 15)
AHEAD, HOPS = 3, (1, 2, 3)


def weight_views(refs, k, shard, start, size):
    if k < 6:
        return [refs[0].at[k, rows_at(shard * 256 + start, size, 8), :]]
    if k < 8:
        return [refs[1].at[k - 6, rows_at(shard * 256 + start, size, 8), :]]
    if k < 12:
        rows = rows_at(shard * 256 + start, size, 8)
        return [refs[2].at[rows, pl.ds(i * 1024 + (k - 8) * 256, 256)] for i in range(4)]
    return [refs[3].at[rows_at(shard * 1024 + (k - 12) * 256 + start, size, 8), :]]


class Gatherer:
    def __init__(self, s, shards, full):
        self.s, self.shards, self.full, self.done = s, shards, full, -AHEAD - 1
        z, y, x, c = self.at = place()
        self.side = lax.rem(z, 2)
        self.core = device(z, y, x, 1 - c)
        self.xmate = device(z, y, 1 - x, c)
        self.diag = device(z, y, 1 - x, 1 - c)
        self.ymate = device(z, 1 - y, x, c)
        self.zmate = device(z + 1 - 2 * self.side, y, x, c)
        self.mine, self.other = x * 2 + c, (1 - x) * 2 + c

    def greet(self):
        greet([self.core, self.xmate, self.diag, self.ymate, self.zmate])

    def send(self, k, sources, target_shard, start, size, send, recv, peer):
        targets = weight_views(self.full, k, target_shard, start, size)
        return [
            remote(src, dst, send.at[i], recv.at[i], peer)
            for i, (src, dst) in enumerate(zip(sources, targets))
        ]

    def x_copy(self, k):
        q = (self.at[1] * 2 + self.side) * 64
        return self.send(
            k, weight_views(self.shards, k, 0, q, 64), self.mine, q, 64,
            self.s.x_send.at[k], self.s.x_recv.at[k], self.xmate,
        )

    def core_copy(self, k):
        return self.send(
            k, weight_views(self.shards, k, 0, 0, 256), self.mine, 0, 256,
            self.s.c_send.at[k, 0], self.s.c_recv.at[k, 0], self.core,
        )

    def own_copy(self, k):
        pairs = zip(weight_views(self.shards, k, 0, 0, 256), weight_views(self.full, k, self.mine, 0, 256))
        return [
            pltpu.make_async_copy(src, dst, self.s.own_sem.at[k, i]) for i, (src, dst) in enumerate(pairs)
        ]

    def relay(self, k, start, size, send, recv, peer):
        return self.send(k, weight_views(self.full, k, self.other, start, size), self.other, start, size, send, recv, peer)

    def first_hops(self, k):
        s, q = self.s, (self.at[1] * 2 + self.side) * 64
        return self.relay(k, q, 64, s.y_send.at[k, 0], s.y_recv.at[k, 0], self.ymate) + self.relay(
            k, q, 64, s.z_send.at[k, 0], s.z_recv.at[k, 0], self.zmate
        )

    def second_hops(self, k):
        s, y = self.s, self.at[1]
        return self.relay(
            k, (y * 2 + 1 - self.side) * 64, 32, s.y_send.at[k, 1], s.y_recv.at[k, 1], self.ymate
        ) + self.relay(
            k, ((1 - y) * 2 + self.side) * 64 + 32, 32, s.z_send.at[k, 1], s.z_recv.at[k, 1], self.zmate
        )

    def last_hop(self, k):
        return self.relay(k, 0, 256, self.s.c_send.at[k, 1], self.s.c_recv.at[k, 1], self.core)

    def step(self, t):
        def chunk(lag):
            return GATHER_ORDER[t - lag] if 0 <= t - lag < 16 else None

        def start(copies):
            for copy in copies:
                copy.start()

        def wait(copies):
            for copy in copies:
                copy.wait()

        if (k := chunk(-AHEAD)) is not None:
            start(self.x_copy(k) + self.core_copy(k) + self.own_copy(k))
        if (k := chunk(0)) is not None:
            wait(self.x_copy(k))
            start(self.first_hops(k))
        if (k := chunk(HOPS[0])) is not None:
            wait(self.first_hops(k))
            start(self.second_hops(k))
        if (k := chunk(HOPS[1])) is not None:
            wait(self.second_hops(k))
            start(self.last_hop(k))
        if (k := chunk(HOPS[2])) is not None:
            wait(self.last_hop(k) + self.core_copy(k) + self.own_copy(k))

    def advance(self, t):
        while self.done < t:
            self.done += 1
            self.step(self.done)

    def ready(self, index):
        self.advance(index + HOPS[2])


def forward_kernel(*refs):
    owner, lengths, bias, gain_in, shift_in, up_bias, down_bias, tok_in, cot_in = refs[:9]
    w_in, w_out, w_up, w_down, enc = refs[9:14]
    f_in, f_out, f_up, f_down, f_cot, gains, mask, g_all, d_all = refs[14:23]
    saved = dict(zip(SAVED, refs[23:38]))
    s = types.SimpleNamespace(**dict(zip(FORWARD_SCRATCH, refs[38:])))
    sequence_at = [
        jnp.clip(sum(jnp.where(owner[0, j] == i, j, 0) for j in range(4)), 0, 3) for i in range(4)
    ]
    small, tok = s.small, s.s_tok
    full = (s.v_in, s.v_out, s.v_up, s.v_down)
    gather = Gatherer(s, (w_in, w_out, w_up, w_down), full)
    mine, (_, _, x, c) = gather.mine, gather.at
    peers = ((gather.core, x * 2 + 1 - c), (gather.xmate, gather.other), (gather.diag, (1 - x) * 2 + 1 - c))

    def rows_of(index):
        return rows_at(index * 128, 128, 128)

    def arrange(source, target):
        for i in range(4):
            def block(n, i=i):
                p = rows_at(n * 32, 32, 32)
                target[i, p, :] = source[sequence_at[i], p, :]

            loop(4, block)

    def token_copies():
        return [
            remote(tok.at[slot], s.x.at[rows_of(mine), :], s.t_send.at[0, i], s.t_recv.at[0, i], peer)
            for i, (peer, slot) in enumerate(peers)
        ] + [
            remote(small, s.v_small.at[mine], s.t_send.at[2, i], s.t_recv.at[2, i], peer)
            for i, (peer, slot) in enumerate(peers)
        ] + [
            pltpu.make_async_copy(tok.at[mine], s.x.at[rows_of(mine), :], s.t_own.at[0]),
            pltpu.make_async_copy(small, s.v_small.at[mine], s.t_own.at[1]),
        ]

    def cot_copies():
        return [
            remote(tok.at[slot], f_cot.at[mine], s.t_send.at[1, i], s.t_recv.at[1, i], peer)
            for i, (peer, slot) in enumerate(peers)
        ] + [pltpu.make_async_copy(tok.at[mine], f_cot.at[mine], s.t_own.at[2])]

    enc_copy = pltpu.make_async_copy(enc, s.e, s.t_own.at[3])
    enc_copy.start()
    arrange(tok_in, s.s_tok)
    small[...] = jnp.zeros_like(small)
    small[0:6, :] = bias[...].astype(F32)
    small[6:9, :] = gain_in[...].astype(F32)
    small[9:12, :] = shift_in[...].astype(F32)
    for i in range(4):
        small[12 + i:13 + i, :] = up_bias[:, i * 256:(i + 1) * 256].astype(F32)
    small[16:17, :] = down_bias[...].astype(F32)
    gather.greet()
    gather.advance(1 - AHEAD)
    for copy in token_copies():
        copy.start()

    def save(name, ref):
        return pltpu.make_async_copy(ref, saved[name], s.save_sem.at[SAVED.index(name)])

    def weight_saves(k):
        if k < 6:
            return [pltpu.make_async_copy(s.v_in.at[k], f_in.at[k], s.weight_sem.at[k])]
        if k < 8:
            return [pltpu.make_async_copy(s.v_out.at[k - 6], f_out.at[k - 6], s.weight_sem.at[k])]
        if k == 11:
            return [pltpu.make_async_copy(s.v_up, f_up, s.weight_sem.at[k])]
        return [
            pltpu.make_async_copy(src, dst, s.late_sem.at[k - 8, i])
            for i, (src, dst) in enumerate(zip(late_views(full, k), late_views((f_in, f_out, f_up, f_down), k)))
        ] if k > 11 else []

    def late_views(refs, k):
        return [view for shard in range(4) for view in weight_views(refs, k, shard, 0, 256)]

    def ready(index):
        gather.ready(index)
        for copy in weight_saves(GATHER_ORDER[index]):
            copy.start()

    def project(dst, left, weight, count, bias):
        def block(i):
            columns = rows_at(i * 256, 256, 256)
            product = dot_nn(left[0:count, :], weight[:, columns])
            if bias is not None:
                product = product + s.vec[bias:bias + 1, columns]
            dst[0:count, columns] = product.astype(BF16)

        loop(4, block)

    def join(dst, base, left, weight, bias):
        def block(i):
            columns = rows_at(i * 256, 256, 256)
            dst[:, columns] = base[:, columns].astype(F32) + (
                dot_nn(left[...], weight[:, columns]) + s.vec[bias:bias + 1, columns]
            )

        loop(4, block)

    def normalize(sum_ref, index, low, last):
        gain, shift = s.vec[6 + index:7 + index, :], s.vec[9 + index:10 + index, :]

        def block(i):
            p = rows_at(i * 32, 32, 32)
            value = sum_ref[p, :]
            center = value - jnp.mean(value, axis=1, keepdims=True)
            scale = lax.rsqrt(jnp.mean(center * center, axis=1, keepdims=True) + epsilon)
            result = center * scale * gain + shift
            if last:
                low[p, :] = (result * mask[p, 0:1]).astype(BF16)
            else:
                s.hf[p, :] = result
                low[p, :] = result.astype(BF16)

        loop(16, block)

    lane = lax.broadcasted_iota(jnp.int32, (1, 128), 1)
    head_masks = [(lane < 64).astype(F32).astype(BF16), (lane >= 64).astype(F32).astype(BF16)]

    def attend_pair(i, q_ref, k_ref, v_ref, o_ref, key_count, causal):
        lanes = rows_at(i * 128, 128, 128)
        for block in (0, 1):
            rows = pl.ds(block * 256, 256)
            reach = (block + 1) * 256 if causal else key_count
            query = q_ref[rows, lanes]
            key, value = k_ref[0:reach, lanes], v_ref[0:reach, lanes]
            context = jnp.zeros((256, 128), F32)
            for head_mask in head_masks:
                scores = dot_nt(query * head_mask, key) * 0.125
                if causal:
                    query_at = lax.broadcasted_iota(jnp.int32, (256, reach), 0) + block * 256
                    key_at = lax.broadcasted_iota(jnp.int32, (256, reach), 1)
                    scores = jnp.where(key_at <= query_at, scores, -1e30)
                weights = jnp.exp(scores - jnp.max(scores, axis=1, keepdims=True))
                weights = weights * (1.0 / jnp.sum(weights, axis=1, keepdims=True))
                context = context + dot_nn(weights.astype(BF16), value * head_mask)
            o_ref[rows, lanes] = context.astype(BF16)

    length = jnp.int32(0)
    for i in range(4):
        here = sum(jnp.where(sequence_at[i] == j, lengths[0, j], 0) for j in range(4))
        length = length + jnp.where(mine == i, here, 0)
    mask[...] = (lax.broadcasted_iota(jnp.int32, (512, 128), 0) < length).astype(F32)
    ready(0)
    for copy in token_copies():
        copy.wait()
    for i in range(4):
        s.vec[:, i * 256:(i + 1) * 256] = s.v_small[i]
    gains[...] = s.vec[0:16, :]
    save("x", s.x).start()
    project(s.q, s.x, s.v_in.at[0], 512, 0)
    save("q", s.q).start()
    ready(1)
    project(s.k, s.x, s.v_in.at[1], 512, None)
    save("k", s.k).start()
    ready(2)
    project(s.v, s.x, s.v_in.at[2], 512, 1)
    save("v", s.v).start()
    for part in range(4):
        loop(2, lambda i, part=part: attend_pair(part * 2 + i, s.q, s.k, s.v, s.o, 512, True))
        gather.advance(HOPS[2] + 3 + part // 2)
    save("o", s.o).start()
    ready(3)
    join(s.sum_a, s.x, s.o, s.v_out.at[0], 2)
    save("sum1", s.sum_a).start()
    ready(4)
    normalize(s.sum_a, 0, s.h1, False)
    save("h1", s.h1).start()
    enc_copy.wait()
    project(s.k2, s.e, s.v_in.at[4], 256, None)
    save("k2", s.k2).start()
    ready(5)
    project(s.v2, s.e, s.v_in.at[5], 256, 4)
    save("v2", s.v2).start()
    ready(6)
    project(s.q2, s.h1, s.v_in.at[3], 512, 3)
    save("q2", s.q2).start()
    ready(7)
    for part in range(4):
        loop(2, lambda i, part=part: attend_pair(part * 2 + i, s.q2, s.k2, s.v2, s.o2, 256, False))
        gather.advance(HOPS[2] + 8 + part // 2)
    save("o2", s.o2).start()
    join(s.sum_b, s.hf, s.o2, s.v_out.at[1], 5)
    save("sum2", s.sum_b).start()
    gather.advance(HOPS[2] + 9)
    normalize(s.sum_b, 1, s.h2, False)
    save("h2", s.h2).start()
    arrange(cot_in, s.s_tok)
    for copy in cot_copies():
        copy.start()
    save("sum1", s.sum_a).wait()

    def widen(i):
        p = rows_at(i * 64, 64, 64)
        s.sum_a[p, :] = s.hf[p, :] + s.vec[16:17, :]

    loop(8, widen)

    def nudge():
        gather.advance(min(gather.done + 1, 15 + HOPS[2]))

    def block_copies(j, pair):
        copies = []
        for h in (0, 1):
            columns = rows_at((2 * pair + h) * 1024 + j * 256, 256, 256)
            part = pl.ds(h * 256, 256)
            copies += [
                pltpu.make_async_copy(s.gblock.at[pair, :, part], g_all.at[:, columns], s.block_sem.at[pair, h]),
                pltpu.make_async_copy(s.dblock.at[pair, :, part], d_all.at[:, columns], s.block_sem.at[pair, 2 + h]),
            ]
        return copies

    for j in range(4):
        ready(8 + 2 * j)
        ready(9 + 2 * j)

        def mlp(pair, j=j):
            if j > 0:
                for copy in block_copies(j, pair):
                    copy.wait()
            starts = [(2 * pair + h) * 1024 + j * 256 for h in (0, 1)]
            for h in (0, 1):
                s.ublock[:, h * 256:(h + 1) * 256] = (
                    dot_nn(s.h2[...], s.v_up[:, rows_at(starts[h], 256, 256)])
                    + s.v_small[2 * pair + h, 12 + j:13 + j, :]
                )

            def hidden(r):
                p = rows_at(r * 64, 64, 64)
                value = s.ublock[p, :]
                cdf = normal_cdf(value)
                pdf = jnp.exp(-0.5 * value * value) * 0.3989422804014327
                s.gblock[pair, p, :] = (value * cdf).astype(BF16)
                s.dblock[pair, p, :] = cdf + value * pdf

            nudge()
            loop(8, hidden)
            for copy in block_copies(j, pair):
                copy.start()

            def out(n):
                wide = rows_at(n * 256, 256, 256)
                s.sum_a[:, wide] += dot_nn(
                    s.gblock[pair, :, 0:256], s.v_down[rows_at(starts[0], 256, 256), wide]
                ) + dot_nn(s.gblock[pair, :, 256:512], s.v_down[rows_at(starts[1], 256, 256), wide])

            loop(4, out)

        for pair in (0, 1):
            mlp(pair)

    save("sum3", s.sum_a).start()
    normalize(s.sum_a, 2, s.y, True)
    save("y", s.y).start()
    for copy in block_copies(3, 0) + block_copies(3, 1) + cot_copies():
        copy.wait()
    for k in range(16):
        for copy in weight_saves(k):
            copy.wait()
    ends = dict(
        x=s.x, q=s.q, k=s.k, v=s.v, o=s.o, h1=s.h1, q2=s.q2, k2=s.k2, v2=s.v2, o2=s.o2, h2=s.h2,
        sum2=s.sum_b, sum3=s.sum_a, y=s.y,
    )
    for name, ref in ends.items():
        save(name, ref).wait()


def forward(*operands):
    any_space = pl.BlockSpec(memory_space=pl.ANY)
    in_vmem = pl.BlockSpec(memory_space=pltpu.VMEM)
    in_smem = pl.BlockSpec(memory_space=pltpu.SMEM)
    wide = {"sum1", "sum2", "sum3"}
    return pl.pallas_call(
        forward_kernel,
        out_shape=(
            jax.ShapeDtypeStruct((6, 1024, 1024), BF16),
            jax.ShapeDtypeStruct((2, 1024, 1024), BF16),
            jax.ShapeDtypeStruct((1024, 4096), BF16),
            jax.ShapeDtypeStruct((4096, 1024), BF16),
            jax.ShapeDtypeStruct((4, 128, 1024), BF16),
            jax.ShapeDtypeStruct((16, 1024), F32),
            jax.ShapeDtypeStruct((512, 128), F32),
            jax.ShapeDtypeStruct((512, 4096), BF16),
            jax.ShapeDtypeStruct((512, 4096), F32),
        ) + tuple(
            jax.ShapeDtypeStruct((256 if name in ("k2", "v2") else 512, 1024), F32 if name in wide else BF16)
            for name in SAVED
        ),
        in_specs=[in_smem] * 2 + [in_vmem] * 7 + [any_space] * 5,
        out_specs=(any_space,) * 5 + (in_vmem,) * 2 + (any_space,) * 17,
        scratch_shapes=list(FORWARD_SCRATCH.values()),
        compiler_params=pltpu.CompilerParams(
            collective_id=2, has_side_effects=True, vmem_limit_bytes=62 << 20
        ),
    )(*operands)


def sum_plain(*parts):
    dims = (1, 1, 1, 1, 1, 0, 0, 0, 0)
    scattered = [
        lax.psum_scatter(part.astype(jnp.bfloat16), "shard", scatter_dimension=dim, tiled=True)
        for part, dim in zip(parts, dims)
    ]
    return tuple(lax.psum(part, "rep").astype(jnp.float32) for part in scattered)


def finish_kernel(owner, total, small_total, out_back, grad_back, *refs):
    out, grad_tok, g_in, g_out, g_up, g_down, g_bias, g_gain, g_shift, g_up_bias, g_down_bias, w_in, w_out, w_up, w_down, sem, row_sem = refs
    copies = []
    for i in range(4):
        for j, (src, dst) in enumerate(((out_back, out), (grad_back, grad_tok))):
            copies.append(pltpu.make_async_copy(src.at[jnp.clip(owner[0, i], 0, 3)], dst.at[i], row_sem.at[i, j]))
            copies[-1].start()
    g_bias[...] = small_total[0:6, :]
    g_gain[...] = small_total[6:9, :]
    g_shift[...] = small_total[9:12, :]
    for i in range(4):
        g_up_bias[:, i * 256:(i + 1) * 256] = small_total[12 + i:13 + i, :]
    g_down_bias[...] = small_total[16:17, :]

    def widen(k, dst):
        def block(i):
            p = rows_at(i * 32, 32, 32)
            dst(p, total[k, p, :].astype(F32))

        loop(4, block)

    def send(src, dst, index):
        copies.append(pltpu.make_async_copy(src, dst, sem.at[index]))
        copies[-1].start()

    for j in range(8):
        def up(p, value):
            for half in (0, 1):
                rows = rows_at(p.start + half * 128, 32, 32)
                for c in range(4):
                    w_up[rows, c * 1024 + j * 128:c * 1024 + j * 128 + 128] = (
                        value[:, half * 512 + c * 128:half * 512 + c * 128 + 128]
                    )

        widen(2 * j + 1, up)
        rows = pl.ds(j * 128, 128)

        def down(p, value):
            w_down[rows_at(j * 128 + p.start, 32, 32), :] = value

        widen(2 * j, down)
        send(w_down.at[rows, :], g_down.at[rows, :], j)
    send(w_up, g_up, 8)
    order = [(g_out, w_out, 1, 16), (g_in, w_in, 3, 18), (g_in, w_in, 4, 20), (g_in, w_in, 5, 22),
             (g_out, w_out, 0, 24), (g_in, w_in, 0, 26), (g_in, w_in, 1, 28), (g_in, w_in, 2, 30)]
    for n, (dst, held, index, chunk) in enumerate(order):
        for half in (0, 1):
            def place_rows(p, value):
                held[index, rows_at(half * 128 + p.start, 32, 32), :] = value

            widen(chunk + half, place_rows)
        send(held.at[index], dst.at[index], 9 + n)
    for copy in copies:
        copy.wait()


def finish(owner, total, small_total, out_back, grad_back):
    any_space = pl.BlockSpec(memory_space=pl.ANY)
    in_vmem = pl.BlockSpec(memory_space=pltpu.VMEM)
    narrow = [(6, 256), (3, 256), (3, 256), (1, 1024), (1, 256)]
    wide = [(6, 256, 1024), (2, 256, 1024), (256, 4096), (1024, 1024)]
    return pl.pallas_call(
        finish_kernel,
        out_shape=tuple(
            [jax.ShapeDtypeStruct((4, 128, 1024), BF16)] * 2
            + [jax.ShapeDtypeStruct(shape, F32) for shape in wide]
            + [jax.ShapeDtypeStruct(shape, F32) for shape in narrow]
        ),
        in_specs=[pl.BlockSpec(memory_space=pltpu.SMEM)] + [in_vmem] * 4,
        out_specs=tuple([any_space] * 6 + [in_vmem] * 5),
        scratch_shapes=[pltpu.VMEM(shape, F32) for shape in wide]
        + [pltpu.SemaphoreType.DMA((17,)), pltpu.SemaphoreType.DMA((4, 2))],
        compiler_params=pltpu.CompilerParams(vmem_limit_bytes=60 << 20),
    )(owner, total, small_total, out_back, grad_back)


def fast_layer(
    tokens, enc_states, cotangent, lengths, owner, attn_in, attn_out, attn_bias,
    norm_gain, norm_bias, mlp_in, mlp_bias_in, mlp_out, mlp_bias_out,
):
    encoder = enc_states[0]
    full_in, full_out, up_full, down_full, cot, vectors, mask, g_all, d_all, *saved = forward(
        owner, lengths, attn_bias, norm_gain, norm_bias, mlp_bias_in.reshape(1, 1024),
        mlp_bias_out.reshape(1, 256), tokens, cotangent, attn_in, attn_out, mlp_in, mlp_out, encoder,
    )
    saved = dict(zip(SAVED, saved))
    loads = dict(
        x1=saved["x"], q1=saved["q"], k1=saved["k"], v1=saved["v"], o1=saved["o"], h1=saved["h1"],
        q2=saved["q2"], k2=saved["k2"], v2=saved["v2"], o2=saved["o2"], h2=saved["h2"], e1=encoder,
        cot=cot.reshape(512, 1024), sum1=saved["sum1"], sum2=saved["sum2"], sum3=saved["sum3"],
    )
    total, small_total, encoder_grad, back_blocks, grad_blocks, _ = backward(
        loads, d_all, g_all, full_in, full_out, up_full, down_full, vectors, saved["y"], mask
    )
    out, grad_tokens, g_in, g_out, g_up, g_down, *small = finish(
        owner, total, small_total, back_blocks, grad_blocks
    )
    return (
        out, grad_tokens, encoder_grad[None], g_in, g_out, small[0], small[1], small[2],
        g_up, small[3].reshape(1024), g_down, small[4].reshape(256),
    )


def local(
    tokens,
    enc_states,
    cotangent,
    lengths,
    owner,
    attn_in,
    attn_out,
    attn_bias,
    norm_gain,
    norm_bias,
    mlp_in,
    mlp_bias_in,
    mlp_out,
    mlp_bias_out,
):
    groups = lax.axis_size("shard")
    if (lax.axis_size("rep"), groups) == (8, 4):
        return fast_layer(
            tokens, enc_states, cotangent, lengths, owner, attn_in, attn_out, attn_bias,
            norm_gain, norm_bias, mlp_in, mlp_bias_in, mlp_out, mlp_bias_out,
        )
    my_index = lax.axis_index("shard")
    owner_row = owner[0]
    slot_ids = jnp.arange(groups, dtype=jnp.int32)
    matches = owner_row[None, :] == slot_ids[:, None]
    sequence_at = jnp.sum(jnp.where(matches, slot_ids[None, :], 0), axis=1)
    my_sequence = jnp.sum(jnp.where(slot_ids == my_index, sequence_at, 0))
    my_length = jnp.sum(jnp.where(slot_ids == my_sequence, lengths[0], 0))
    sent_tokens = pick_blocks(tokens, sequence_at)
    sent_grads = pick_blocks(cotangent, sequence_at)
    got_tokens, got_grads = (
        lax.all_to_all(sent_tokens, "shard", split_axis=0, concat_axis=1, tiled=True),
        lax.all_to_all(sent_grads, "shard", split_axis=0, concat_axis=1, tiled=True),
    )
    full_in, full_out, full_bias, full_gain, full_shift = (
        lax.all_gather(attn_in, "shard", axis=1, tiled=True),
        lax.all_gather(attn_out, "shard", axis=1, tiled=True),
        lax.all_gather(attn_bias, "shard", axis=1, tiled=True),
        lax.all_gather(norm_gain, "shard", axis=1, tiled=True),
        lax.all_gather(norm_bias, "shard", axis=1, tiled=True),
    )
    bias_rows = full_bias.astype(jnp.float32)
    gain_rows = full_gain.astype(jnp.float32)
    shift_rows = full_shift.astype(jnp.float32)
    up_full, up_bias, down_full, down_bias = (
        lax.all_gather(mlp_in, "shard", axis=0, tiled=True),
        lax.all_gather(mlp_bias_in, "shard", axis=0, tiled=True),
        lax.all_gather(mlp_out, "shard", axis=0, tiled=True),
        lax.all_gather(mlp_bias_out, "shard", axis=0, tiled=True),
    )
    in_back, out_back, up_back, down_back = full_in, full_out, up_full, down_full
    inputs = got_tokens[0]
    row_count = inputs.shape[0]
    row_mask = (jnp.arange(row_count, dtype=jnp.int32) < my_length).astype(jnp.float32)[:, None]
    encoder = enc_states[0]
    projected = jnp.einsum("rd,wde->wre", inputs, full_in[:3], preferred_element_type=jnp.float32)
    queries = (projected[0] + bias_rows[0]).astype(jnp.bfloat16)
    keys = projected[1].astype(jnp.bfloat16)
    values = (projected[2] + bias_rows[1]).astype(jnp.bfloat16)
    context, log_totals = attention_forward(queries, keys, values, True)
    first_sum = inputs.astype(jnp.float32) + (matmul(context, full_out[0]) + bias_rows[2])
    first_norm = layer_norm(first_sum, gain_rows[0], shift_rows[0])
    first_low = first_norm.astype(jnp.bfloat16)
    cross_queries = (matmul(first_low, full_in[3]) + bias_rows[3]).astype(jnp.bfloat16)
    cross_projected = jnp.einsum(
        "rd,wde->wre", encoder, full_in[4:6], preferred_element_type=jnp.float32
    )
    cross_keys = cross_projected[0].astype(jnp.bfloat16)
    cross_values = (cross_projected[1] + bias_rows[4]).astype(jnp.bfloat16)
    cross_context, cross_totals = attention_forward(cross_queries, cross_keys, cross_values, False)
    second_sum = first_norm + (matmul(cross_context, full_out[1]) + bias_rows[5])
    second_norm = layer_norm(second_sum, gain_rows[1], shift_rows[1])
    second_low = second_norm.astype(jnp.bfloat16)
    hidden_pre = matmul(second_low, up_full) + up_bias.astype(jnp.float32)
    hidden_low = gelu_exact(hidden_pre).astype(jnp.bfloat16)
    third_sum = second_norm + (matmul(hidden_low, down_full) + down_bias.astype(jnp.float32))
    result = (layer_norm(third_sum, gain_rows[2], shift_rows[2]) * row_mask).astype(jnp.bfloat16)
    back_blocks = lax.all_to_all(result[None], "shard", split_axis=1, concat_axis=0, tiled=True)
    output = pick_blocks(back_blocks, owner_row)
    out_grad = got_grads[0].astype(jnp.float32) * row_mask
    third_grad, third_gain_grad, third_shift_grad = jax.vjp(
        layer_norm, third_sum, gain_rows[2], shift_rows[2]
    )[1](out_grad)
    down_grad_in = third_grad.astype(jnp.bfloat16)
    grad_down = contract_rows(hidden_low, down_grad_in)
    grad_down_bias = column_sum(down_grad_in)
    hidden_grad = contract_cols(down_grad_in, down_back)
    hidden_pre_grad = jax.vjp(gelu_exact, hidden_pre)[1](hidden_grad)[0].astype(jnp.bfloat16)
    grad_up = contract_rows(second_low, hidden_pre_grad)
    grad_up_bias = column_sum(hidden_pre_grad)
    second_norm_grad = third_grad + contract_cols(hidden_pre_grad, up_back)
    second_grad, second_gain_grad, second_shift_grad = jax.vjp(
        layer_norm, second_sum, gain_rows[1], shift_rows[1]
    )[1](second_norm_grad)
    cross_out_grad = second_grad.astype(jnp.bfloat16)
    grad_cross_out = contract_rows(cross_context, cross_out_grad)
    grad_cross_out_bias = column_sum(cross_out_grad)
    cross_context_grad = contract_cols(cross_out_grad, out_back[1]).astype(jnp.bfloat16)
    cross_query_grad, cross_key_grad, cross_value_grad = attention_backward(
        cross_queries, cross_keys, cross_values, cross_totals, cross_context_grad, False
    )
    cross_query_low = cross_query_grad.astype(jnp.bfloat16)
    cross_key_low = cross_key_grad.astype(jnp.bfloat16)
    cross_value_low = cross_value_grad.astype(jnp.bfloat16)
    grad_cross_query = contract_rows(first_low, cross_query_low)
    grad_cross_query_bias = column_sum(cross_query_low)
    grad_cross_key = contract_rows(encoder, cross_key_low)
    grad_cross_value = contract_rows(encoder, cross_value_low)
    grad_cross_value_bias = column_sum(cross_value_low)
    encoder_grad = (
        contract_cols(cross_key_low, in_back[4]) + contract_cols(cross_value_low, in_back[5])
    ).astype(jnp.bfloat16)
    first_norm_grad = second_grad + contract_cols(cross_query_low, in_back[3])
    first_grad, first_gain_grad, first_shift_grad = jax.vjp(
        layer_norm, first_sum, gain_rows[0], shift_rows[0]
    )[1](first_norm_grad)
    self_out_grad = first_grad.astype(jnp.bfloat16)
    grad_self_out = contract_rows(context, self_out_grad)
    grad_self_out_bias = column_sum(self_out_grad)
    context_grad = contract_cols(self_out_grad, out_back[0]).astype(jnp.bfloat16)
    query_grad, key_grad, value_grad = attention_backward(
        queries, keys, values, log_totals, context_grad, True
    )
    query_low = query_grad.astype(jnp.bfloat16)
    key_low = key_grad.astype(jnp.bfloat16)
    value_low = value_grad.astype(jnp.bfloat16)
    grad_query = contract_rows(inputs, query_low)
    grad_query_bias = column_sum(query_low)
    grad_key = contract_rows(inputs, key_low)
    grad_value = contract_rows(inputs, value_low)
    grad_value_bias = column_sum(value_low)
    input_grad = (
        first_grad
        + contract_cols(query_low, in_back[0])
        + contract_cols(key_low, in_back[1])
        + contract_cols(value_low, in_back[2])
    ).astype(jnp.bfloat16)
    grad_blocks = lax.all_to_all(input_grad[None], "shard", split_axis=1, concat_axis=0, tiled=True)
    grad_tokens = pick_blocks(grad_blocks, owner_row)
    grad_in_full = jnp.stack(
        [grad_query, grad_key, grad_value, grad_cross_query, grad_cross_key, grad_cross_value]
    )
    grad_out_full = jnp.stack([grad_self_out, grad_cross_out])
    grad_bias_full = jnp.stack(
        [
            grad_query_bias,
            grad_value_bias,
            grad_self_out_bias,
            grad_cross_query_bias,
            grad_cross_value_bias,
            grad_cross_out_bias,
        ]
    )
    grad_gain_full = jnp.stack([first_gain_grad, second_gain_grad, third_gain_grad])
    grad_shift_full = jnp.stack([first_shift_grad, second_shift_grad, third_shift_grad])
    summed = sum_plain(
        grad_in_full, grad_out_full, grad_bias_full, grad_gain_full, grad_shift_full,
        grad_up, grad_up_bias, grad_down, grad_down_bias,
    )
    return (
        output,
        grad_tokens,
        encoder_grad[None],
        summed[0],
        summed[1],
        summed[2],
        summed[3],
        summed[4],
        summed[5],
        summed[6],
        summed[7],
        summed[8],
    )


def solution(mesh):
    placed = (
        P("rep", "shard", None),
        P(("rep", "shard"), None, None),
        P("rep", "shard", None),
        P("rep", None),
        P("rep", None),
        P(None, "shard", None),
        P(None, "shard", None),
        P(None, "shard"),
        P(None, "shard"),
        P(None, "shard"),
        P("shard", None),
        P("shard"),
        P("shard", None),
        P("shard"),
    )
    return jax.shard_map(
        local,
        mesh=mesh,
        in_specs=placed,
        out_specs=(
            P("rep", "shard", None),
            P("rep", "shard", None),
            P(("rep", "shard"), None, None),
            P(None, "shard", None),
            P(None, "shard", None),
            P(None, "shard"),
            P(None, "shard"),
            P(None, "shard"),
            P("shard", None),
            P("shard"),
            P("shard", None),
            P("shard"),
        ),
        check_vma=False,
    )
```

```python
import types

import jax
import jax.numpy as jnp
from jax import lax
from jax.experimental import pallas as pl
from jax.experimental.pallas import tpu as pltpu
from jax.sharding import PartitionSpec as P

HEADS = 16
HEAD_DIM = 64


epsilon = 1e-05


def matmul(left, right):
    return jnp.dot(left, right, preferred_element_type=jnp.float32)


def contract_rows(left, right):
    return lax.dot_general(
        left, right, (((0,), (0,)), ((), ())), preferred_element_type=jnp.float32
    )


def contract_cols(left, right):
    return lax.dot_general(
        left, right, (((1,), (1,)), ((), ())), preferred_element_type=jnp.float32
    )


def layer_norm(features, norm_scale, norm_shift):
    center = features - jnp.mean(features, axis=-1, keepdims=True)
    spread = jnp.mean(center * center, axis=-1, keepdims=True)
    return center * lax.rsqrt(spread + epsilon) * norm_scale + norm_shift


def gelu_exact(features):
    return jax.nn.gelu(features, approximate=False)


def column_sum(matrix):
    return jnp.sum(matrix.astype(jnp.float32), axis=0)


def split_heads(matrix):
    width = min(4, HEADS)
    return jnp.moveaxis(matrix.reshape(matrix.shape[0], HEADS // width, width, HEAD_DIM), 1, 0)


def merge_heads(stacked):
    return jnp.moveaxis(stacked, 0, 1).reshape(stacked.shape[1], HEADS * HEAD_DIM)


def block_scores(query_block, key_group, offset, causal):
    scores = jnp.einsum(
        "qgd,kgd->gqk", query_block, key_group, preferred_element_type=jnp.float32
    ) * HEAD_DIM ** (-0.5)
    if causal:
        query_pos = offset + jnp.arange(query_block.shape[0], dtype=jnp.int32)
        key_pos = jnp.arange(key_group.shape[0], dtype=jnp.int32)
        scores = jnp.where(key_pos[None, None, :] <= query_pos[None, :, None], scores, -jnp.inf)
    return scores


def attention_forward(queries, keys, values, causal):
    row_count = queries.shape[0]
    block_rows = min(512, row_count)
    block_count = row_count // block_rows
    offsets = jnp.arange(block_count, dtype=jnp.int32) * block_rows

    def per_group(operands):
        query_group, key_group, value_group = operands
        width = query_group.shape[1]
        query_blocks = query_group.reshape(block_count, block_rows, width, HEAD_DIM)

        def per_block(block_items):
            query_block, offset = block_items
            scores = block_scores(query_block, key_group, offset, causal)
            peak = jnp.max(scores, axis=-1, keepdims=True)
            log_total = peak + jnp.log(jnp.sum(jnp.exp(scores - peak), axis=-1, keepdims=True))
            weights_low = jnp.exp(scores - log_total).astype(jnp.bfloat16)
            context = jnp.einsum(
                "gqk,kgd->qgd", weights_low, value_group, preferred_element_type=jnp.float32
            )
            return (context.astype(jnp.bfloat16), log_total)

        context, log_totals = lax.map(per_block, (query_blocks, offsets))
        return (context.reshape(row_count, width, HEAD_DIM), log_totals)

    context, log_totals = lax.map(
        per_group, (split_heads(queries), split_heads(keys), split_heads(values))
    )
    return (merge_heads(context), log_totals)


def attention_backward(queries, keys, values, log_totals, context_grad, causal):
    row_count = queries.shape[0]
    block_rows = min(512, row_count)
    block_count = row_count // block_rows
    offsets = jnp.arange(block_count, dtype=jnp.int32) * block_rows
    scale = HEAD_DIM ** (-0.5)

    def per_group(operands):
        query_group, key_group, value_group, grad_group, total_group = operands
        width = query_group.shape[1]
        query_blocks = query_group.reshape(block_count, block_rows, width, HEAD_DIM)
        grad_blocks = grad_group.reshape(block_count, block_rows, width, HEAD_DIM)

        def per_block(accumulated, block_items):
            key_grad, value_grad = accumulated
            query_block, grad_block, log_total, offset = block_items
            scores = block_scores(query_block, key_group, offset, causal)
            weights_full = jnp.exp(scores - log_total)
            weights_low = weights_full.astype(jnp.bfloat16)
            value_grad = value_grad + jnp.einsum(
                "gqk,qgd->kgd", weights_low, grad_block, preferred_element_type=jnp.float32
            )
            weight_grad = jnp.einsum(
                "qgd,kgd->gqk", grad_block, value_group, preferred_element_type=jnp.float32
            )
            row_dot = jnp.sum(weights_full * weight_grad, axis=-1, keepdims=True)
            score_grad = (weights_full * (weight_grad - row_dot)).astype(jnp.bfloat16)
            query_grad = (
                jnp.einsum(
                    "gqk,kgd->qgd", score_grad, key_group, preferred_element_type=jnp.float32
                )
                * scale
            )
            key_grad = (
                key_grad
                + jnp.einsum(
                    "gqk,qgd->kgd", score_grad, query_block, preferred_element_type=jnp.float32
                )
                * scale
            )
            return ((key_grad, value_grad), query_grad)

        empty_grad = jnp.zeros(key_group.shape, jnp.float32)
        (key_grad, value_grad), query_grad = lax.scan(
            per_block, (empty_grad, empty_grad), (query_blocks, grad_blocks, total_group, offsets)
        )
        return (query_grad.reshape(row_count, width, HEAD_DIM), key_grad, value_grad)

    query_grad, key_grad, value_grad = lax.map(
        per_group,
        (
            split_heads(queries),
            split_heads(keys),
            split_heads(values),
            split_heads(context_grad),
            log_totals,
        ),
    )
    return (merge_heads(query_grad), merge_heads(key_grad), merge_heads(value_grad))


def pick_blocks(blocks, order):
    count = blocks.shape[0]
    return jnp.concatenate(
        [lax.dynamic_slice_in_dim(blocks, order[i], 1, axis=0) for i in range(count)], axis=0
    )


MESH = pl.DeviceIdType.MESH
ROWS = 128
CHUNKS = 32


def place():
    rep, shard = lax.axis_index("rep"), lax.axis_index("shard")
    return rep // 2, lax.rem(rep, 2), shard // 2, lax.rem(shard, 2)


def device(z, y, x, c):
    return (z * 2 + y, x * 2 + c)


def greet(peers):
    barrier = pltpu.get_barrier_semaphore()
    for peer in peers:
        pl.semaphore_signal(barrier, inc=1, device_id=peer, device_id_type=MESH)
    pl.semaphore_wait(barrier, len(peers))


def rows_at(base, size, align):
    return pl.ds(pl.multiple_of(base, align), size)


F32, BF16 = jnp.float32, jnp.bfloat16
RING = 8
LAGS = (0, 1, 3, 4, 5, 6, 7)


def dot_over(left, right, a, b):
    return lax.dot_general(left, right, (((a,), (b,)), ((), ())), preferred_element_type=F32)


def dot_nn(left, right):
    return dot_over(left, right, 1, 0)


def dot_nt(left, right):
    return dot_over(left, right, 1, 1)


def dot_tn(left, right):
    return dot_over(left, right, 0, 0)


def remote(src, dst, send, recv, peer):
    return pltpu.make_async_remote_copy(
        src_ref=src, dst_ref=dst, send_sem=send, recv_sem=recv, device_id=peer, device_id_type=MESH
    )


def loop(count, body):
    def step(i, carry):
        body(i)
        return carry

    lax.fori_loop(0, count, step, 0)


ERF_TOP = (
    -2.72614225801306e-10, 2.77068142495902e-08, -2.10102402082508e-06, -5.69250639462346e-05,
    -7.34990630326855e-04, -2.95459980854025e-03, -1.60960333262415e-02,
)
ERF_BOTTOM = (
    -1.45660718464996e-05, -2.13374055278905e-04, -1.68282697438203e-03, -7.37332916720468e-03,
    -1.42647390514189e-02,
)


def normal_cdf(value):
    arg = jnp.clip(value * 0.7071067811865476, -3.832506856900711, 3.832506856900711)
    square = arg * arg
    top, bottom = jnp.full_like(arg, ERF_TOP[0]), jnp.full_like(arg, ERF_BOTTOM[0])
    for factor in ERF_TOP[1:]:
        top = top * square + factor
    for factor in ERF_BOTTOM[1:]:
        bottom = bottom * square + factor
    return 0.5 + 0.5 * (arg * top / bottom)


BACK_SCRATCH = dict(
    mine=pltpu.VMEM((4, 2, ROWS, 1024), BF16),
    r0=pltpu.VMEM((RING, 2, ROWS, 1024), BF16),
    r1=pltpu.VMEM((RING, ROWS, 1024), BF16),
    r2=pltpu.VMEM((RING, ROWS // 2, 1024), BF16),
    r3=pltpu.VMEM((RING, 3, ROWS // 8, 1024), BF16),
    held=pltpu.VMEM((RING, ROWS // 8, 1024), BF16),
    small=pltpu.VMEM((4, 24, 256), F32),
    s0=pltpu.VMEM((2, 24, 256), F32),
    s1=pltpu.VMEM((24, 256), F32),
    s2=pltpu.VMEM((24, 256), F32),
    s3=pltpu.VMEM((3, 24, 256), F32),
    own_sem=pltpu.SemaphoreType.DMA((4, 2)),
    c_send=pltpu.SemaphoreType.DMA((CHUNKS, 2)),
    c_recv=pltpu.SemaphoreType.DMA((CHUNKS, 2)),
    x_send=pltpu.SemaphoreType.DMA((CHUNKS,)),
    x_recv=pltpu.SemaphoreType.DMA((CHUNKS,)),
    y_send=pltpu.SemaphoreType.DMA((CHUNKS,)),
    y_recv=pltpu.SemaphoreType.DMA((CHUNKS,)),
    z_send=pltpu.SemaphoreType.DMA((CHUNKS, 3)),
    z_recv=pltpu.SemaphoreType.DMA((CHUNKS, 3)),
    a_send=pltpu.SemaphoreType.DMA((CHUNKS, 3)),
    a_recv=pltpu.SemaphoreType.DMA((CHUNKS, 3)),
    a_own=pltpu.SemaphoreType.DMA((CHUNKS,)),
    b_send=pltpu.SemaphoreType.DMA((CHUNKS,)),
    b_recv=pltpu.SemaphoreType.DMA((CHUNKS,)),
    t_send=pltpu.SemaphoreType.DMA((7,)),
    t_recv=pltpu.SemaphoreType.DMA((7,)),
    o_send=pltpu.SemaphoreType.DMA((2, 3)),
    o_recv=pltpu.SemaphoreType.DMA((2, 3)),
    o_own=pltpu.SemaphoreType.DMA((2,)),
    load_sem=pltpu.SemaphoreType.DMA((16,)),
    tile_sem=pltpu.SemaphoreType.DMA((2, 16)),
    weight_sem=pltpu.SemaphoreType.DMA((2,)),
    grad_sem=pltpu.SemaphoreType.DMA((2,)),
    x1=pltpu.VMEM((512, 1024), BF16),
    q1=pltpu.VMEM((512, 1024), BF16),
    k1=pltpu.VMEM((512, 1024), BF16),
    v1=pltpu.VMEM((512, 1024), BF16),
    o1=pltpu.VMEM((512, 1024), BF16),
    h1=pltpu.VMEM((512, 1024), BF16),
    q2=pltpu.VMEM((512, 1024), BF16),
    k2=pltpu.VMEM((256, 1024), BF16),
    v2=pltpu.VMEM((256, 1024), BF16),
    o2=pltpu.VMEM((512, 1024), BF16),
    h2=pltpu.VMEM((512, 1024), BF16),
    e1=pltpu.VMEM((256, 1024), BF16),
    cot=pltpu.VMEM((512, 1024), BF16),
    sum1=pltpu.VMEM((512, 1024), F32),
    sum2=pltpu.VMEM((512, 1024), F32),
    sum3=pltpu.VMEM((512, 1024), F32),
    dz=pltpu.VMEM((512, 1024), F32),
    low=pltpu.VMEM((512, 1024), BF16),
    dob=pltpu.VMEM((512, 1024), BF16),
    dqb=pltpu.VMEM((512, 1024), BF16),
    dkb=pltpu.VMEM((512, 1024), BF16),
    dvb=pltpu.VMEM((512, 1024), BF16),
    dka=pltpu.VMEM((512, 128), F32),
    dva=pltpu.VMEM((512, 128), F32),
    ut=pltpu.VMEM((2, 512, 512), F32),
    wd=pltpu.VMEM((2, 512, 1024), BF16),
    wu=pltpu.VMEM((2, 1024, 512), BF16),
    wb=pltpu.VMEM((2, 1024, 1024), BF16),
    gt=pltpu.VMEM((2, 512, 512), BF16),
    dut=pltpu.VMEM((512, 512), BF16),
    stage=pltpu.VMEM((2, 4, ROWS, 1024), BF16),
    sums=pltpu.VMEM((8, 1024), F32),
    ub=pltpu.VMEM((8, 1, 512), F32),
)
BACK_LOADS = (
    "x1", "q1", "k1", "v1", "o1", "h1", "q2", "k2", "v2", "o2", "h2", "e1", "cot", "sum1", "sum2", "sum3",
)


class Reducer:
    def __init__(self, s, parts, total, small_total):
        self.s, self.parts, self.total, self.small_total = s, parts, total, small_total
        z, y, x, c = self.at = place()
        self.core = device(z, y, x, 1 - c)
        self.xmate = device(z, y, 1 - x, c)
        self.diag = device(z, y, 1 - x, 1 - c)
        self.ymate = device(z, 1 - y, x, c)
        self.others = [device(lax.rem(z + i, 4), y, x, c) for i in (1, 2, 3)]

    def greet(self):
        greet([self.core, self.xmate, self.diag, self.ymate] + self.others)

    def core_copy(self, k, side):
        s, (_, _, _, c) = self.s, self.at
        return remote(
            self.parts.at[k, side * 2 + 1 - c], s.r0.at[lax.rem(k, RING), side],
            s.c_send.at[k, side], s.c_recv.at[k, side], self.core,
        )

    def own_copy(self, k, side):
        s, (_, _, _, c) = self.s, self.at
        slot = lax.rem(k, 4)
        return pltpu.make_async_copy(
            self.parts.at[k, side * 2 + c], s.mine.at[slot, side], s.own_sem.at[slot, side]
        )

    def fetch(self, k):
        for side in (0, 1):
            self.core_copy(k, side).start()
            self.own_copy(k, side).start()

    def x_copy(self, k):
        s, (_, _, x, _) = self.s, self.at
        slot = lax.rem(k, RING)
        return remote(s.r0.at[slot, 1 - x], s.r1.at[slot], s.x_send.at[k], s.x_recv.at[k], self.xmate)

    def core_sum(self, k):
        s, slot, near = self.s, lax.rem(k, RING), lax.rem(k, 4)
        for side in (0, 1):
            self.core_copy(k, side).wait()
            self.own_copy(k, side).wait()

        def add(i):
            piece = rows_at(i * 32, 32, 32)
            for side in (0, 1):
                s.r0[slot, side, piece, :] = s.r0[slot, side, piece, :] + s.mine[near, side, piece, :]

        loop(ROWS // 32, add)
        self.x_copy(k).start()

    def y_copy(self, k):
        s, (_, y, _, _) = self.s, self.at
        slot, half = lax.rem(k, RING), ROWS // 2
        return remote(
            s.r1.at[slot, rows_at((1 - y) * half, half, half), :], s.r2.at[slot],
            s.y_send.at[k], s.y_recv.at[k], self.ymate,
        )

    def x_sum(self, k):
        s, (_, _, x, _) = self.s, self.at
        slot = lax.rem(k, RING)
        self.x_copy(k).wait()

        def add(i):
            piece = rows_at(i * 32, 32, 32)
            s.r1[slot, piece, :] = s.r0[slot, x, piece, :] + s.r1[slot, piece, :]

        loop(ROWS // 32, add)
        self.y_copy(k).start()

    def z_copies(self, k):
        s, (z, _, _, _) = self.s, self.at
        slot, quarter = lax.rem(k, RING), ROWS // 8
        return [
            remote(
                s.r2.at[slot, rows_at(lax.rem(z + i + 1, 4) * quarter, quarter, quarter), :], s.r3.at[slot, i],
                s.z_send.at[k, i], s.z_recv.at[k, i], self.others[i],
            )
            for i in (0, 1, 2)
        ]

    def y_sum(self, k):
        s, (_, y, _, _) = self.s, self.at
        slot, half = lax.rem(k, RING), ROWS // 2
        self.y_copy(k).wait()

        def add(i):
            piece = rows_at(i * 32, 32, 32)
            s.r2[slot, piece, :] = s.r1[slot, rows_at(y * half + i * 32, 32, 32), :] + s.r2[slot, piece, :]

        loop(half // 32, add)
        for copy in self.z_copies(k):
            copy.start()

    def out_piece(self, k):
        z, y, _, _ = self.at
        return self.total.at[k, rows_at(y * (ROWS // 2) + z * (ROWS // 8), ROWS // 8, ROWS // 8), :]

    def spread_copies(self, k):
        s, slot = self.s, lax.rem(k, RING)
        return [
            remote(s.held.at[slot], self.out_piece(k), s.a_send.at[k, i], s.a_recv.at[k, i], self.others[i])
            for i in (0, 1, 2)
        ]

    def held_copy(self, k):
        return pltpu.make_async_copy(self.s.held.at[lax.rem(k, RING)], self.out_piece(k), self.s.a_own.at[k])

    def z_sum(self, k):
        s, (z, _, _, _) = self.s, self.at
        slot, quarter = lax.rem(k, RING), ROWS // 8
        for copy in self.z_copies(k):
            copy.wait()
        added = s.r2[slot, rows_at(z * quarter, quarter, quarter), :].astype(F32)
        for i in (0, 1, 2):
            added = added + s.r3[slot, i].astype(F32)
        s.held[slot] = added.astype(BF16)
        for copy in self.spread_copies(k):
            copy.start()
        self.held_copy(k).start()

    def half_copy(self, k):
        s, (_, y, _, _) = self.s, self.at
        half = ROWS // 2
        part = self.total.at[k, rows_at(y * half, half, half), :]
        return remote(part, part, s.b_send.at[k], s.b_recv.at[k], self.ymate)

    def spread_y(self, k):
        for copy in self.spread_copies(k):
            copy.wait()
        self.held_copy(k).wait()
        self.half_copy(k).start()

    def finish(self, k):
        self.half_copy(k).wait()

    def tick(self, t):
        stages = (self.fetch, self.core_sum, self.x_sum, self.y_sum, self.z_sum, self.spread_y, self.finish)
        for lag, act in zip(LAGS, stages):
            k = t - lag

            @pl.when((k >= 0) & (k < CHUNKS))
            def _(k=k, act=act):
                act(k)

    def small_steps(self, t):
        s, (_, _, x, c) = self.s, self.at
        send, recv = s.t_send, s.t_recv
        firsts = [
            remote(s.small.at[side * 2 + 1 - c], s.s0.at[side], send.at[side], recv.at[side], self.core)
            for side in (0, 1)
        ]
        across = remote(s.s0.at[1 - x], s.s1, send.at[2], recv.at[2], self.xmate)
        along = remote(s.s1, s.s2, send.at[3], recv.at[3], self.ymate)
        lasts = [
            remote(s.s2, s.s3.at[i], send.at[4 + i], recv.at[4 + i], self.others[i]) for i in (0, 1, 2)
        ]

        @pl.when(t == 0)
        def _():
            for copy in firsts:
                copy.start()

        @pl.when(t == 2)
        def _():
            for side in (0, 1):
                firsts[side].wait()
                s.s0[side] = s.s0[side] + s.small[side * 2 + c]
            across.start()

        @pl.when(t == 4)
        def _():
            across.wait()
            s.s1[...] = s.s1[...] + s.s0[x]
            along.start()

        @pl.when(t == 6)
        def _():
            along.wait()
            s.s2[...] = s.s2[...] + s.s1[...]
            for copy in lasts:
                copy.start()

        @pl.when(t == 8)
        def _():
            for copy in lasts:
                copy.wait()
            self.small_total[...] = s.s2[...] + s.s3[0] + s.s3[1] + s.s3[2]


def back_kernel(*refs):
    loads = dict(zip(BACK_LOADS, refs[:16]))
    d_all, g_all, f_in, f_out, f_up, f_down, gains, out_rows, mask = refs[16:25]
    total, small_total, grad_enc, out_back, grad_back, parts = refs[25:31]
    s = types.SimpleNamespace(**dict(zip(BACK_SCRATCH, refs[31:])))
    reducer = Reducer(s, parts, total, small_total)
    z, y, x, c = reducer.at
    mine = x * 2 + c
    peers = ((reducer.core, x * 2 + 1 - c), (reducer.xmate, (1 - x) * 2 + c), (reducer.diag, (1 - x) * 2 + 1 - c))

    def row_copies(which, src, dst):
        return [
            remote(
                src.at[rows_at(slot * 128, 128, 128), :], dst.at[mine],
                s.o_send.at[which, i], s.o_recv.at[which, i], peer,
            )
            for i, (peer, slot) in enumerate(peers)
        ] + [pltpu.make_async_copy(src.at[rows_at(mine * 128, 128, 128), :], dst.at[mine], s.o_own.at[which])]

    def load(name):
        return pltpu.make_async_copy(loads[name], getattr(s, name), s.load_sem.at[BACK_LOADS.index(name)])

    for name in ("sum3", "cot", "h2"):
        load(name).start()

    def tile_copies(j, slot):
        copies = []
        for i in range(4):
            columns = rows_at(i * 1024 + j * 128, 128, 128)
            copies += [
                pltpu.make_async_copy(
                    d_all.at[:, columns], s.ut.at[slot, :, pl.ds(i * 128, 128)], s.tile_sem.at[slot, i]
                ),
                pltpu.make_async_copy(
                    g_all.at[:, columns], s.gt.at[slot, :, pl.ds(i * 128, 128)], s.tile_sem.at[slot, 12 + i]
                ),
                pltpu.make_async_copy(
                    f_down.at[columns, :], s.wd.at[slot, pl.ds(i * 128, 128), :], s.tile_sem.at[slot, 4 + i]
                ),
                pltpu.make_async_copy(
                    f_up.at[:, columns], s.wu.at[slot, :, pl.ds(i * 128, 128)], s.tile_sem.at[slot, 8 + i]
                ),
            ]
        return copies

    for copy in tile_copies(0, 0):
        copy.start()
    weights = (
        f_out.at[1], f_in.at[4], f_in.at[5], f_in.at[3], f_out.at[0], f_in.at[0], f_in.at[1], f_in.at[2],
    )

    def weight(i):
        return pltpu.make_async_copy(weights[i], s.wb.at[i % 2], s.weight_sem.at[i % 2])

    reducer.greet()
    for copy in row_copies(0, out_rows, out_back):
        copy.start()
    for name in ("sum2", "o2", "q2", "k2", "v2", "h1", "e1", "sum1", "o1", "q1", "k1", "v1", "x1"):
        load(name).start()
    weight(0).start()
    weight(1).start()
    s.small[...] = jnp.zeros_like(s.small)

    def put(row, value):
        for i in range(4):
            s.small[i, row:row + 1, :] = value[:, i * 256:(i + 1) * 256]

    def norm_back(sum_ref, index, first, bias_row):
        s.sums[...] = jnp.zeros_like(s.sums)
        gain = gains[6 + index:7 + index, :]

        def block(i):
            p = rows_at(i * 32, 32, 32)
            value = sum_ref[p, :]
            grad = s.cot[p, :].astype(F32) * mask[p, 0:1] if first else s.dz[p, :]
            center = value - jnp.mean(value, axis=1, keepdims=True)
            scale = lax.rsqrt(jnp.mean(center * center, axis=1, keepdims=True) + epsilon)
            normal = center * scale
            scaled = grad * gain
            back = scale * (
                scaled - jnp.mean(scaled, axis=1, keepdims=True)
                - normal * jnp.mean(scaled * normal, axis=1, keepdims=True)
            )
            rounded = back.astype(BF16)
            s.dz[p, :] = back
            s.low[p, :] = rounded
            s.sums[0:1, :] += jnp.sum(grad * normal, axis=0, keepdims=True)
            s.sums[1:2, :] += jnp.sum(grad, axis=0, keepdims=True)
            s.sums[2:3, :] += jnp.sum(rounded.astype(F32), axis=0, keepdims=True)

        loop(16, block)
        put(6 + index, s.sums[0:1, :])
        put(9 + index, s.sums[1:2, :])
        put(bias_row, s.sums[2:3, :])

    def column_sums(ref, count, row):
        s.sums[...] = jnp.zeros_like(s.sums)

        def block(i):
            p = rows_at(i * 64, 64, 64)
            s.sums[0:1, :] += jnp.sum(ref[p, :].astype(F32), axis=0, keepdims=True)

        loop(count // 64, block)
        put(row, s.sums[0:1, :])

    pending = []

    def flush():
        if pending:
            pending.pop().wait()

    def store_grad(chunk, left, right):
        count = left.shape[0]
        flush()

        def block(i):
            product = dot_tn(left[:, rows_at(i * 256, 256, 256)], right[0:count, :]).astype(BF16)
            s.stage[0, i] = product[:128]
            s.stage[1, i] = product[128:]

        loop(4, block)
        pending.append(pltpu.make_async_copy(s.stage, parts.at[pl.ds(chunk, 2)], s.grad_sem.at[0]))
        pending[-1].start()

    load("sum3").wait()
    load("cot").wait()
    norm_back(s.sum3, 2, True, 16)
    load("h2").wait()

    def down_save(j):
        return pltpu.make_async_copy(s.stage.at[0], parts.at[2 * j], s.grad_sem.at[0])

    def up_save(j):
        return pltpu.make_async_copy(s.stage.at[1], parts.at[2 * j + 1], s.grad_sem.at[1])

    def tile(j):
        slot = lax.rem(j, 2)
        for copy in tile_copies(j, slot):
            copy.wait()

        @pl.when(j < 7)
        def _():
            for copy in tile_copies(j + 1, 1 - slot):
                copy.start()

        def down(i):
            product = dot_tn(s.gt[slot, :, rows_at(i * 256, 256, 256)], s.low[...]).astype(BF16)
            s.stage[0, 2 * i] = product[:128]
            s.stage[0, 2 * i + 1] = product[128:]

        loop(2, down)
        down_save(j).start()

        def hidden(i):
            p = rows_at(i * 256, 256, 256)
            grad = dot_nt(s.low[...], s.wd[slot, p, :])
            rounded = (grad * s.ut[slot, :, p]).astype(BF16)
            s.dut[:, p] = rounded
            s.ub[j, :, p] = jnp.sum(rounded.astype(F32), axis=0, keepdims=True)

        loop(2, hidden)
        down_save(j).wait()

        @pl.when(lax.rem(j, 2) == 0)
        def _():
            reducer.tick(3 * j // 2)


        def up(i):
            product = dot_tn(s.h2[:, rows_at(i * 256, 256, 256)], s.dut[...]).astype(BF16)
            s.stage[1, i, :, 0:512] = product[:128]
            s.stage[1, i, :, 512:1024] = product[128:]

        loop(4, up)
        up_save(j).start()

        def back(i):
            p = rows_at(i * 256, 256, 256)
            s.dz[:, p] += dot_nt(s.dut[...], s.wu[slot, p, :])

        loop(4, back)
        up_save(j).wait()
        reducer.tick((3 * j + 2) // 2)

    loop(8, tile)
    for j in range(8):
        for i in range(4):
            s.small[i, 12 + j // 2:13 + j // 2, (j % 2) * 128:(j % 2) * 128 + 128] = s.ub[j, :, i * 128:(i + 1) * 128]
    load("sum2").wait()
    norm_back(s.sum2, 1, False, 5)
    reducer.tick(12)
    load("o2").wait()
    store_grad(16, s.o2, s.low)

    def times_weight(dst, left, count, slot):
        def block(i):
            p = rows_at(i * 256, 256, 256)
            dst[:, p] = dot_nt(left[...], s.wb[slot, p, :]).astype(BF16)

        loop(count, block)

    def add_weight(left, slot):
        def block(i):
            p = rows_at(i * 256, 256, 256)
            s.dz[:, p] += dot_nt(left[...], s.wb[slot, p, :])

        loop(4, block)

    weight(0).wait()
    times_weight(s.dob, s.low, 4, 0)
    weight(2).start()
    flush()
    reducer.tick(13)
    for name in ("q2", "k2", "v2"):
        load(name).wait()

    lane = lax.broadcasted_iota(jnp.int32, (1, 128), 1)
    head_masks = [(lane < 64).astype(F32).astype(BF16), (lane >= 64).astype(F32).astype(BF16)]

    def attention_pair(i, q_ref, k_ref, v_ref, key_count, causal):
        lanes = rows_at(i * 128, 128, 128)
        s.dka[...] = jnp.zeros_like(s.dka)
        s.dva[...] = jnp.zeros_like(s.dva)
        for block in (0, 1):
            rows = pl.ds(block * 256, 256)
            reach = (block + 1) * 256 if causal else key_count
            query, grad = q_ref[rows, lanes], s.dob[rows, lanes]
            key, value = k_ref[0:reach, lanes], v_ref[0:reach, lanes]
            query_grad = jnp.zeros((256, 128), F32)
            for mask in head_masks:
                query_one, grad_one = query * mask, grad * mask
                scores = dot_nt(key, query_one) * 0.125
                if causal:
                    key_at = lax.broadcasted_iota(jnp.int32, (reach, 256), 0)
                    query_at = lax.broadcasted_iota(jnp.int32, (reach, 256), 1) + block * 256
                    scores = jnp.where(key_at <= query_at, scores, -1e30)
                peak = jnp.max(scores, axis=0, keepdims=True)
                full = jnp.exp(scores - peak)
                full = full * (1.0 / jnp.sum(full, axis=0, keepdims=True))
                full_grad = dot_nt(value, grad_one)
                row_dot = jnp.sum(full * full_grad, axis=0, keepdims=True)
                score_grad = (full * (full_grad - row_dot)).astype(BF16)
                s.dva[0:reach, :] += dot_nn(full.astype(BF16), grad_one)
                s.dka[0:reach, :] += dot_nn(score_grad, query_one)
                query_grad = query_grad + dot_tn(score_grad, key * mask)
            s.dqb[rows, lanes] = (query_grad * 0.125).astype(BF16)
        s.dkb[0:key_count, lanes] = (s.dka[0:key_count, :] * 0.125).astype(BF16)
        s.dvb[0:key_count, lanes] = s.dva[0:key_count, :].astype(BF16)

    def cross(i):
        attention_pair(i, s.q2, s.k2, s.v2, 256, False)

        @pl.when((lax.rem(i, 2) == 1) & (i < 7))
        def _():
            reducer.tick(14 + i // 2)

    loop(8, cross)
    load("h1").wait()
    load("e1").wait()
    store_grad(18, s.h1, s.dqb)
    reducer.tick(17)
    store_grad(20, s.e1, s.dkb)
    reducer.tick(18)
    store_grad(22, s.e1, s.dvb)
    reducer.tick(19)
    column_sums(s.dqb, 512, 3)
    column_sums(s.dvb, 256, 4)
    weight(1).wait()
    weight(2).wait()

    def enc_block(i):
        p = rows_at(i * 256, 256, 256)
        grad_enc[:, p] = (
            dot_nt(s.dkb[0:256, :], s.wb[1, p, :]) + dot_nt(s.dvb[0:256, :], s.wb[0, p, :])
        ).astype(BF16)

    loop(4, enc_block)
    flush()
    reducer.tick(20)
    weight(3).start()
    weight(4).start()
    weight(3).wait()
    add_weight(s.dqb, 1)
    weight(5).start()
    reducer.tick(21)
    load("sum1").wait()
    norm_back(s.sum1, 0, False, 2)
    load("o1").wait()
    store_grad(24, s.o1, s.low)
    reducer.tick(22)
    weight(4).wait()
    times_weight(s.dob, s.low, 4, 0)
    weight(6).start()
    flush()
    reducer.tick(23)
    for name in ("q1", "k1", "v1"):
        load(name).wait()

    def own(i):
        attention_pair(i, s.q1, s.k1, s.v1, 512, True)

        @pl.when(lax.rem(i, 3) == 2)
        def _():
            reducer.tick(24 + i // 3)

    loop(8, own)
    load("x1").wait()
    store_grad(26, s.x1, s.dqb)
    store_grad(28, s.x1, s.dkb)
    reducer.tick(26)
    store_grad(30, s.x1, s.dvb)
    reducer.tick(27)
    column_sums(s.dqb, 512, 0)
    column_sums(s.dvb, 512, 1)
    flush()
    reducer.tick(28)
    weight(5).wait()
    add_weight(s.dqb, 1)
    weight(7).start()
    reducer.tick(29)
    weight(6).wait()
    add_weight(s.dkb, 0)
    reducer.tick(30)
    weight(7).wait()

    def last(i):
        p = rows_at(i * 256, 256, 256)
        s.low[:, p] = (s.dz[:, p] + dot_nt(s.dvb[...], s.wb[1, p, :])).astype(BF16)

    loop(4, last)
    def drain(i):
        reducer.tick(31 + i)

        @pl.when(i == LAGS[1])
        def _():
            for copy in row_copies(1, s.low, grad_back):
                copy.start()

        reducer.small_steps(i)

    loop(max(9, CHUNKS + LAGS[-1] - 31), drain)
    for copy in row_copies(0, out_rows, out_back) + row_copies(1, s.low, grad_back):
        copy.wait()


def backward(loads, *rest):
    any_space = pl.BlockSpec(memory_space=pl.ANY)
    in_vmem = pl.BlockSpec(memory_space=pltpu.VMEM)
    return pl.pallas_call(
        back_kernel,
        out_shape=(
            jax.ShapeDtypeStruct((CHUNKS, ROWS, 1024), BF16),
            jax.ShapeDtypeStruct((24, 256), F32),
            jax.ShapeDtypeStruct((256, 1024), BF16),
            jax.ShapeDtypeStruct((4, 128, 1024), BF16),
            jax.ShapeDtypeStruct((4, 128, 1024), BF16),
            jax.ShapeDtypeStruct((CHUNKS, 4, ROWS, 1024), BF16),
        ),
        in_specs=[any_space] * 22 + [in_vmem] * 3,
        out_specs=(any_space, in_vmem, in_vmem, any_space, any_space, any_space),
        scratch_shapes=list(BACK_SCRATCH.values()),
        compiler_params=pltpu.CompilerParams(
            collective_id=1, has_side_effects=True, vmem_limit_bytes=62 << 20
        ),
    )(*[loads[name] for name in BACK_LOADS], *rest)


FORWARD_SCRATCH = dict(
    v_in=pltpu.VMEM((6, 1024, 1024), BF16),
    v_out=pltpu.VMEM((2, 1024, 1024), BF16),
    v_up=pltpu.VMEM((1024, 4096), BF16),
    v_down=pltpu.VMEM((4096, 1024), BF16),
    small=pltpu.VMEM((24, 256), F32),
    s_tok=pltpu.VMEM((4, 128, 1024), BF16),
    v_small=pltpu.VMEM((4, 24, 256), F32),
    vec=pltpu.VMEM((24, 1024), F32),
    x=pltpu.VMEM((512, 1024), BF16),
    e=pltpu.VMEM((256, 1024), BF16),
    q=pltpu.VMEM((512, 1024), BF16),
    k=pltpu.VMEM((512, 1024), BF16),
    v=pltpu.VMEM((512, 1024), BF16),
    o=pltpu.VMEM((512, 1024), BF16),
    h1=pltpu.VMEM((512, 1024), BF16),
    q2=pltpu.VMEM((512, 1024), BF16),
    k2=pltpu.VMEM((256, 1024), BF16),
    v2=pltpu.VMEM((256, 1024), BF16),
    o2=pltpu.VMEM((512, 1024), BF16),
    h2=pltpu.VMEM((512, 1024), BF16),
    y=pltpu.VMEM((512, 1024), BF16),
    hf=pltpu.VMEM((512, 1024), F32),
    sum_a=pltpu.VMEM((512, 1024), F32),
    sum_b=pltpu.VMEM((512, 1024), F32),
    ublock=pltpu.VMEM((512, 512), F32),
    gblock=pltpu.VMEM((2, 512, 512), BF16),
    dblock=pltpu.VMEM((2, 512, 512), F32),
    own_sem=pltpu.SemaphoreType.DMA((16, 4)),
    x_send=pltpu.SemaphoreType.DMA((16, 4)),
    x_recv=pltpu.SemaphoreType.DMA((16, 4)),
    y_send=pltpu.SemaphoreType.DMA((16, 2, 4)),
    y_recv=pltpu.SemaphoreType.DMA((16, 2, 4)),
    z_send=pltpu.SemaphoreType.DMA((16, 2, 4)),
    z_recv=pltpu.SemaphoreType.DMA((16, 2, 4)),
    c_send=pltpu.SemaphoreType.DMA((16, 2, 4)),
    c_recv=pltpu.SemaphoreType.DMA((16, 2, 4)),
    t_send=pltpu.SemaphoreType.DMA((3, 3)),
    t_recv=pltpu.SemaphoreType.DMA((3, 3)),
    t_own=pltpu.SemaphoreType.DMA((4,)),
    save_sem=pltpu.SemaphoreType.DMA((16,)),
    weight_sem=pltpu.SemaphoreType.DMA((16,)),
    late_sem=pltpu.SemaphoreType.DMA((8, 4)),
    block_sem=pltpu.SemaphoreType.DMA((2, 4)),
)
SAVED = ("x", "q", "k", "v", "o", "h1", "q2", "k2", "v2", "o2", "h2", "sum1", "sum2", "sum3", "y")
GATHER_ORDER = (0, 1, 2, 6, 4, 5, 3, 7, 8, 12, 9, 13, 10, 14, 11, 15)
AHEAD, HOPS = 3, (1, 2, 3)


def weight_views(refs, k, shard, start, size):
    if k < 6:
        return [refs[0].at[k, rows_at(shard * 256 + start, size, 8), :]]
    if k < 8:
        return [refs[1].at[k - 6, rows_at(shard * 256 + start, size, 8), :]]
    if k < 12:
        rows = rows_at(shard * 256 + start, size, 8)
        return [refs[2].at[rows, pl.ds(i * 1024 + (k - 8) * 256, 256)] for i in range(4)]
    return [refs[3].at[rows_at(shard * 1024 + (k - 12) * 256 + start, size, 8), :]]


class Gatherer:
    def __init__(self, s, shards, full):
        self.s, self.shards, self.full, self.done = s, shards, full, -AHEAD - 1
        z, y, x, c = self.at = place()
        self.side = lax.rem(z, 2)
        self.core = device(z, y, x, 1 - c)
        self.xmate = device(z, y, 1 - x, c)
        self.diag = device(z, y, 1 - x, 1 - c)
        self.ymate = device(z, 1 - y, x, c)
        self.zmate = device(z + 1 - 2 * self.side, y, x, c)
        self.mine, self.other = x * 2 + c, (1 - x) * 2 + c

    def greet(self):
        greet([self.core, self.xmate, self.diag, self.ymate, self.zmate])

    def send(self, k, sources, target_shard, start, size, send, recv, peer):
        targets = weight_views(self.full, k, target_shard, start, size)
        return [
            remote(src, dst, send.at[i], recv.at[i], peer)
            for i, (src, dst) in enumerate(zip(sources, targets))
        ]

    def x_copy(self, k):
        q = (self.at[1] * 2 + self.side) * 64
        return self.send(
            k, weight_views(self.shards, k, 0, q, 64), self.mine, q, 64,
            self.s.x_send.at[k], self.s.x_recv.at[k], self.xmate,
        )

    def core_copy(self, k):
        return self.send(
            k, weight_views(self.shards, k, 0, 0, 256), self.mine, 0, 256,
            self.s.c_send.at[k, 0], self.s.c_recv.at[k, 0], self.core,
        )

    def own_copy(self, k):
        pairs = zip(weight_views(self.shards, k, 0, 0, 256), weight_views(self.full, k, self.mine, 0, 256))
        return [
            pltpu.make_async_copy(src, dst, self.s.own_sem.at[k, i]) for i, (src, dst) in enumerate(pairs)
        ]

    def relay(self, k, start, size, send, recv, peer):
        return self.send(k, weight_views(self.full, k, self.other, start, size), self.other, start, size, send, recv, peer)

    def first_hops(self, k):
        s, q = self.s, (self.at[1] * 2 + self.side) * 64
        return self.relay(k, q, 64, s.y_send.at[k, 0], s.y_recv.at[k, 0], self.ymate) + self.relay(
            k, q, 64, s.z_send.at[k, 0], s.z_recv.at[k, 0], self.zmate
        )

    def second_hops(self, k):
        s, y = self.s, self.at[1]
        return self.relay(
            k, (y * 2 + 1 - self.side) * 64, 32, s.y_send.at[k, 1], s.y_recv.at[k, 1], self.ymate
        ) + self.relay(
            k, ((1 - y) * 2 + self.side) * 64 + 32, 32, s.z_send.at[k, 1], s.z_recv.at[k, 1], self.zmate
        )

    def last_hop(self, k):
        return self.relay(k, 0, 256, self.s.c_send.at[k, 1], self.s.c_recv.at[k, 1], self.core)

    def step(self, t):
        def chunk(lag):
            return GATHER_ORDER[t - lag] if 0 <= t - lag < 16 else None

        def start(copies):
            for copy in copies:
                copy.start()

        def wait(copies):
            for copy in copies:
                copy.wait()

        if (k := chunk(-AHEAD)) is not None:
            start(self.x_copy(k) + self.core_copy(k) + self.own_copy(k))
        if (k := chunk(0)) is not None:
            wait(self.x_copy(k))
            start(self.first_hops(k))
        if (k := chunk(HOPS[0])) is not None:
            wait(self.first_hops(k))
            start(self.second_hops(k))
        if (k := chunk(HOPS[1])) is not None:
            wait(self.second_hops(k))
            start(self.last_hop(k))
        if (k := chunk(HOPS[2])) is not None:
            wait(self.last_hop(k) + self.core_copy(k) + self.own_copy(k))

    def advance(self, t):
        while self.done < t:
            self.done += 1
            self.step(self.done)

    def ready(self, index):
        self.advance(index + HOPS[2])


def forward_kernel(*refs):
    owner, lengths, bias, gain_in, shift_in, up_bias, down_bias, tok_in, cot_in = refs[:9]
    w_in, w_out, w_up, w_down, enc = refs[9:14]
    f_in, f_out, f_up, f_down, f_cot, gains, mask, g_all, d_all = refs[14:23]
    saved = dict(zip(SAVED, refs[23:38]))
    s = types.SimpleNamespace(**dict(zip(FORWARD_SCRATCH, refs[38:])))
    sequence_at = [
        jnp.clip(sum(jnp.where(owner[0, j] == i, j, 0) for j in range(4)), 0, 3) for i in range(4)
    ]
    small, tok = s.small, s.s_tok
    full = (s.v_in, s.v_out, s.v_up, s.v_down)
    gather = Gatherer(s, (w_in, w_out, w_up, w_down), full)
    mine, (_, _, x, c) = gather.mine, gather.at
    peers = ((gather.core, x * 2 + 1 - c), (gather.xmate, gather.other), (gather.diag, (1 - x) * 2 + 1 - c))

    def rows_of(index):
        return rows_at(index * 128, 128, 128)

    def arrange(source, target):
        for i in range(4):
            def block(n, i=i):
                p = rows_at(n * 32, 32, 32)
                target[i, p, :] = source[sequence_at[i], p, :]

            loop(4, block)

    def token_copies():
        return [
            remote(tok.at[slot], s.x.at[rows_of(mine), :], s.t_send.at[0, i], s.t_recv.at[0, i], peer)
            for i, (peer, slot) in enumerate(peers)
        ] + [
            remote(small, s.v_small.at[mine], s.t_send.at[2, i], s.t_recv.at[2, i], peer)
            for i, (peer, slot) in enumerate(peers)
        ] + [
            pltpu.make_async_copy(tok.at[mine], s.x.at[rows_of(mine), :], s.t_own.at[0]),
            pltpu.make_async_copy(small, s.v_small.at[mine], s.t_own.at[1]),
        ]

    def cot_copies():
        return [
            remote(tok.at[slot], f_cot.at[mine], s.t_send.at[1, i], s.t_recv.at[1, i], peer)
            for i, (peer, slot) in enumerate(peers)
        ] + [pltpu.make_async_copy(tok.at[mine], f_cot.at[mine], s.t_own.at[2])]

    enc_copy = pltpu.make_async_copy(enc, s.e, s.t_own.at[3])
    enc_copy.start()
    arrange(tok_in, s.s_tok)
    small[...] = jnp.zeros_like(small)
    small[0:6, :] = bias[...].astype(F32)
    small[6:9, :] = gain_in[...].astype(F32)
    small[9:12, :] = shift_in[...].astype(F32)
    for i in range(4):
        small[12 + i:13 + i, :] = up_bias[:, i * 256:(i + 1) * 256].astype(F32)
    small[16:17, :] = down_bias[...].astype(F32)
    gather.greet()
    gather.advance(1 - AHEAD)
    for copy in token_copies():
        copy.start()

    def save(name, ref):
        return pltpu.make_async_copy(ref, saved[name], s.save_sem.at[SAVED.index(name)])

    def weight_saves(k):
        if k < 6:
            return [pltpu.make_async_copy(s.v_in.at[k], f_in.at[k], s.weight_sem.at[k])]
        if k < 8:
            return [pltpu.make_async_copy(s.v_out.at[k - 6], f_out.at[k - 6], s.weight_sem.at[k])]
        if k == 11:
            return [pltpu.make_async_copy(s.v_up, f_up, s.weight_sem.at[k])]
        return [
            pltpu.make_async_copy(src, dst, s.late_sem.at[k - 8, i])
            for i, (src, dst) in enumerate(zip(late_views(full, k), late_views((f_in, f_out, f_up, f_down), k)))
        ] if k > 11 else []

    def late_views(refs, k):
        return [view for shard in range(4) for view in weight_views(refs, k, shard, 0, 256)]

    def ready(index):
        gather.ready(index)
        for copy in weight_saves(GATHER_ORDER[index]):
            copy.start()

    def project(dst, left, weight, count, bias):
        def block(i):
            columns = rows_at(i * 256, 256, 256)
            product = dot_nn(left[0:count, :], weight[:, columns])
            if bias is not None:
                product = product + s.vec[bias:bias + 1, columns]
            dst[0:count, columns] = product.astype(BF16)

        loop(4, block)

    def join(dst, base, left, weight, bias):
        def block(i):
            columns = rows_at(i * 256, 256, 256)
            dst[:, columns] = base[:, columns].astype(F32) + (
                dot_nn(left[...], weight[:, columns]) + s.vec[bias:bias + 1, columns]
            )

        loop(4, block)

    def normalize(sum_ref, index, low, last):
        gain, shift = s.vec[6 + index:7 + index, :], s.vec[9 + index:10 + index, :]

        def block(i):
            p = rows_at(i * 32, 32, 32)
            value = sum_ref[p, :]
            center = value - jnp.mean(value, axis=1, keepdims=True)
            scale = lax.rsqrt(jnp.mean(center * center, axis=1, keepdims=True) + epsilon)
            result = center * scale * gain + shift
            if last:
                low[p, :] = (result * mask[p, 0:1]).astype(BF16)
            else:
                s.hf[p, :] = result
                low[p, :] = result.astype(BF16)

        loop(16, block)

    lane = lax.broadcasted_iota(jnp.int32, (1, 128), 1)
    head_masks = [(lane < 64).astype(F32).astype(BF16), (lane >= 64).astype(F32).astype(BF16)]

    def attend_pair(i, q_ref, k_ref, v_ref, o_ref, key_count, causal):
        lanes = rows_at(i * 128, 128, 128)
        for block in (0, 1):
            rows = pl.ds(block * 256, 256)
            reach = (block + 1) * 256 if causal else key_count
            query = q_ref[rows, lanes]
            key, value = k_ref[0:reach, lanes], v_ref[0:reach, lanes]
            context = jnp.zeros((256, 128), F32)
            for head_mask in head_masks:
                scores = dot_nt(query * head_mask, key) * 0.125
                if causal:
                    query_at = lax.broadcasted_iota(jnp.int32, (256, reach), 0) + block * 256
                    key_at = lax.broadcasted_iota(jnp.int32, (256, reach), 1)
                    scores = jnp.where(key_at <= query_at, scores, -1e30)
                weights = jnp.exp(scores - jnp.max(scores, axis=1, keepdims=True))
                weights = weights * (1.0 / jnp.sum(weights, axis=1, keepdims=True))
                context = context + dot_nn(weights.astype(BF16), value * head_mask)
            o_ref[rows, lanes] = context.astype(BF16)

    length = jnp.int32(0)
    for i in range(4):
        here = sum(jnp.where(sequence_at[i] == j, lengths[0, j], 0) for j in range(4))
        length = length + jnp.where(mine == i, here, 0)
    mask[...] = (lax.broadcasted_iota(jnp.int32, (512, 128), 0) < length).astype(F32)
    ready(0)
    for copy in token_copies():
        copy.wait()
    for i in range(4):
        s.vec[:, i * 256:(i + 1) * 256] = s.v_small[i]
    gains[...] = s.vec[0:16, :]
    save("x", s.x).start()
    project(s.q, s.x, s.v_in.at[0], 512, 0)
    save("q", s.q).start()
    ready(1)
    project(s.k, s.x, s.v_in.at[1], 512, None)
    save("k", s.k).start()
    ready(2)
    project(s.v, s.x, s.v_in.at[2], 512, 1)
    save("v", s.v).start()
    for part in range(4):
        loop(2, lambda i, part=part: attend_pair(part * 2 + i, s.q, s.k, s.v, s.o, 512, True))
        gather.advance(HOPS[2] + 3 + part // 2)
    save("o", s.o).start()
    arrange(cot_in, s.s_tok)
    for copy in cot_copies():
        copy.start()
    ready(3)
    join(s.sum_a, s.x, s.o, s.v_out.at[0], 2)
    save("sum1", s.sum_a).start()
    ready(4)
    normalize(s.sum_a, 0, s.h1, False)
    save("h1", s.h1).start()
    enc_copy.wait()
    project(s.k2, s.e, s.v_in.at[4], 256, None)
    save("k2", s.k2).start()
    ready(5)
    project(s.v2, s.e, s.v_in.at[5], 256, 4)
    save("v2", s.v2).start()
    ready(6)
    project(s.q2, s.h1, s.v_in.at[3], 512, 3)
    save("q2", s.q2).start()
    ready(7)
    for part in range(4):
        loop(2, lambda i, part=part: attend_pair(part * 2 + i, s.q2, s.k2, s.v2, s.o2, 256, False))
        gather.advance(HOPS[2] + 8 + part // 2)
    save("o2", s.o2).start()
    join(s.sum_b, s.hf, s.o2, s.v_out.at[1], 5)
    save("sum2", s.sum_b).start()
    gather.advance(HOPS[2] + 9)
    normalize(s.sum_b, 1, s.h2, False)
    save("h2", s.h2).start()
    save("sum1", s.sum_a).wait()

    def widen(i):
        p = rows_at(i * 64, 64, 64)
        s.sum_a[p, :] = s.hf[p, :] + s.vec[16:17, :]

    loop(8, widen)

    def nudge():
        gather.advance(min(gather.done + 1, 15 + HOPS[2]))

    def block_copies(j, pair):
        copies = []
        for h in (0, 1):
            columns = rows_at((2 * pair + h) * 1024 + j * 256, 256, 256)
            part = pl.ds(h * 256, 256)
            copies += [
                pltpu.make_async_copy(s.gblock.at[pair, :, part], g_all.at[:, columns], s.block_sem.at[pair, h]),
                pltpu.make_async_copy(s.dblock.at[pair, :, part], d_all.at[:, columns], s.block_sem.at[pair, 2 + h]),
            ]
        return copies

    for j in range(4):
        ready(8 + 2 * j)
        ready(9 + 2 * j)

        def mlp(pair, j=j):
            if j > 0:
                for copy in block_copies(j, pair):
                    copy.wait()
            starts = [(2 * pair + h) * 1024 + j * 256 for h in (0, 1)]
            for h in (0, 1):
                s.ublock[:, h * 256:(h + 1) * 256] = (
                    dot_nn(s.h2[...], s.v_up[:, rows_at(starts[h], 256, 256)])
                    + s.v_small[2 * pair + h, 12 + j:13 + j, :]
                )

            def hidden(r):
                p = rows_at(r * 64, 64, 64)
                value = s.ublock[p, :]
                cdf = normal_cdf(value)
                pdf = jnp.exp(-0.5 * value * value) * 0.3989422804014327
                s.gblock[pair, p, :] = (value * cdf).astype(BF16)
                s.dblock[pair, p, :] = cdf + value * pdf

            loop(4, hidden)
            nudge()
            loop(4, lambda r: hidden(r + 4))
            for copy in block_copies(j, pair):
                copy.start()

            def out(n):
                wide = rows_at(n * 256, 256, 256)
                s.sum_a[:, wide] += dot_nn(
                    s.gblock[pair, :, 0:256], s.v_down[rows_at(starts[0], 256, 256), wide]
                ) + dot_nn(s.gblock[pair, :, 256:512], s.v_down[rows_at(starts[1], 256, 256), wide])

            loop(4, out)

        for pair in (0, 1):
            mlp(pair)

    save("sum3", s.sum_a).start()
    normalize(s.sum_a, 2, s.y, True)
    save("y", s.y).start()
    for copy in block_copies(3, 0) + block_copies(3, 1) + cot_copies():
        copy.wait()
    for k in range(16):
        for copy in weight_saves(k):
            copy.wait()
    ends = dict(
        x=s.x, q=s.q, k=s.k, v=s.v, o=s.o, h1=s.h1, q2=s.q2, k2=s.k2, v2=s.v2, o2=s.o2, h2=s.h2,
        sum2=s.sum_b, sum3=s.sum_a, y=s.y,
    )
    for name, ref in ends.items():
        save(name, ref).wait()


def forward(*operands):
    any_space = pl.BlockSpec(memory_space=pl.ANY)
    in_vmem = pl.BlockSpec(memory_space=pltpu.VMEM)
    in_smem = pl.BlockSpec(memory_space=pltpu.SMEM)
    wide = {"sum1", "sum2", "sum3"}
    return pl.pallas_call(
        forward_kernel,
        out_shape=(
            jax.ShapeDtypeStruct((6, 1024, 1024), BF16),
            jax.ShapeDtypeStruct((2, 1024, 1024), BF16),
            jax.ShapeDtypeStruct((1024, 4096), BF16),
            jax.ShapeDtypeStruct((4096, 1024), BF16),
            jax.ShapeDtypeStruct((4, 128, 1024), BF16),
            jax.ShapeDtypeStruct((16, 1024), F32),
            jax.ShapeDtypeStruct((512, 128), F32),
            jax.ShapeDtypeStruct((512, 4096), BF16),
            jax.ShapeDtypeStruct((512, 4096), F32),
        ) + tuple(
            jax.ShapeDtypeStruct((256 if name in ("k2", "v2") else 512, 1024), F32 if name in wide else BF16)
            for name in SAVED
        ),
        in_specs=[in_smem] * 2 + [in_vmem] * 7 + [any_space] * 5,
        out_specs=(any_space,) * 5 + (in_vmem,) * 2 + (any_space,) * 17,
        scratch_shapes=list(FORWARD_SCRATCH.values()),
        compiler_params=pltpu.CompilerParams(
            collective_id=2, has_side_effects=True, vmem_limit_bytes=62 << 20
        ),
    )(*operands)


def sum_plain(*parts):
    dims = (1, 1, 1, 1, 1, 0, 0, 0, 0)
    scattered = [
        lax.psum_scatter(part.astype(jnp.bfloat16), "shard", scatter_dimension=dim, tiled=True)
        for part, dim in zip(parts, dims)
    ]
    return tuple(lax.psum(part, "rep").astype(jnp.float32) for part in scattered)


def finish_kernel(owner, total, small_total, out_back, grad_back, *refs):
    out, grad_tok, g_in, g_out, g_up, g_down, g_bias, g_gain, g_shift, g_up_bias, g_down_bias, w_in, w_out, w_up, w_down, sem, row_sem = refs
    copies = []
    for i in range(4):
        for j, (src, dst) in enumerate(((out_back, out), (grad_back, grad_tok))):
            copies.append(pltpu.make_async_copy(src.at[jnp.clip(owner[0, i], 0, 3)], dst.at[i], row_sem.at[i, j]))
            copies[-1].start()
    g_bias[...] = small_total[0:6, :]
    g_gain[...] = small_total[6:9, :]
    g_shift[...] = small_total[9:12, :]
    for i in range(4):
        g_up_bias[:, i * 256:(i + 1) * 256] = small_total[12 + i:13 + i, :]
    g_down_bias[...] = small_total[16:17, :]

    def widen(k, dst):
        def block(i):
            p = rows_at(i * 32, 32, 32)
            dst(p, total[k, p, :].astype(F32))

        loop(4, block)

    def send(src, dst, index):
        copies.append(pltpu.make_async_copy(src, dst, sem.at[index]))
        copies[-1].start()

    for j in range(8):
        def up(p, value):
            for half in (0, 1):
                rows = rows_at(p.start + half * 128, 32, 32)
                for c in range(4):
                    w_up[rows, c * 1024 + j * 128:c * 1024 + j * 128 + 128] = (
                        value[:, half * 512 + c * 128:half * 512 + c * 128 + 128]
                    )

        widen(2 * j + 1, up)
        rows = pl.ds(j * 128, 128)

        def down(p, value):
            w_down[rows_at(j * 128 + p.start, 32, 32), :] = value

        widen(2 * j, down)
        send(w_down.at[rows, :], g_down.at[rows, :], j)
    send(w_up, g_up, 8)
    order = [(g_out, w_out, 1, 16), (g_in, w_in, 3, 18), (g_in, w_in, 4, 20), (g_in, w_in, 5, 22),
             (g_out, w_out, 0, 24), (g_in, w_in, 0, 26), (g_in, w_in, 1, 28), (g_in, w_in, 2, 30)]
    for n, (dst, held, index, chunk) in enumerate(order):
        for half in (0, 1):
            def place_rows(p, value):
                held[index, rows_at(half * 128 + p.start, 32, 32), :] = value

            widen(chunk + half, place_rows)
        send(held.at[index], dst.at[index], 9 + n)
    for copy in copies:
        copy.wait()


def finish(owner, total, small_total, out_back, grad_back):
    any_space = pl.BlockSpec(memory_space=pl.ANY)
    in_vmem = pl.BlockSpec(memory_space=pltpu.VMEM)
    narrow = [(6, 256), (3, 256), (3, 256), (1, 1024), (1, 256)]
    wide = [(6, 256, 1024), (2, 256, 1024), (256, 4096), (1024, 1024)]
    return pl.pallas_call(
        finish_kernel,
        out_shape=tuple(
            [jax.ShapeDtypeStruct((4, 128, 1024), BF16)] * 2
            + [jax.ShapeDtypeStruct(shape, F32) for shape in wide]
            + [jax.ShapeDtypeStruct(shape, F32) for shape in narrow]
        ),
        in_specs=[pl.BlockSpec(memory_space=pltpu.SMEM)] + [in_vmem] * 4,
        out_specs=tuple([any_space] * 6 + [in_vmem] * 5),
        scratch_shapes=[pltpu.VMEM(shape, F32) for shape in wide]
        + [pltpu.SemaphoreType.DMA((17,)), pltpu.SemaphoreType.DMA((4, 2))],
        compiler_params=pltpu.CompilerParams(vmem_limit_bytes=60 << 20),
    )(owner, total, small_total, out_back, grad_back)


def fast_layer(
    tokens, enc_states, cotangent, lengths, owner, attn_in, attn_out, attn_bias,
    norm_gain, norm_bias, mlp_in, mlp_bias_in, mlp_out, mlp_bias_out,
):
    encoder = enc_states[0]
    full_in, full_out, up_full, down_full, cot, vectors, mask, g_all, d_all, *saved = forward(
        owner, lengths, attn_bias, norm_gain, norm_bias, mlp_bias_in.reshape(1, 1024),
        mlp_bias_out.reshape(1, 256), tokens, cotangent, attn_in, attn_out, mlp_in, mlp_out, encoder,
    )
    saved = dict(zip(SAVED, saved))
    loads = dict(
        x1=saved["x"], q1=saved["q"], k1=saved["k"], v1=saved["v"], o1=saved["o"], h1=saved["h1"],
        q2=saved["q2"], k2=saved["k2"], v2=saved["v2"], o2=saved["o2"], h2=saved["h2"], e1=encoder,
        cot=cot.reshape(512, 1024), sum1=saved["sum1"], sum2=saved["sum2"], sum3=saved["sum3"],
    )
    total, small_total, encoder_grad, back_blocks, grad_blocks, _ = backward(
        loads, d_all, g_all, full_in, full_out, up_full, down_full, vectors, saved["y"], mask
    )
    out, grad_tokens, g_in, g_out, g_up, g_down, *small = finish(
        owner, total, small_total, back_blocks, grad_blocks
    )
    return (
        out, grad_tokens, encoder_grad[None], g_in, g_out, small[0], small[1], small[2],
        g_up, small[3].reshape(1024), g_down, small[4].reshape(256),
    )


def local(
    tokens,
    enc_states,
    cotangent,
    lengths,
    owner,
    attn_in,
    attn_out,
    attn_bias,
    norm_gain,
    norm_bias,
    mlp_in,
    mlp_bias_in,
    mlp_out,
    mlp_bias_out,
):
    groups = lax.axis_size("shard")
    if (lax.axis_size("rep"), groups) == (8, 4):
        return fast_layer(
            tokens, enc_states, cotangent, lengths, owner, attn_in, attn_out, attn_bias,
            norm_gain, norm_bias, mlp_in, mlp_bias_in, mlp_out, mlp_bias_out,
        )
    my_index = lax.axis_index("shard")
    owner_row = owner[0]
    slot_ids = jnp.arange(groups, dtype=jnp.int32)
    matches = owner_row[None, :] == slot_ids[:, None]
    sequence_at = jnp.sum(jnp.where(matches, slot_ids[None, :], 0), axis=1)
    my_sequence = jnp.sum(jnp.where(slot_ids == my_index, sequence_at, 0))
    my_length = jnp.sum(jnp.where(slot_ids == my_sequence, lengths[0], 0))
    sent_tokens = pick_blocks(tokens, sequence_at)
    sent_grads = pick_blocks(cotangent, sequence_at)
    got_tokens, got_grads = (
        lax.all_to_all(sent_tokens, "shard", split_axis=0, concat_axis=1, tiled=True),
        lax.all_to_all(sent_grads, "shard", split_axis=0, concat_axis=1, tiled=True),
    )
    full_in, full_out, full_bias, full_gain, full_shift = (
        lax.all_gather(attn_in, "shard", axis=1, tiled=True),
        lax.all_gather(attn_out, "shard", axis=1, tiled=True),
        lax.all_gather(attn_bias, "shard", axis=1, tiled=True),
        lax.all_gather(norm_gain, "shard", axis=1, tiled=True),
        lax.all_gather(norm_bias, "shard", axis=1, tiled=True),
    )
    bias_rows = full_bias.astype(jnp.float32)
    gain_rows = full_gain.astype(jnp.float32)
    shift_rows = full_shift.astype(jnp.float32)
    up_full, up_bias, down_full, down_bias = (
        lax.all_gather(mlp_in, "shard", axis=0, tiled=True),
        lax.all_gather(mlp_bias_in, "shard", axis=0, tiled=True),
        lax.all_gather(mlp_out, "shard", axis=0, tiled=True),
        lax.all_gather(mlp_bias_out, "shard", axis=0, tiled=True),
    )
    in_back, out_back, up_back, down_back = full_in, full_out, up_full, down_full
    inputs = got_tokens[0]
    row_count = inputs.shape[0]
    row_mask = (jnp.arange(row_count, dtype=jnp.int32) < my_length).astype(jnp.float32)[:, None]
    encoder = enc_states[0]
    projected = jnp.einsum("rd,wde->wre", inputs, full_in[:3], preferred_element_type=jnp.float32)
    queries = (projected[0] + bias_rows[0]).astype(jnp.bfloat16)
    keys = projected[1].astype(jnp.bfloat16)
    values = (projected[2] + bias_rows[1]).astype(jnp.bfloat16)
    context, log_totals = attention_forward(queries, keys, values, True)
    first_sum = inputs.astype(jnp.float32) + (matmul(context, full_out[0]) + bias_rows[2])
    first_norm = layer_norm(first_sum, gain_rows[0], shift_rows[0])
    first_low = first_norm.astype(jnp.bfloat16)
    cross_queries = (matmul(first_low, full_in[3]) + bias_rows[3]).astype(jnp.bfloat16)
    cross_projected = jnp.einsum(
        "rd,wde->wre", encoder, full_in[4:6], preferred_element_type=jnp.float32
    )
    cross_keys = cross_projected[0].astype(jnp.bfloat16)
    cross_values = (cross_projected[1] + bias_rows[4]).astype(jnp.bfloat16)
    cross_context, cross_totals = attention_forward(cross_queries, cross_keys, cross_values, False)
    second_sum = first_norm + (matmul(cross_context, full_out[1]) + bias_rows[5])
    second_norm = layer_norm(second_sum, gain_rows[1], shift_rows[1])
    second_low = second_norm.astype(jnp.bfloat16)
    hidden_pre = matmul(second_low, up_full) + up_bias.astype(jnp.float32)
    hidden_low = gelu_exact(hidden_pre).astype(jnp.bfloat16)
    third_sum = second_norm + (matmul(hidden_low, down_full) + down_bias.astype(jnp.float32))
    result = (layer_norm(third_sum, gain_rows[2], shift_rows[2]) * row_mask).astype(jnp.bfloat16)
    back_blocks = lax.all_to_all(result[None], "shard", split_axis=1, concat_axis=0, tiled=True)
    output = pick_blocks(back_blocks, owner_row)
    out_grad = got_grads[0].astype(jnp.float32) * row_mask
    third_grad, third_gain_grad, third_shift_grad = jax.vjp(
        layer_norm, third_sum, gain_rows[2], shift_rows[2]
    )[1](out_grad)
    down_grad_in = third_grad.astype(jnp.bfloat16)
    grad_down = contract_rows(hidden_low, down_grad_in)
    grad_down_bias = column_sum(down_grad_in)
    hidden_grad = contract_cols(down_grad_in, down_back)
    hidden_pre_grad = jax.vjp(gelu_exact, hidden_pre)[1](hidden_grad)[0].astype(jnp.bfloat16)
    grad_up = contract_rows(second_low, hidden_pre_grad)
    grad_up_bias = column_sum(hidden_pre_grad)
    second_norm_grad = third_grad + contract_cols(hidden_pre_grad, up_back)
    second_grad, second_gain_grad, second_shift_grad = jax.vjp(
        layer_norm, second_sum, gain_rows[1], shift_rows[1]
    )[1](second_norm_grad)
    cross_out_grad = second_grad.astype(jnp.bfloat16)
    grad_cross_out = contract_rows(cross_context, cross_out_grad)
    grad_cross_out_bias = column_sum(cross_out_grad)
    cross_context_grad = contract_cols(cross_out_grad, out_back[1]).astype(jnp.bfloat16)
    cross_query_grad, cross_key_grad, cross_value_grad = attention_backward(
        cross_queries, cross_keys, cross_values, cross_totals, cross_context_grad, False
    )
    cross_query_low = cross_query_grad.astype(jnp.bfloat16)
    cross_key_low = cross_key_grad.astype(jnp.bfloat16)
    cross_value_low = cross_value_grad.astype(jnp.bfloat16)
    grad_cross_query = contract_rows(first_low, cross_query_low)
    grad_cross_query_bias = column_sum(cross_query_low)
    grad_cross_key = contract_rows(encoder, cross_key_low)
    grad_cross_value = contract_rows(encoder, cross_value_low)
    grad_cross_value_bias = column_sum(cross_value_low)
    encoder_grad = (
        contract_cols(cross_key_low, in_back[4]) + contract_cols(cross_value_low, in_back[5])
    ).astype(jnp.bfloat16)
    first_norm_grad = second_grad + contract_cols(cross_query_low, in_back[3])
    first_grad, first_gain_grad, first_shift_grad = jax.vjp(
        layer_norm, first_sum, gain_rows[0], shift_rows[0]
    )[1](first_norm_grad)
    self_out_grad = first_grad.astype(jnp.bfloat16)
    grad_self_out = contract_rows(context, self_out_grad)
    grad_self_out_bias = column_sum(self_out_grad)
    context_grad = contract_cols(self_out_grad, out_back[0]).astype(jnp.bfloat16)
    query_grad, key_grad, value_grad = attention_backward(
        queries, keys, values, log_totals, context_grad, True
    )
    query_low = query_grad.astype(jnp.bfloat16)
    key_low = key_grad.astype(jnp.bfloat16)
    value_low = value_grad.astype(jnp.bfloat16)
    grad_query = contract_rows(inputs, query_low)
    grad_query_bias = column_sum(query_low)
    grad_key = contract_rows(inputs, key_low)
    grad_value = contract_rows(inputs, value_low)
    grad_value_bias = column_sum(value_low)
    input_grad = (
        first_grad
        + contract_cols(query_low, in_back[0])
        + contract_cols(key_low, in_back[1])
        + contract_cols(value_low, in_back[2])
    ).astype(jnp.bfloat16)
    grad_blocks = lax.all_to_all(input_grad[None], "shard", split_axis=1, concat_axis=0, tiled=True)
    grad_tokens = pick_blocks(grad_blocks, owner_row)
    grad_in_full = jnp.stack(
        [grad_query, grad_key, grad_value, grad_cross_query, grad_cross_key, grad_cross_value]
    )
    grad_out_full = jnp.stack([grad_self_out, grad_cross_out])
    grad_bias_full = jnp.stack(
        [
            grad_query_bias,
            grad_value_bias,
            grad_self_out_bias,
            grad_cross_query_bias,
            grad_cross_value_bias,
            grad_cross_out_bias,
        ]
    )
    grad_gain_full = jnp.stack([first_gain_grad, second_gain_grad, third_gain_grad])
    grad_shift_full = jnp.stack([first_shift_grad, second_shift_grad, third_shift_grad])
    summed = sum_plain(
        grad_in_full, grad_out_full, grad_bias_full, grad_gain_full, grad_shift_full,
        grad_up, grad_up_bias, grad_down, grad_down_bias,
    )
    return (
        output,
        grad_tokens,
        encoder_grad[None],
        summed[0],
        summed[1],
        summed[2],
        summed[3],
        summed[4],
        summed[5],
        summed[6],
        summed[7],
        summed[8],
    )


def solution(mesh):
    placed = (
        P("rep", "shard", None),
        P(("rep", "shard"), None, None),
        P("rep", "shard", None),
        P("rep", None),
        P("rep", None),
        P(None, "shard", None),
        P(None, "shard", None),
        P(None, "shard"),
        P(None, "shard"),
        P(None, "shard"),
        P("shard", None),
        P("shard"),
        P("shard", None),
        P("shard"),
    )
    return jax.shard_map(
        local,
        mesh=mesh,
        in_specs=placed,
        out_specs=(
            P("rep", "shard", None),
            P("rep", "shard", None),
            P(("rep", "shard"), None, None),
            P(None, "shard", None),
            P(None, "shard", None),
            P(None, "shard"),
            P(None, "shard"),
            P(None, "shard"),
            P("shard", None),
            P("shard"),
            P("shard", None),
            P("shard"),
        ),
        check_vma=False,
    )
```
